32 devices in a mesh: groups: 2 (over x), cols: 16 (over z, y, core).
Axes of the slice: x: 2, y: 2, z: 4, core: 2. Of those that a mesh axis runs over, the one named last changes fastest.
Arguments:
- image_feats: bfloat16 [64, 16384], P('groups', 'cols'), parts along dimension 0, may hold values from -6 to 6
- teacher: bfloat16 [64, 256, 512], P('groups', 'cols'), parts along dimension 0, may hold values from -40 to 40
- w_first: bfloat16 [128, 576], P('cols'), may hold values from -0.25 to 0.25
- w_middle: bfloat16 [128, 1152], P('cols'), may hold values from -0.1875 to 0.1875
- w_last: bfloat16 [512, 1152], P('cols'), may hold values from -0.1875 to 0.1875
Outputs:
- grad_first: float32 [256, 576], P(('groups', 'cols')), parts along dimension 0
- grad_middle: float32 [256, 1152], P(('groups', 'cols')), parts along dimension 0
- grad_last: float32 [1024, 1152], P(('groups', 'cols')), parts along dimension 0
The draws below stay inside these ranges and needn't reach their ends.
There are 2 independent parts, one for each index of `groups`. The reference program is written for one: setup_inputs(seed, part) draws one part's arguments, and reference() takes and returns one part's arrays. A program takes and returns all parts, laid end to end along the dimension named above; an argument that names none is the same for every part. Nothing has to cross between parts.
All inputs are finite; a program needn't handle non-finite values.
Results may differ from the reference program's by a relative error of at most 0.012.
Values may be sent and summed in bfloat16 or wider, within the bound.
A program may use at most 64 MiB of HBM per device.

```python
import jax
import jax.numpy as jnp
from jax import lax

C_IN = 64
WIDTH = 128
TEACHER_CH = 512
ROWS = 32
COLS = 256


def draw_teacher(key, part):
    base_key = jax.random.fold_in(key, 7)
    value_key, order_key = jax.random.split(base_key, 2)
    ranking = jax.random.permutation(order_key, TEACHER_CH)
    channel_scale = jnp.power(10.0, ranking.astype(jnp.float32) / (TEACHER_CH - 1))
    values = jnp.clip(jax.random.normal(value_key, (ROWS, COLS, TEACHER_CH), jnp.float32), -4.0, 4.0)
    return (values * channel_scale).astype(jnp.bfloat16)


def block_levels(stream_key, shape, cuts, smallest, high):
    level, own = 1.0, jax.random.fold_in(stream_key, 6)
    for axis_at, blocks in cuts:
        steps = jnp.exp(jax.random.uniform(jax.random.fold_in(own, axis_at), (blocks,), jnp.float32, smallest / len(cuts), high / len(cuts)))
        level = level * jnp.repeat(steps, shape[axis_at] // blocks).reshape([-1 if axis == axis_at else 1 for axis in range(len(shape))])
    return level


def normal_values(own_key, dims, deviation, reach, pieces=(), kind=jnp.bfloat16):
    values = deviation * jax.random.normal(own_key, dims, jnp.float32)
    if pieces:
        values = values * block_levels(own_key, dims, pieces, -0.22, 0.18)
    return jnp.clip(values, -reach, reach).astype(kind)


def setup_inputs(seed: int = 0, part: int = 0) -> dict:
    keys = jax.random.split(jax.random.key(seed), 6)
    own_keys = jax.random.split(jax.random.fold_in(keys[5], part), 6)
    image_feats = normal_values(own_keys[0], (ROWS, COLS * C_IN), 1.0, 6.0, ((1, 16),))
    teacher = draw_teacher(jax.random.fold_in(jax.random.fold_in(keys[5], part), 71), part)
    w_first = normal_values(keys[2], (WIDTH, 9 * C_IN), (9 * C_IN) ** -0.5, 0.25, ((0, 16),))
    w_middle = normal_values(keys[3], (WIDTH, 9 * WIDTH), (9 * WIDTH) ** -0.5, 0.1875, ((0, 16),))
    w_last = normal_values(keys[4], (TEACHER_CH, 9 * WIDTH), (9 * WIDTH) ** -0.5, 0.1875, ((0, 16),))
    return dict(image_feats=image_feats, teacher=teacher, w_first=w_first, w_middle=w_middle, w_last=w_last)


epsilon = 1e-06

def to_kernel(weight, depth):
    outputs = weight.shape[0]
    return weight.astype(jnp.float32).reshape(outputs, 3, 3, depth).transpose(1, 2, 3, 0)

def from_kernel(kernel):
    return kernel.transpose(3, 0, 1, 2).reshape(kernel.shape[3], -1)

def conv_layer(inputs, kernel, spread):
    result = lax.conv_general_dilated(inputs[None], kernel, (1, 1), [(spread, spread), (spread, spread)], rhs_dilation=(spread, spread), dimension_numbers=('NHWC', 'HWIO', 'NHWC'), precision=lax.Precision.HIGHEST)
    return result[0]

def silu_slope(pre):
    sigma = jax.nn.sigmoid(pre)
    return sigma * (1.0 + pre * (1.0 - sigma))

def reference(image_feats, teacher, w_first, w_middle, w_last):
    stem = image_feats.reshape(ROWS, COLS, C_IN).astype(jnp.float32)
    kernel_first = to_kernel(w_first, C_IN)
    kernel_middle = to_kernel(w_middle, WIDTH)
    kernel_last = to_kernel(w_last, WIDTH)
    first_pre = conv_layer(stem, kernel_first, 2)
    first_act = jax.nn.silu(first_pre).astype(jnp.bfloat16)
    second_pre = conv_layer(first_act.astype(jnp.float32), kernel_middle, 4)
    second_act = jax.nn.silu(second_pre).astype(jnp.bfloat16)
    student = conv_layer(second_act.astype(jnp.float32), kernel_last, 8)
    s_norm = jnp.sqrt(lax.optimization_barrier(jnp.sum(student * student, -1, keepdims=True)) + epsilon)
    target = teacher.astype(jnp.float32)
    t_norm = jnp.sqrt(lax.optimization_barrier(jnp.sum(target * target, -1, keepdims=True)) + epsilon)
    s_unit = student / s_norm
    differ = s_unit - target / t_norm
    slope = ((differ - s_unit * lax.optimization_barrier(jnp.sum(s_unit * differ, -1, keepdims=True))) / s_norm).astype(jnp.bfloat16)
    unused, back_last = jax.vjp(lambda acts, kern: conv_layer(acts, kern, 8), second_act.astype(jnp.float32), kernel_last)
    back_second, kgrad_last = back_last(slope.astype(jnp.float32))
    slope_second = (back_second * silu_slope(second_pre)).astype(jnp.bfloat16)
    unused, back_middle = jax.vjp(lambda acts, kern: conv_layer(acts, kern, 4), first_act.astype(jnp.float32), kernel_middle)
    back_first, kgrad_middle = back_middle(slope_second.astype(jnp.float32))
    slope_first = (back_first * silu_slope(first_pre)).astype(jnp.bfloat16)
    unused, back_stem = jax.vjp(lambda kern: conv_layer(stem, kern, 2), kernel_first)
    kgrad_first = back_stem(slope_first.astype(jnp.float32))[0]
    return (from_kernel(kgrad_first), from_kernel(kgrad_middle), from_kernel(kgrad_last))
```

```python
import functools

import jax
import jax.numpy as jnp
from jax import lax
from jax.experimental import pallas as pl
from jax.experimental.pallas import tpu as pltpu
from jax.sharding import PartitionSpec as P

epsilon = 1e-06
MESH = pl.DeviceIdType.MESH
LANES = 128
F32 = jnp.float32
BF16 = jnp.bfloat16


def split_axis(n):
    half = n // 2
    y = 1
    while 4 * y * y <= half:
        y *= 2
    return half // y, y


def place(n, z_size, y_size):
    me = lax.axis_index("cols")
    core = lax.rem(me, 2)
    y = lax.rem(me // 2, y_size)
    z = me // (2 * y_size)
    return me, z, y, core


def at(z, y, core, y_size):
    return {"cols": (z * y_size + y) * 2 + core}


def greet(peers):
    barrier = pltpu.get_barrier_semaphore()
    for peer in peers:
        pl.semaphore_signal(barrier, inc=1, device_id=peer, device_id_type=MESH)
    pl.semaphore_wait(barrier, len(peers))


def gather_kernel(n, zs, ys, edge, p_ref, x_ref, g_ref, xh_ref, sz, rz, sy, ry, sc, rc, sx, rx):
    me, z, y, core = place(n, zs, ys)
    other = 1 - core
    zmod = [lax.rem(z + i, zs) for i in range(zs)]
    zback = [lax.rem(z + zs - i, zs) for i in range(zs)]
    ymod = [lax.rem(y + i, ys) for i in range(ys)]
    yback = [lax.rem(y + ys - i, ys) for i in range(ys)]
    left, right = lax.rem(me + n - 1, n), lax.rem(me + 1, n)
    greet(
        [at(zmod[i], y, core, ys) for i in range(1, zs)]
        + [at(z, ymod[j], core, ys) for j in range(1, ys)]
        + [at(z, y, other, ys), {"cols": left}, {"cols": right}]
    )

    def block(zi, yi, c):
        return g_ref.at[zi, yi, c]

    def to_z(i):
        return pltpu.make_async_remote_copy(
            p_ref, block(z, y, core), sz.at[i], rz.at[i],
            device_id=at(zmod[i], y, core, ys), device_id_type=MESH)

    def from_z(i):
        return pltpu.make_async_remote_copy(
            p_ref, block(zback[i], y, core), sz.at[i], rz.at[i],
            device_id=at(zmod[i], y, core, ys), device_id_type=MESH)

    def to_y(j, i):
        src = p_ref if i == 0 else block(zback[i], y, core)
        return pltpu.make_async_remote_copy(
            src, block(zback[i], y, core), sy.at[j, i], ry.at[j, i],
            device_id=at(z, ymod[j], core, ys), device_id_type=MESH)

    def from_y(j, i):
        return pltpu.make_async_remote_copy(
            p_ref, block(zback[i], yback[j], core), sy.at[j, i], ry.at[j, i],
            device_id=at(z, ymod[j], core, ys), device_id_type=MESH)

    def to_core(j, i):
        src = p_ref if i == 0 and j == 0 else block(zback[i], yback[j], core)
        return pltpu.make_async_remote_copy(
            src, block(zback[i], yback[j], core), sc.at[j, i], rc.at[j, i],
            device_id=at(z, y, other, ys), device_id_type=MESH)

    def from_core(j, i):
        return pltpu.make_async_remote_copy(
            p_ref, block(zback[i], yback[j], other), sc.at[j, i], rc.at[j, i],
            device_id=at(z, y, other, ys), device_id_type=MESH)

    cells = x_ref.shape[0]
    to_right = pltpu.make_async_remote_copy(
        x_ref.at[pl.ds(cells - edge, edge)], xh_ref.at[0], sx.at[0], rx.at[0],
        device_id={"cols": right}, device_id_type=MESH)
    to_left = pltpu.make_async_remote_copy(
        x_ref.at[pl.ds(0, edge)], xh_ref.at[1], sx.at[1], rx.at[1],
        device_id={"cols": left}, device_id_type=MESH)
    started = []

    def go(copy):
        copy.start()
        started.append(copy)

    for i in range(1, zs):
        go(to_z(i))
    for j in range(1, ys):
        go(to_y(j, 0))
    go(to_right)
    go(to_left)
    go(to_core(0, 0))
    g_ref[z, y, core] = p_ref[...]
    for i in range(1, zs):
        from_z(i).wait_recv()
        for j in range(1, ys):
            go(to_y(j, i))
        go(to_core(0, i))
    for i in range(zs):
        for j in range(1, ys):
            from_y(j, i).wait_recv()
            go(to_core(j, i))
    to_right.wait_recv()
    to_left.wait_recv()
    for i in range(zs):
        for j in range(ys):
            from_core(j, i).wait_recv()
    for copy in started:
        copy.wait_send()


def gather(n, packed, x_cells, edge):
    zs, ys = split_axis(n)
    sem = pltpu.SemaphoreType.DMA
    vmem = pl.BlockSpec(memory_space=pltpu.VMEM)
    return pl.pallas_call(
        functools.partial(gather_kernel, n, zs, ys, edge),
        out_shape=(
            jax.ShapeDtypeStruct((zs, ys, 2) + packed.shape, BF16),
            jax.ShapeDtypeStruct((2, edge, x_cells.shape[1]), BF16),
        ),
        in_specs=[vmem, vmem],
        out_specs=(vmem, vmem),
        scratch_shapes=[
            sem((zs,)), sem((zs,)), sem((ys, zs)), sem((ys, zs)), sem((ys, zs)), sem((ys, zs)),
            sem((2,)), sem((2,)),
        ],
        compiler_params=pltpu.CompilerParams(
            collective_id=0, has_side_effects=True, vmem_limit_bytes=48 << 20),
        name="gather_weights",
    )(packed, x_cells)


def scatter_kernel(n, zs, ys, t_ref, out_ref, s1, s2, bufc, bufy, bufz, sc, rc, sy, ry, sz, rz):
    me, z, y, core = place(n, zs, ys)
    other = 1 - core
    zmod = [lax.rem(z + i, zs) for i in range(zs)]
    ymod = [lax.rem(y + i, ys) for i in range(ys)]
    greet(
        [at(zmod[i], y, core, ys) for i in range(1, zs)]
        + [at(z, ymod[j], core, ys) for j in range(1, ys)]
        + [at(z, y, other, ys)]
    )
    zorder = list(range(1, zs)) + [0]
    yorder = list(range(1, ys)) + [0]

    def core_copy(j, i):
        return pltpu.make_async_remote_copy(
            t_ref.at[zmod[i], ymod[j], other], bufc.at[j, i], sc.at[j, i], rc.at[j, i],
            device_id=at(z, y, other, ys), device_id_type=MESH)

    def y_copy(j, i):
        return pltpu.make_async_remote_copy(
            s1.at[j, i], bufy.at[j, i], sy.at[j, i], ry.at[j, i],
            device_id=at(z, ymod[j], core, ys), device_id_type=MESH)

    def z_copy(i):
        return pltpu.make_async_remote_copy(
            s2.at[i], bufz.at[i], sz.at[i], rz.at[i],
            device_id=at(zmod[i], y, core, ys), device_id_type=MESH)

    started = []

    def go(copy):
        copy.start()
        started.append(copy)

    for j in yorder:
        for i in zorder:
            go(core_copy(j, i))
    for j in yorder:
        for i in zorder:
            core_copy(j, i).wait_recv()
            both = t_ref[zmod[i], ymod[j], core].astype(F32) + bufc[j, i].astype(F32)
            s1[j, i] = both.astype(BF16)
            if j:
                go(y_copy(j, i))
    for i in zorder:
        total = s1[0, i].astype(F32)
        for j in range(1, ys):
            y_copy(j, i).wait_recv()
            total = total + bufy[j, i].astype(F32)
        if i:
            s2[i] = total.astype(BF16)
            go(z_copy(i))
        else:
            out_ref[...] = total
    for i in range(1, zs):
        z_copy(i).wait_recv()
        out_ref[...] = out_ref[...] + bufz[i].astype(F32)
    for copy in started:
        copy.wait_send()


def scatter(n, terms):
    zs, ys = split_axis(n)
    sem = pltpu.SemaphoreType.DMA
    block = terms.shape[3:]
    vmem = pl.BlockSpec(memory_space=pltpu.VMEM)
    return pl.pallas_call(
        functools.partial(scatter_kernel, n, zs, ys),
        out_shape=jax.ShapeDtypeStruct(block, F32),
        in_specs=[vmem],
        out_specs=vmem,
        scratch_shapes=[
            pltpu.VMEM((ys, zs) + block, BF16),
            pltpu.VMEM((zs,) + block, BF16),
            pltpu.VMEM((ys, zs) + block, BF16),
            pltpu.VMEM((ys, zs) + block, BF16),
            pltpu.VMEM((zs,) + block, BF16),
            sem((ys, zs)), sem((ys, zs)), sem((ys, zs)), sem((ys, zs)), sem((zs,)), sem((zs,)),
        ],
        compiler_params=pltpu.CompilerParams(
            collective_id=2, has_side_effects=True, vmem_limit_bytes=48 << 20),
        name="scatter_terms",
    )(terms)


def row_of(count, height):
    return lax.rem(lax.broadcasted_iota(jnp.int32, (count, LANES), 0), height)


def column_of(count, height, first):
    return lax.broadcasted_iota(jnp.int32, (count, LANES), 0) // height + first


def from_above(v, d, height):
    return jnp.where(row_of(v.shape[0], height) >= d, pltpu.roll(v, d, 0), 0.0)


def from_below(v, d, height):
    count = v.shape[0]
    return jnp.where(row_of(count, height) < height - d, pltpu.roll(v, count - d, 0), 0.0)


def spread_rows(ref, v, d, height):
    ref[:, 0:LANES] = from_above(v, d, height).astype(BF16)
    ref[:, LANES : 2 * LANES] = v.astype(BF16)
    ref[:, 2 * LANES : 3 * LANES] = from_below(v, d, height).astype(BF16)


def sigmoid(v):
    return 1.0 / (1.0 + jnp.exp(-v))


def silu_slope(pre):
    sigma = sigmoid(pre)
    return sigma * (1.0 + pre * (1.0 - sigma))


def conv(ref, w_ref, start, step, count):
    total = None
    for kx in range(3):
        term = lax.dot_general(
            ref[pl.ds(start + kx * step, count), :],
            w_ref[:, kx * 3 * LANES : (kx + 1) * 3 * LANES],
            (((1,), (1,)), ((), ())),
            preferred_element_type=F32,
        )
        total = term if total is None else total + term
    return total


def gather_rows(prod, d, height, kx):
    base = kx * 3 * LANES
    up = from_below(prod[:, base : base + LANES], d, height)
    same = prod[:, base + LANES : base + 2 * LANES]
    down = from_above(prod[:, base + 2 * LANES : base + 3 * LANES], d, height)
    return up + same + down


def weight_grad(out_ref, slope_f32, ref, start, step):
    count = slope_f32.shape[0]
    turned = slope_f32.T.astype(BF16)
    for kx in range(3):
        out_ref[:, kx * 3 * LANES : (kx + 1) * 3 * LANES] = jnp.dot(
            turned, ref[pl.ds(start + kx * step, count), :], preferred_element_type=F32
        ).astype(BF16)


def step_kernel(
    n, height, breadth,
    x_ref, xh_ref, t_ref, w1_ref, w2_ref, w3_ref, g1_ref, g2_ref, g3_ref,
    x3x, x3f, x3s, pre1, pre2, acc, send, recv, ssem, rsem,
):
    me = lax.axis_index("cols")
    left, right = lax.rem(me + n - 1, n), lax.rem(me + 1, n)
    greet([{"cols": left}, {"cols": right}])
    h, b = height, breadth
    first_col = me * b
    width = n * b

    def inside(v, first):
        cols = column_of(v.shape[0], h, first_col + first)
        return jnp.where((cols >= 0) & (cols < width), v, 0.0)

    wide_x = jnp.concatenate([xh_ref[0], x_ref[...], xh_ref[1]], axis=0).astype(F32)
    spread_rows(x3x, inside(wide_x, -14), 2, h)
    v = conv(x3x, w1_ref, 0, 2 * h, (b + 24) * h)
    pre1[...] = v
    act = inside(v * sigmoid(v), -12).astype(BF16).astype(F32)
    spread_rows(x3f, act, 4, h)
    v = conv(x3f, w2_ref, 0, 4 * h, (b + 16) * h)
    pre2[...] = v
    act = inside(v * sigmoid(v), -8).astype(BF16).astype(F32)
    spread_rows(x3s, act, 8, h)
    student = conv(x3s, w3_ref, 0, 8 * h, b * h)
    s_norm = jnp.sqrt(jnp.sum(student * student, -1, keepdims=True) + epsilon)
    target = t_ref[...].astype(F32)
    t_norm = jnp.sqrt(jnp.sum(target * target, -1, keepdims=True) + epsilon)
    s_unit = student / s_norm
    differ = s_unit - target / t_norm
    slope = (differ - s_unit * jnp.sum(s_unit * differ, -1, keepdims=True)) / s_norm
    slope_b = slope.astype(BF16)

    prod = jnp.dot(slope_b, w3_ref[...], preferred_element_type=F32)
    u0 = gather_rows(prod, 8, h, 0)
    u1 = gather_rows(prod, 8, h, 1)
    u2 = gather_rows(prod, 8, h, 2)
    e = 8 * h
    m = b * h
    acc[pl.ds(0, m), :] = u0
    acc[pl.ds(m, 2 * e), :] = jnp.zeros((2 * e, LANES), F32)
    acc[pl.ds(e, m), :] += u1
    acc[pl.ds(2 * e, m), :] += u2
    part = 12 * h
    send[0] = acc[pl.ds(m + 2 * e - part, part), :].astype(BF16)
    send[1] = acc[pl.ds(0, part), :].astype(BF16)
    copies = []
    for side, target_id in ((0, right), (1, left)):
        copy = pltpu.make_async_remote_copy(
            send.at[side], recv.at[side], ssem.at[side], rsem.at[side],
            device_id={"cols": target_id}, device_id_type=MESH)
        copy.start()
        copies.append(copy)
    weight_grad(g3_ref, slope, x3s, 0, 8 * h)
    for copy in copies:
        copy.wait()
    inner = (b + 8) * h
    split = inner - part
    from_left = jnp.where(me > 0, recv[0].astype(F32), 0.0)
    from_right = jnp.where(me < n - 1, recv[1].astype(F32), 0.0)
    acc[pl.ds(4 * h, part), :] += from_left
    acc[pl.ds(4 * h + split, part), :] += from_right
    back = acc[pl.ds(4 * h, inner), :]
    slope2 = inside(back * silu_slope(pre2[pl.ds(4 * h, inner), :]), -4).astype(BF16)
    prod = jnp.dot(slope2, w2_ref[...], preferred_element_type=F32)
    back = (
        gather_rows(prod, 4, h, 0)[8 * h : 8 * h + m]
        + gather_rows(prod, 4, h, 1)[4 * h : 4 * h + m]
        + gather_rows(prod, 4, h, 2)[0:m]
    )
    weight_grad(g2_ref, slope2.astype(F32)[4 * h : 4 * h + m], x3f, 8 * h, 4 * h)
    slope1 = back * silu_slope(pre1[pl.ds(12 * h, m), :])
    weight_grad(g1_ref, slope1, x3x, 12 * h, 2 * h)


def local_step(n, height, breadth, x_cells, x_edges, teacher, w1, w2, w3):
    sem = pltpu.SemaphoreType.DMA
    vmem = pl.BlockSpec(memory_space=pltpu.VMEM)
    h, b = height, breadth
    return pl.pallas_call(
        functools.partial(step_kernel, n, h, b),
        out_shape=tuple(jax.ShapeDtypeStruct(w.shape, BF16) for w in (w1, w2, w3)),
        in_specs=[vmem] * 6,
        out_specs=(vmem,) * 3,
        scratch_shapes=[
            pltpu.VMEM(((b + 28) * h, 3 * LANES), BF16),
            pltpu.VMEM(((b + 24) * h, 3 * LANES), BF16),
            pltpu.VMEM(((b + 16) * h, 3 * LANES), BF16),
            pltpu.VMEM(((b + 24) * h, LANES), F32),
            pltpu.VMEM(((b + 16) * h, LANES), F32),
            pltpu.VMEM(((b + 16) * h, LANES), F32),
            pltpu.VMEM((2, 12 * h, LANES), BF16),
            pltpu.VMEM((2, 12 * h, LANES), BF16),
            sem((2,)), sem((2,)),
        ],
        compiler_params=pltpu.CompilerParams(
            collective_id=1, has_side_effects=True, vmem_limit_bytes=56 << 20),
        name="student_step",
    )(x_cells, x_edges, teacher, w1, w2, w3)


def taps_by_column(w):
    rows, depth = w.shape[0], w.shape[1] // 9
    w = w.reshape(rows, 3, 3, depth).transpose(0, 2, 1, 3)
    w = jnp.pad(w, ((0, 0), (0, 0), (0, 0), (0, LANES - depth)))
    return w.reshape(rows, 9 * LANES)


def taps_by_row(g, depth):
    rows = g.shape[0]
    g = g.reshape(rows, 3, 3, LANES)[..., :depth].transpose(0, 2, 1, 3)
    return g.reshape(rows, 9 * depth)


class Line:
    def __init__(self, pos, zs, ys, src, out, first, rows, sems):
        self.pos, self.zs, self.ys = pos, zs, ys
        self.rows = pl.ds(first, rows)
        self.src, self.out = src.at[self.rows], out
        self.szr, self.rzr, self.szl, self.rzl, self.sy, self.ry, self.sc, self.rc = sems

    def copy(self, src, dst, ssem, rsem, device):
        return pltpu.make_async_remote_copy(
            src, dst, ssem, rsem, device_id=device, device_id_type=MESH)

    def block(self, zi, yi, c):
        return self.out.at[zi, yi, c, self.rows]

    def hop(self, way, s):
        z, y, core = self.pos
        zi = z - way * s
        src = self.src if s == 0 else self.block(zi, y, core)
        ss, rs = (self.szr, self.rzr) if way > 0 else (self.szl, self.rzl)
        ok = (zi >= 0) & (zi < self.zs) & (z + way >= 0) & (z + way < self.zs)
        return ok, self.copy(
            src, self.block(zi, y, core), ss.at[s], rs.at[s + 1], at(z + way, y, core, self.ys))

    def arrived(self, way, s):
        z, y, core = self.pos
        zi = z - way * s
        ss, rs = (self.szr, self.rzr) if way > 0 else (self.szl, self.rzl)
        ok = (zi >= 0) & (zi < self.zs)
        return ok, zi, self.copy(
            self.src, self.block(zi, y, core), ss.at[0], rs.at[s], at(z, y, 1 - core, self.ys))

    def to_y(self, j, zi, own):
        z, y, core = self.pos
        src = self.src if own else self.block(zi, y, core)
        return self.copy(src, self.block(zi, y, core), self.sy.at[j, zi], self.ry.at[j, zi],
                         at(z, lax.rem(y + j, self.ys), core, self.ys))

    def from_y(self, j, zi):
        z, y, core = self.pos
        yi = lax.rem(y + self.ys - j, self.ys)
        return self.copy(self.src, self.block(zi, yi, core), self.sy.at[j, zi], self.ry.at[j, zi],
                         at(z, lax.rem(y + j, self.ys), core, self.ys))

    def to_core(self, j, zi, own):
        z, y, core = self.pos
        yi = lax.rem(y + self.ys - j, self.ys)
        src = self.src if own else self.block(zi, yi, core)
        return self.copy(src, self.block(zi, yi, core), self.sc.at[j, zi], self.rc.at[j, zi],
                         at(z, y, 1 - core, self.ys))

    def from_core(self, j, zi):
        z, y, core = self.pos
        yi = lax.rem(y + self.ys - j, self.ys)
        return self.copy(self.src, self.block(zi, yi, 1 - core), self.sc.at[j, zi],
                         self.rc.at[j, zi], at(z, y, 1 - core, self.ys))

    def start(self):
        z, y, core = self.pos
        for way in (1, -1):
            ok, copy = self.hop(way, 0)
            pl.when(ok)(copy.start)
        for j in range(1, self.ys):
            self.to_y(j, z, True).start()
        self.to_core(0, z, True).start()
        self.out[z, y, core, self.rows] = self.src[...]

    def forward_z(self, s):
        for way in (1, -1):
            ok, zi, here = self.arrived(way, s)

            @pl.when(ok)
            def _():
                here.wait_recv()
                for j in range(1, self.ys):
                    self.to_y(j, zi, False).start()

            if s < self.zs - 1:
                more, on = self.hop(way, s)
                pl.when(more)(on.start)

            @pl.when(ok)
            def _():
                self.to_core(0, zi, False).start()

    def forward_y(self, s):
        z = self.pos[0]
        todo = [(None, z)] if s == 0 else [
            ((z - way * s >= 0) & (z - way * s < self.zs), z - way * s) for way in (1, -1)]
        for ok, zi in todo:

            def step(zi=zi):
                for j in range(1, self.ys):
                    self.from_y(j, zi).wait_recv()
                    self.to_core(j, zi, False).start()

            step() if ok is None else pl.when(ok)(step)

    def finish(self):
        for zi in range(self.zs):
            for j in range(self.ys):
                self.from_core(j, zi).wait_recv()

    def drain(self):
        for s in range(self.zs - 1):
            for way in (1, -1):
                ok, copy = self.hop(way, s)
                pl.when(ok)(copy.wait_send)
        for zi in range(self.zs):
            for j in range(self.ys):
                if j:
                    self.to_y(j, zi, False).wait_send()
                self.to_core(j, zi, False).wait_send()


class Sum:
    def __init__(self, pos, zs, ys, terms, bufs, sems):
        self.pos, self.zs, self.ys, self.terms = pos, zs, ys, terms
        self.s1, self.s2, self.bufc, self.bufy, self.bufz = bufs
        self.sc, self.rc, self.sy, self.ry, self.sz, self.rz = sems
        self.zorder = list(range(1, zs)) + [0]
        self.yorder = list(range(1, ys)) + [0]

    def zi(self, i):
        return lax.rem(self.pos[0] + i, self.zs)

    def yi(self, j):
        return lax.rem(self.pos[1] + j, self.ys)

    def copy(self, src, dst, ssem, rsem, device):
        return pltpu.make_async_remote_copy(
            src, dst, ssem, rsem, device_id=device, device_id_type=MESH)

    def core_copy(self, j, i):
        z, y, core = self.pos
        return self.copy(self.terms.at[self.zi(i), self.yi(j), 1 - core], self.bufc.at[j, i],
                         self.sc.at[j, i], self.rc.at[j, i], at(z, y, 1 - core, self.ys))

    def y_copy(self, j, i):
        z, y, core = self.pos
        return self.copy(self.s1.at[j, i], self.bufy.at[j, i], self.sy.at[j, i],
                         self.ry.at[j, i], at(z, self.yi(j), core, self.ys))

    def z_copy(self, i):
        z, y, core = self.pos
        return self.copy(self.s2.at[i], self.bufz.at[i], self.sz.at[i], self.rz.at[i],
                         at(self.zi(i), y, core, self.ys))

    def start(self):
        for j in self.yorder:
            for i in self.zorder:
                self.core_copy(j, i).start()

    def pair(self):
        core = self.pos[2]
        for j in self.yorder:
            for i in self.zorder:
                self.core_copy(j, i).wait_recv()
                both = self.terms[self.zi(i), self.yi(j), core].astype(F32)
                self.s1[j, i] = (both + self.bufc[j, i].astype(F32)).astype(BF16)
                if j:
                    self.y_copy(j, i).start()

    def along_y(self, begin, end):
        for i in self.zorder[begin:end]:
            total = self.s1[0, i].astype(F32)
            for j in range(1, self.ys):
                self.y_copy(j, i).wait_recv()
                total = total + self.bufy[j, i].astype(F32)
            if i:
                self.s2[i] = total.astype(BF16)
                self.z_copy(i).start()
            else:
                self.own = total

    def along_z(self):
        total = self.own
        for i in range(1, self.zs):
            self.z_copy(i).wait_recv()
            total = total + self.bufz[i].astype(F32)
        return total

    def drain(self):
        for j in self.yorder:
            for i in self.zorder:
                self.core_copy(j, i).wait_send()
                if j:
                    self.y_copy(j, i).wait_send()
        for i in range(1, self.zs):
            self.z_copy(i).wait_send()


def tap(t):
    return slice(t * LANES, (t + 1) * LANES)


def conv_taps(ref, w, start, step, count):
    total = None
    for kx in range(3):
        rhs = jnp.concatenate([w[:, tap(3 * ky + kx)] for ky in range(3)], axis=1)
        term = lax.dot_general(ref[pl.ds(start + kx * step, count), :], rhs,
                               (((1,), (1,)), ((), ())), preferred_element_type=F32)
        total = term if total is None else total + term
    return total


def join_rows(prod, d, height, kx):
    up = from_below(prod[:, tap(kx)], d, height)
    down = from_above(prod[:, tap(6 + kx)], d, height)
    return up + prod[:, tap(3 + kx)] + down


def put_terms(ref, rows, t, value):
    zs, ys = ref.shape[0], ref.shape[1]
    count = rows[1] - rows[0]
    ref[:, :, :, rows[0] : rows[1], tap(t)] = value.reshape(zs, ys, 2, count, LANES).astype(BF16)


def grad_taps(ref, rows, slope_f32, acts, start, step):
    count = slope_f32.shape[0]
    turned = slope_f32.T.astype(BF16)
    for kx in range(3):
        prod = jnp.dot(turned, acts[pl.ds(start + kx * step, count), :],
                       preferred_element_type=F32)
        for ky in range(3):
            put_terms(ref, rows, 3 * ky + kx, prod[:, tap(ky)])


def fused_kernel(
    n, zs, ys, height, breadth, rl, rm, rf,
    x_ref, t_ref, wl_ref, wm_ref, wf_ref, o1_ref, o2_ref, o3_ref,
    pa, ga, gb, ta, tb, xh, xs, x9, x3f, x3s, pre1, pre2, acc, send, recv, tf, tn,
    a1, a2, a3, a4, a5, b1, b2, b3, b4, b5, sx, rx, ssem, rsem, *sems,
):
    me, z, y, core = place(n, zs, ys)
    pos = (z, y, core)
    h, b = height, breadth
    depth = wf_ref.shape[1] // 9
    left, right = lax.rem(me + n - 1, n), lax.rem(me + 1, n)
    low = Line(pos, zs, ys, pa, ga, 0, rm + rf, sems[0:8])
    cut = rl // 16 * 8
    parts = ((0, cut), (cut, rl - cut)) if cut else ((0, rl),)
    high = [Line(pos, zs, ys, wl_ref, gb, first, rows, sems[8 * i + 8 : 8 * i + 16])
            for i, (first, rows) in enumerate(parts)]
    lines = [low] + high
    sum_a = Sum(pos, zs, ys, ta, (a1, a2, a3, a4, a5), sems[24:30])
    sum_b = Sum(pos, zs, ys, tb, (b1, b2, b3, b4, b5), sems[30:36])
    pa[0:rm, :] = wm_ref[...]
    pa[rm : rm + rf, :] = jnp.zeros((rf, pa.shape[1]), BF16)
    pa[rm : rm + rf, 0 : 9 * depth] = wf_ref[...]
    greet(
        [at(lax.rem(z + i, zs), y, core, ys) for i in range(1, zs)]
        + [at(z, lax.rem(y + j, ys), core, ys) for j in range(1, ys)]
        + [at(z, y, 1 - core, ys), {"cols": left}, {"cols": right}]
    )
    edge = 14 * depth
    halo = []
    for side, peer, first in ((0, right, b * depth - edge), (1, left, 0)):
        copy = pltpu.make_async_remote_copy(
            x_ref.at[:, pl.ds(first, edge)], xh.at[side], sx.at[side], rx.at[side],
            device_id={"cols": peer}, device_id_type=MESH)
        copy.start()
        halo.append(copy)
    for line in lines:
        line.start()

    target = t_ref[...].astype(F32)
    t_norm = jnp.sqrt(jnp.sum(target * target, -1, keepdims=True) + epsilon)
    target = target / t_norm
    for q in range(tf.shape[0]):
        tf[q] = target[:, tap(q)]
    for c in range(b):
        for q in range(tf.shape[0]):
            tn[pl.ds(c * h, h), tap(q)] = tf[q, pl.ds(c, h, stride=b), :]
    for line in lines:
        line.forward_z(1)

    first_col = me * b
    width = n * b

    def inside(v, first):
        cols = column_of(v.shape[0], h, first_col + first)
        return jnp.where((cols >= 0) & (cols < width), v, 0.0)

    for copy in halo:
        copy.wait()
    half = lax.broadcasted_iota(jnp.int32, (h, LANES), 1) < depth
    at_col = 0
    for part, pairs in ((xh[0], 7), (x_ref[...], b // 2), (xh[1], 7)):
        part = part.astype(F32)
        for q in range(pairs):
            both = part[:, tap(q)]
            turned = pltpu.roll(both, depth, 1)
            xs[pl.ds(at_col * h, h), :] = jnp.where(half, both, turned)
            xs[pl.ds((at_col + 1) * h, h), :] = jnp.where(half, turned, both)
            at_col += 2
    for line in lines:
        line.forward_z(2)
    wide_x = inside(xs[...], -14)
    count1 = (b + 24) * h
    rows3 = (from_above(wide_x, 2, h), wide_x, from_below(wide_x, 2, h))

    def piece(t):
        ky, kx = t // 3, t % 3
        return rows3[ky][kx * 2 * h : kx * 2 * h + count1]

    lower = lax.broadcasted_iota(jnp.int32, (count1, LANES), 1) < depth
    for q in range(5):
        odd = piece(2 * q + 1) if q < 4 else 0.0
        x9[:, tap(q)] = jnp.where(lower, piece(2 * q), odd).astype(BF16)
    for s in range(3, zs):
        for line in lines:
            line.forward_z(s)
    for s in range(zs):
        low.forward_y(s)
    for line in high:
        for s in range(zs - 1):
            line.forward_y(s)
    low.finish()
    w1 = ga[:, :, :, rm : rm + rf, 0 : 5 * LANES].reshape(n * rf, 5 * LANES)
    v = lax.dot_general(x9[...], w1, (((1,), (1,)), ((), ())), preferred_element_type=F32)
    pre1[...] = v
    act = inside(v * sigmoid(v), -12).astype(BF16).astype(F32)
    spread_rows(x3f, act, 4, h)
    for line in high:
        line.forward_y(zs - 1)
    w2 = ga[:, :, :, 0:rm, :].reshape(n * rm, 9 * LANES)
    v = conv_taps(x3f, w2, 0, 4 * h, (b + 16) * h)
    pre2[...] = v
    act = inside(v * sigmoid(v), -8).astype(BF16).astype(F32)
    spread_rows(x3s, act, 8, h)
    for line in high:
        line.finish()
    w3 = gb[...].reshape(n * rl, 9 * LANES)
    student = conv_taps(x3s, w3, 0, 8 * h, b * h)
    s_norm = jnp.sqrt(jnp.sum(student * student, -1, keepdims=True) + epsilon)
    s_unit = student / s_norm
    differ = s_unit - tn[...]
    slope = (differ - s_unit * jnp.sum(s_unit * differ, -1, keepdims=True)) / s_norm

    prod = jnp.dot(slope.astype(BF16), w3, preferred_element_type=F32)
    e = 8 * h
    m = b * h
    acc[pl.ds(0, m), :] = join_rows(prod, 8, h, 0)
    acc[pl.ds(m, 2 * e), :] = jnp.zeros((2 * e, LANES), F32)
    acc[pl.ds(e, m), :] += join_rows(prod, 8, h, 1)
    acc[pl.ds(2 * e, m), :] += join_rows(prod, 8, h, 2)
    part = 12 * h
    send[0] = acc[pl.ds(m + 2 * e - part, part), :].astype(BF16)
    send[1] = acc[pl.ds(0, part), :].astype(BF16)
    copies = []
    for side, peer in ((0, right), (1, left)):
        copy = pltpu.make_async_remote_copy(
            send.at[side], recv.at[side], ssem.at[side], rsem.at[side],
            device_id={"cols": peer}, device_id_type=MESH)
        copy.start()
        copies.append(copy)
    grad_taps(tb, (0, rl), slope, x3s, 0, 8 * h)
    sum_b.start()
    sum_b.pair()
    for copy in copies:
        copy.wait()
    inner = (b + 8) * h
    split = inner - part
    from_left = jnp.where(me > 0, recv[0].astype(F32), 0.0)
    from_right = jnp.where(me < n - 1, recv[1].astype(F32), 0.0)
    acc[pl.ds(4 * h, part), :] += from_left
    acc[pl.ds(4 * h + split, part), :] += from_right
    back = acc[pl.ds(4 * h, inner), :]
    slope2 = inside(back * silu_slope(pre2[pl.ds(4 * h, inner), :]), -4).astype(BF16)
    prod = jnp.dot(slope2, w2, preferred_element_type=F32)
    back = (
        join_rows(prod, 4, h, 0)[8 * h : 8 * h + m]
        + join_rows(prod, 4, h, 1)[4 * h : 4 * h + m]
        + join_rows(prod, 4, h, 2)[0:m]
    )
    grad_taps(ta, (0, rm), slope2.astype(F32)[4 * h : 4 * h + m], x3f, 8 * h, 4 * h)
    slope1 = back * silu_slope(pre1[pl.ds(12 * h, m), :])
    prod = jnp.dot(slope1.T.astype(BF16), x9[pl.ds(12 * h, m), :], preferred_element_type=F32)
    for q in range(5):
        put_terms(ta, (rm, rm + rf), q, prod[:, tap(q)])
    for q in range(5, 9):
        put_terms(ta, (rm, rm + rf), q, jnp.zeros((n * rf, LANES), F32))
    sum_a.start()
    sum_b.along_y(0, 1)
    sum_a.pair()
    sum_b.along_y(1, zs)
    sum_a.along_y(0, zs)
    o3_ref[...] = sum_b.along_z()
    total = sum_a.along_z()
    o2_ref[...] = total[0:rm]
    o1_ref[...] = total[rm : rm + rf, 0 : 9 * depth]
    for each in (*lines, sum_a, sum_b):
        each.drain()


def hand_over_kernel(a_ref, b_ref, c_ref, x_ref, y_ref, z_ref):
    x_ref[...] = a_ref[...]
    y_ref[...] = b_ref[...]
    z_ref[...] = c_ref[...]


def hand_over(arrays):
    vmem = pl.BlockSpec(memory_space=pltpu.VMEM)
    return pl.pallas_call(
        hand_over_kernel,
        out_shape=tuple(jax.ShapeDtypeStruct(a.shape, a.dtype) for a in arrays),
        in_specs=[vmem] * 3,
        out_specs=(vmem,) * 3,
        name="hand_over",
    )(*(pltpu.with_memory_space_constraint(a, pltpu.VMEM) for a in arrays))


def fused(n, height, breadth, x, t, wl, wm, wf):
    zs, ys = split_axis(n)
    sem = pltpu.SemaphoreType.DMA
    vmem = pl.BlockSpec(memory_space=pltpu.VMEM)
    h, b = height, breadth
    rl, rm, rf = wl.shape[0], wm.shape[0], wf.shape[0]
    wide = wl.shape[1]
    low, high = (rm + rf, wide), (rl, wide)
    channels = t.shape[1]

    def sum_bufs(block):
        return [
            pltpu.VMEM((ys, zs) + block, BF16), pltpu.VMEM((zs,) + block, BF16),
            pltpu.VMEM((ys, zs) + block, BF16), pltpu.VMEM((ys, zs) + block, BF16),
            pltpu.VMEM((zs,) + block, BF16),
        ]

    line_sems = [sem((zs,))] * 4 + [sem((ys, zs))] * 4
    sum_sems = [sem((ys, zs))] * 4 + [sem((zs,))] * 2
    return pl.pallas_call(
        functools.partial(fused_kernel, n, zs, ys, h, b, rl, rm, rf),
        out_shape=tuple(pltpu.VMEM(w.shape, F32) for w in (wf, wm, wl)),
        in_specs=[vmem] * 5,
        out_specs=(vmem,) * 3,
        scratch_shapes=[
            pltpu.VMEM(low, BF16),
            pltpu.VMEM((zs, ys, 2) + low, BF16),
            pltpu.VMEM((zs, ys, 2) + high, BF16),
            pltpu.VMEM((zs, ys, 2) + low, BF16),
            pltpu.VMEM((zs, ys, 2) + high, BF16),
            pltpu.VMEM((2, h, 14 * wf.shape[1] // 9), BF16),
            pltpu.VMEM(((b + 28) * h, LANES), F32),
            pltpu.VMEM(((b + 24) * h, 5 * LANES), BF16),
            pltpu.VMEM(((b + 24) * h, 3 * LANES), BF16),
            pltpu.VMEM(((b + 16) * h, 3 * LANES), BF16),
            pltpu.VMEM(((b + 24) * h, LANES), F32),
            pltpu.VMEM(((b + 16) * h, LANES), F32),
            pltpu.VMEM(((b + 16) * h, LANES), F32),
            pltpu.VMEM((2, 12 * h, LANES), BF16),
            pltpu.VMEM((2, 12 * h, LANES), BF16),
            pltpu.VMEM((channels // LANES, b * h, LANES), F32),
            pltpu.VMEM((b * h, channels), F32),
        ]
        + sum_bufs(low) + sum_bufs(high)
        + [sem((2,))] * 4 + line_sems * 3 + sum_sems * 2,
        compiler_params=pltpu.CompilerParams(
            collective_id=3, has_side_effects=True, vmem_limit_bytes=56 << 20),
        name="fused_step",
    )(x, t, wl, wm, wf)


def on_device(n, image_feats, teacher, w_first, w_middle, w_last):
    height, breadth, channels = teacher.shape
    in_depth = w_first.shape[1] // 9
    rl, rm, rf = w_last.shape[0], w_middle.shape[0], w_first.shape[0]
    if split_axis(n)[0] > 2 and all(r % 8 == 0 for r in (rl, rm, rf)) and breadth % 8 == 0 and 2 * in_depth == LANES:
        return hand_over(fused(n, height, breadth, image_feats,
                               teacher.reshape(height * breadth, channels), w_last, w_middle, w_first))
    packed = jnp.concatenate([taps_by_column(w) for w in (w_last, w_middle, w_first)], axis=0)
    x = image_feats.reshape(height, breadth, in_depth).transpose(1, 0, 2)
    x = jnp.pad(x, ((0, 0), (0, 0), (0, LANES - in_depth)))
    x_cells = x.reshape(breadth * height, LANES)
    t_cells = teacher.transpose(1, 0, 2).reshape(breadth * height, channels)
    gathered, x_edges = gather(n, packed, x_cells, 14 * height)
    g = gathered.reshape((n,) + packed.shape)
    w3 = g[:, :rl].reshape(n * rl, -1)
    w2 = g[:, rl : rl + rm].reshape(n * rm, -1)
    w1 = g[:, rl + rm :].reshape(n * rf, -1)
    g1, g2, g3 = local_step(n, height, breadth, x_cells, x_edges, t_cells, w1, w2, w3)
    terms = jnp.concatenate(
        [g3.reshape(n, rl, -1), g2.reshape(n, rm, -1), g1.reshape(n, rf, -1)], axis=1)
    out = scatter(n, terms.reshape(gathered.shape))
    return (
        taps_by_row(out[rl + rm :], in_depth),
        taps_by_row(out[rl : rl + rm], LANES),
        taps_by_row(out[:rl], LANES),
    )


def solution(mesh):
    placed = (
        P("groups", "cols"),
        P("groups", "cols", None),
        P("cols", None),
        P("cols", None),
        P("cols", None),
    )
    return jax.shard_map(
        functools.partial(on_device, mesh.shape["cols"]),
        mesh=mesh,
        in_specs=placed,
        out_specs=(P(("groups", "cols"), None),) * 3,
        check_vma=False,
    )
```

```python
import functools

import jax
import jax.numpy as jnp
from jax import lax
from jax.experimental import pallas as pl
from jax.experimental.pallas import tpu as pltpu
from jax.sharding import PartitionSpec as P

epsilon = 1e-06
MESH = pl.DeviceIdType.MESH
LANES = 128
F32 = jnp.float32
BF16 = jnp.bfloat16


def split_axis(n):
    half = n // 2
    y = 1
    while 4 * y * y <= half:
        y *= 2
    return half // y, y


def place(n, z_size, y_size):
    me = lax.axis_index("cols")
    core = lax.rem(me, 2)
    y = lax.rem(me // 2, y_size)
    z = me // (2 * y_size)
    return me, z, y, core


def at(z, y, core, y_size):
    return {"cols": (z * y_size + y) * 2 + core}


def call(peers):
    barrier = pltpu.get_barrier_semaphore()
    for peer in peers:
        pl.semaphore_signal(barrier, inc=1, device_id=peer, device_id_type=MESH)


def hear(peers):
    pl.semaphore_wait(pltpu.get_barrier_semaphore(), len(peers))


def greet(peers):
    call(peers)
    hear(peers)


def gather_kernel(n, zs, ys, edge, p_ref, x_ref, g_ref, xh_ref, sz, rz, sy, ry, sc, rc, sx, rx):
    me, z, y, core = place(n, zs, ys)
    other = 1 - core
    zmod = [lax.rem(z + i, zs) for i in range(zs)]
    zback = [lax.rem(z + zs - i, zs) for i in range(zs)]
    ymod = [lax.rem(y + i, ys) for i in range(ys)]
    yback = [lax.rem(y + ys - i, ys) for i in range(ys)]
    left, right = lax.rem(me + n - 1, n), lax.rem(me + 1, n)
    greet(
        [at(zmod[i], y, core, ys) for i in range(1, zs)]
        + [at(z, ymod[j], core, ys) for j in range(1, ys)]
        + [at(z, y, other, ys), {"cols": left}, {"cols": right}]
    )

    def block(zi, yi, c):
        return g_ref.at[zi, yi, c]

    def to_z(i):
        return pltpu.make_async_remote_copy(
            p_ref, block(z, y, core), sz.at[i], rz.at[i],
            device_id=at(zmod[i], y, core, ys), device_id_type=MESH)

    def from_z(i):
        return pltpu.make_async_remote_copy(
            p_ref, block(zback[i], y, core), sz.at[i], rz.at[i],
            device_id=at(zmod[i], y, core, ys), device_id_type=MESH)

    def to_y(j, i):
        src = p_ref if i == 0 else block(zback[i], y, core)
        return pltpu.make_async_remote_copy(
            src, block(zback[i], y, core), sy.at[j, i], ry.at[j, i],
            device_id=at(z, ymod[j], core, ys), device_id_type=MESH)

    def from_y(j, i):
        return pltpu.make_async_remote_copy(
            p_ref, block(zback[i], yback[j], core), sy.at[j, i], ry.at[j, i],
            device_id=at(z, ymod[j], core, ys), device_id_type=MESH)

    def to_core(j, i):
        src = p_ref if i == 0 and j == 0 else block(zback[i], yback[j], core)
        return pltpu.make_async_remote_copy(
            src, block(zback[i], yback[j], core), sc.at[j, i], rc.at[j, i],
            device_id=at(z, y, other, ys), device_id_type=MESH)

    def from_core(j, i):
        return pltpu.make_async_remote_copy(
            p_ref, block(zback[i], yback[j], other), sc.at[j, i], rc.at[j, i],
            device_id=at(z, y, other, ys), device_id_type=MESH)

    cells = x_ref.shape[0]
    to_right = pltpu.make_async_remote_copy(
        x_ref.at[pl.ds(cells - edge, edge)], xh_ref.at[0], sx.at[0], rx.at[0],
        device_id={"cols": right}, device_id_type=MESH)
    to_left = pltpu.make_async_remote_copy(
        x_ref.at[pl.ds(0, edge)], xh_ref.at[1], sx.at[1], rx.at[1],
        device_id={"cols": left}, device_id_type=MESH)
    started = []

    def go(copy):
        copy.start()
        started.append(copy)

    for i in range(1, zs):
        go(to_z(i))
    for j in range(1, ys):
        go(to_y(j, 0))
    go(to_right)
    go(to_left)
    go(to_core(0, 0))
    g_ref[z, y, core] = p_ref[...]
    for i in range(1, zs):
        from_z(i).wait_recv()
        for j in range(1, ys):
            go(to_y(j, i))
        go(to_core(0, i))
    for i in range(zs):
        for j in range(1, ys):
            from_y(j, i).wait_recv()
            go(to_core(j, i))
    to_right.wait_recv()
    to_left.wait_recv()
    for i in range(zs):
        for j in range(ys):
            from_core(j, i).wait_recv()
    for copy in started:
        copy.wait_send()


def gather(n, packed, x_cells, edge):
    zs, ys = split_axis(n)
    sem = pltpu.SemaphoreType.DMA
    vmem = pl.BlockSpec(memory_space=pltpu.VMEM)
    return pl.pallas_call(
        functools.partial(gather_kernel, n, zs, ys, edge),
        out_shape=(
            jax.ShapeDtypeStruct((zs, ys, 2) + packed.shape, BF16),
            jax.ShapeDtypeStruct((2, edge, x_cells.shape[1]), BF16),
        ),
        in_specs=[vmem, vmem],
        out_specs=(vmem, vmem),
        scratch_shapes=[
            sem((zs,)), sem((zs,)), sem((ys, zs)), sem((ys, zs)), sem((ys, zs)), sem((ys, zs)),
            sem((2,)), sem((2,)),
        ],
        compiler_params=pltpu.CompilerParams(
            collective_id=0, has_side_effects=True, vmem_limit_bytes=48 << 20),
        name="gather_weights",
    )(packed, x_cells)


def scatter_kernel(n, zs, ys, t_ref, out_ref, s1, s2, bufc, bufy, bufz, sc, rc, sy, ry, sz, rz):
    me, z, y, core = place(n, zs, ys)
    other = 1 - core
    zmod = [lax.rem(z + i, zs) for i in range(zs)]
    ymod = [lax.rem(y + i, ys) for i in range(ys)]
    greet(
        [at(zmod[i], y, core, ys) for i in range(1, zs)]
        + [at(z, ymod[j], core, ys) for j in range(1, ys)]
        + [at(z, y, other, ys)]
    )
    zorder = list(range(1, zs)) + [0]
    yorder = list(range(1, ys)) + [0]

    def core_copy(j, i):
        return pltpu.make_async_remote_copy(
            t_ref.at[zmod[i], ymod[j], other], bufc.at[j, i], sc.at[j, i], rc.at[j, i],
            device_id=at(z, y, other, ys), device_id_type=MESH)

    def y_copy(j, i):
        return pltpu.make_async_remote_copy(
            s1.at[j, i], bufy.at[j, i], sy.at[j, i], ry.at[j, i],
            device_id=at(z, ymod[j], core, ys), device_id_type=MESH)

    def z_copy(i):
        return pltpu.make_async_remote_copy(
            s2.at[i], bufz.at[i], sz.at[i], rz.at[i],
            device_id=at(zmod[i], y, core, ys), device_id_type=MESH)

    started = []

    def go(copy):
        copy.start()
        started.append(copy)

    for j in yorder:
        for i in zorder:
            go(core_copy(j, i))
    for j in yorder:
        for i in zorder:
            core_copy(j, i).wait_recv()
            both = t_ref[zmod[i], ymod[j], core].astype(F32) + bufc[j, i].astype(F32)
            s1[j, i] = both.astype(BF16)
            if j:
                go(y_copy(j, i))
    for i in zorder:
        total = s1[0, i].astype(F32)
        for j in range(1, ys):
            y_copy(j, i).wait_recv()
            total = total + bufy[j, i].astype(F32)
        if i:
            s2[i] = total.astype(BF16)
            go(z_copy(i))
        else:
            out_ref[...] = total
    for i in range(1, zs):
        z_copy(i).wait_recv()
        out_ref[...] = out_ref[...] + bufz[i].astype(F32)
    for copy in started:
        copy.wait_send()


def scatter(n, terms):
    zs, ys = split_axis(n)
    sem = pltpu.SemaphoreType.DMA
    block = terms.shape[3:]
    vmem = pl.BlockSpec(memory_space=pltpu.VMEM)
    return pl.pallas_call(
        functools.partial(scatter_kernel, n, zs, ys),
        out_shape=jax.ShapeDtypeStruct(block, F32),
        in_specs=[vmem],
        out_specs=vmem,
        scratch_shapes=[
            pltpu.VMEM((ys, zs) + block, BF16),
            pltpu.VMEM((zs,) + block, BF16),
            pltpu.VMEM((ys, zs) + block, BF16),
            pltpu.VMEM((ys, zs) + block, BF16),
            pltpu.VMEM((zs,) + block, BF16),
            sem((ys, zs)), sem((ys, zs)), sem((ys, zs)), sem((ys, zs)), sem((zs,)), sem((zs,)),
        ],
        compiler_params=pltpu.CompilerParams(
            collective_id=2, has_side_effects=True, vmem_limit_bytes=48 << 20),
        name="scatter_terms",
    )(terms)


def row_of(count, height):
    return lax.rem(lax.broadcasted_iota(jnp.int32, (count, LANES), 0), height)


def column_of(count, height, first):
    return lax.broadcasted_iota(jnp.int32, (count, LANES), 0) // height + first


def from_above(v, d, height):
    return jnp.where(row_of(v.shape[0], height) >= d, pltpu.roll(v, d, 0), 0.0)


def from_below(v, d, height):
    count = v.shape[0]
    return jnp.where(row_of(count, height) < height - d, pltpu.roll(v, count - d, 0), 0.0)


def spread_rows(ref, v, d, height):
    ref[:, 0:LANES] = from_above(v, d, height).astype(BF16)
    ref[:, LANES : 2 * LANES] = v.astype(BF16)
    ref[:, 2 * LANES : 3 * LANES] = from_below(v, d, height).astype(BF16)


def sigmoid(v):
    return 1.0 / (1.0 + jnp.exp(-v))


def silu_slope(pre):
    sigma = sigmoid(pre)
    return sigma * (1.0 + pre * (1.0 - sigma))


def conv(ref, w_ref, start, step, count):
    total = None
    for kx in range(3):
        term = lax.dot_general(
            ref[pl.ds(start + kx * step, count), :],
            w_ref[:, kx * 3 * LANES : (kx + 1) * 3 * LANES],
            (((1,), (1,)), ((), ())),
            preferred_element_type=F32,
        )
        total = term if total is None else total + term
    return total


def gather_rows(prod, d, height, kx):
    base = kx * 3 * LANES
    up = from_below(prod[:, base : base + LANES], d, height)
    same = prod[:, base + LANES : base + 2 * LANES]
    down = from_above(prod[:, base + 2 * LANES : base + 3 * LANES], d, height)
    return up + same + down


def weight_grad(out_ref, slope_f32, ref, start, step):
    count = slope_f32.shape[0]
    turned = slope_f32.T.astype(BF16)
    for kx in range(3):
        out_ref[:, kx * 3 * LANES : (kx + 1) * 3 * LANES] = jnp.dot(
            turned, ref[pl.ds(start + kx * step, count), :], preferred_element_type=F32
        ).astype(BF16)


def step_kernel(
    n, height, breadth,
    x_ref, xh_ref, t_ref, w1_ref, w2_ref, w3_ref, g1_ref, g2_ref, g3_ref,
    x3x, x3f, x3s, pre1, pre2, acc, send, recv, ssem, rsem,
):
    me = lax.axis_index("cols")
    left, right = lax.rem(me + n - 1, n), lax.rem(me + 1, n)
    greet([{"cols": left}, {"cols": right}])
    h, b = height, breadth
    first_col = me * b
    width = n * b

    def inside(v, first):
        cols = column_of(v.shape[0], h, first_col + first)
        return jnp.where((cols >= 0) & (cols < width), v, 0.0)

    wide_x = jnp.concatenate([xh_ref[0], x_ref[...], xh_ref[1]], axis=0).astype(F32)
    spread_rows(x3x, inside(wide_x, -14), 2, h)
    v = conv(x3x, w1_ref, 0, 2 * h, (b + 24) * h)
    pre1[...] = v
    act = inside(v * sigmoid(v), -12).astype(BF16).astype(F32)
    spread_rows(x3f, act, 4, h)
    v = conv(x3f, w2_ref, 0, 4 * h, (b + 16) * h)
    pre2[...] = v
    act = inside(v * sigmoid(v), -8).astype(BF16).astype(F32)
    spread_rows(x3s, act, 8, h)
    student = conv(x3s, w3_ref, 0, 8 * h, b * h)
    s_norm = jnp.sqrt(jnp.sum(student * student, -1, keepdims=True) + epsilon)
    target = t_ref[...].astype(F32)
    t_norm = jnp.sqrt(jnp.sum(target * target, -1, keepdims=True) + epsilon)
    s_unit = student / s_norm
    differ = s_unit - target / t_norm
    slope = (differ - s_unit * jnp.sum(s_unit * differ, -1, keepdims=True)) / s_norm
    slope_b = slope.astype(BF16)

    prod = jnp.dot(slope_b, w3_ref[...], preferred_element_type=F32)
    u0 = gather_rows(prod, 8, h, 0)
    u1 = gather_rows(prod, 8, h, 1)
    u2 = gather_rows(prod, 8, h, 2)
    e = 8 * h
    m = b * h
    acc[pl.ds(0, m), :] = u0
    acc[pl.ds(m, 2 * e), :] = jnp.zeros((2 * e, LANES), F32)
    acc[pl.ds(e, m), :] += u1
    acc[pl.ds(2 * e, m), :] += u2
    part = 12 * h
    send[0] = acc[pl.ds(m + 2 * e - part, part), :].astype(BF16)
    send[1] = acc[pl.ds(0, part), :].astype(BF16)
    copies = []
    for side, target_id in ((0, right), (1, left)):
        copy = pltpu.make_async_remote_copy(
            send.at[side], recv.at[side], ssem.at[side], rsem.at[side],
            device_id={"cols": target_id}, device_id_type=MESH)
        copy.start()
        copies.append(copy)
    weight_grad(g3_ref, slope, x3s, 0, 8 * h)
    for copy in copies:
        copy.wait()
    inner = (b + 8) * h
    split = inner - part
    from_left = jnp.where(me > 0, recv[0].astype(F32), 0.0)
    from_right = jnp.where(me < n - 1, recv[1].astype(F32), 0.0)
    acc[pl.ds(4 * h, part), :] += from_left
    acc[pl.ds(4 * h + split, part), :] += from_right
    back = acc[pl.ds(4 * h, inner), :]
    slope2 = inside(back * silu_slope(pre2[pl.ds(4 * h, inner), :]), -4).astype(BF16)
    prod = jnp.dot(slope2, w2_ref[...], preferred_element_type=F32)
    back = (
        gather_rows(prod, 4, h, 0)[8 * h : 8 * h + m]
        + gather_rows(prod, 4, h, 1)[4 * h : 4 * h + m]
        + gather_rows(prod, 4, h, 2)[0:m]
    )
    weight_grad(g2_ref, slope2.astype(F32)[4 * h : 4 * h + m], x3f, 8 * h, 4 * h)
    slope1 = back * silu_slope(pre1[pl.ds(12 * h, m), :])
    weight_grad(g1_ref, slope1, x3x, 12 * h, 2 * h)


def local_step(n, height, breadth, x_cells, x_edges, teacher, w1, w2, w3):
    sem = pltpu.SemaphoreType.DMA
    vmem = pl.BlockSpec(memory_space=pltpu.VMEM)
    h, b = height, breadth
    return pl.pallas_call(
        functools.partial(step_kernel, n, h, b),
        out_shape=tuple(jax.ShapeDtypeStruct(w.shape, BF16) for w in (w1, w2, w3)),
        in_specs=[vmem] * 6,
        out_specs=(vmem,) * 3,
        scratch_shapes=[
            pltpu.VMEM(((b + 28) * h, 3 * LANES), BF16),
            pltpu.VMEM(((b + 24) * h, 3 * LANES), BF16),
            pltpu.VMEM(((b + 16) * h, 3 * LANES), BF16),
            pltpu.VMEM(((b + 24) * h, LANES), F32),
            pltpu.VMEM(((b + 16) * h, LANES), F32),
            pltpu.VMEM(((b + 16) * h, LANES), F32),
            pltpu.VMEM((2, 12 * h, LANES), BF16),
            pltpu.VMEM((2, 12 * h, LANES), BF16),
            sem((2,)), sem((2,)),
        ],
        compiler_params=pltpu.CompilerParams(
            collective_id=1, has_side_effects=True, vmem_limit_bytes=56 << 20),
        name="student_step",
    )(x_cells, x_edges, teacher, w1, w2, w3)


def taps_by_column(w):
    rows, depth = w.shape[0], w.shape[1] // 9
    w = w.reshape(rows, 3, 3, depth).transpose(0, 2, 1, 3)
    w = jnp.pad(w, ((0, 0), (0, 0), (0, 0), (0, LANES - depth)))
    return w.reshape(rows, 9 * LANES)


def taps_by_row(g, depth):
    rows = g.shape[0]
    g = g.reshape(rows, 3, 3, LANES)[..., :depth].transpose(0, 2, 1, 3)
    return g.reshape(rows, 9 * depth)


class Line:
    def __init__(self, pos, zs, ys, src, out, first, rows, sems):
        self.pos, self.zs, self.ys = pos, zs, ys
        self.rows = pl.ds(first, rows)
        self.src, self.out = src.at[self.rows], out
        self.szr, self.rzr, self.szl, self.rzl, self.sy, self.ry, self.sc, self.rc = sems

    def copy(self, src, dst, ssem, rsem, device):
        return pltpu.make_async_remote_copy(
            src, dst, ssem, rsem, device_id=device, device_id_type=MESH)

    def block(self, zi, yi, c):
        return self.out.at[zi, yi, c, self.rows]

    def hop(self, way, s):
        z, y, core = self.pos
        zi = z - way * s
        src = self.src if s == 0 else self.block(zi, y, core)
        ss, rs = (self.szr, self.rzr) if way > 0 else (self.szl, self.rzl)
        ok = (zi >= 0) & (zi < self.zs) & (z + way >= 0) & (z + way < self.zs)
        return ok, self.copy(
            src, self.block(zi, y, core), ss.at[s], rs.at[s + 1], at(z + way, y, core, self.ys))

    def arrived(self, way, s):
        z, y, core = self.pos
        zi = z - way * s
        ss, rs = (self.szr, self.rzr) if way > 0 else (self.szl, self.rzl)
        ok = (zi >= 0) & (zi < self.zs)
        return ok, zi, self.copy(
            self.src, self.block(zi, y, core), ss.at[0], rs.at[s], at(z, y, 1 - core, self.ys))

    def to_y(self, j, zi, own):
        z, y, core = self.pos
        src = self.src if own else self.block(zi, y, core)
        return self.copy(src, self.block(zi, y, core), self.sy.at[j, zi], self.ry.at[j, zi],
                         at(z, lax.rem(y + j, self.ys), core, self.ys))

    def from_y(self, j, zi):
        z, y, core = self.pos
        yi = lax.rem(y + self.ys - j, self.ys)
        return self.copy(self.src, self.block(zi, yi, core), self.sy.at[j, zi], self.ry.at[j, zi],
                         at(z, lax.rem(y + j, self.ys), core, self.ys))

    def to_core(self, j, zi, own):
        z, y, core = self.pos
        yi = lax.rem(y + self.ys - j, self.ys)
        src = self.src if own else self.block(zi, yi, core)
        return self.copy(src, self.block(zi, yi, core), self.sc.at[j, zi], self.rc.at[j, zi],
                         at(z, y, 1 - core, self.ys))

    def from_core(self, j, zi):
        z, y, core = self.pos
        yi = lax.rem(y + self.ys - j, self.ys)
        return self.copy(self.src, self.block(zi, yi, 1 - core), self.sc.at[j, zi],
                         self.rc.at[j, zi], at(z, y, 1 - core, self.ys))

    def start(self):
        z, y, core = self.pos
        for way in (1, -1):
            ok, copy = self.hop(way, 0)
            pl.when(ok)(copy.start)
        for j in range(1, self.ys):
            self.to_y(j, z, True).start()
        self.to_core(0, z, True).start()
        self.out[z, y, core, self.rows] = self.src[...]

    def forward_z(self, s):
        for way in (1, -1):
            ok, zi, here = self.arrived(way, s)

            @pl.when(ok)
            def _():
                here.wait_recv()
                for j in range(1, self.ys):
                    self.to_y(j, zi, False).start()

            if s < self.zs - 1:
                more, on = self.hop(way, s)
                pl.when(more)(on.start)

            @pl.when(ok)
            def _():
                self.to_core(0, zi, False).start()

    def forward_y(self, s):
        z = self.pos[0]
        todo = [(None, z)] if s == 0 else [
            ((z - way * s >= 0) & (z - way * s < self.zs), z - way * s) for way in (1, -1)]
        for ok, zi in todo:

            def step(zi=zi):
                for j in range(1, self.ys):
                    self.from_y(j, zi).wait_recv()
                    self.to_core(j, zi, False).start()

            step() if ok is None else pl.when(ok)(step)

    def finish(self):
        for zi in range(self.zs):
            for j in range(self.ys):
                self.from_core(j, zi).wait_recv()

    def drain(self):
        for s in range(self.zs - 1):
            for way in (1, -1):
                ok, copy = self.hop(way, s)
                pl.when(ok)(copy.wait_send)
        for zi in range(self.zs):
            for j in range(self.ys):
                if j:
                    self.to_y(j, zi, False).wait_send()
                self.to_core(j, zi, False).wait_send()


def flip(v, i):
    bit = 1
    while bit <= i:
        if i & bit:
            v = v + bit - 2 * bit * lax.rem(v // bit, 2)
        bit *= 2
    return v


class Star:
    def __init__(self, pos, zs, ys, src, out, sems):
        self.pos, self.zs, self.ys, self.src, self.out = pos, zs, ys, src, out
        self.sz, self.rz, self.sy, self.ry, self.sc, self.rc = sems

    def copy(self, src, dst, ssem, rsem, device):
        return pltpu.make_async_remote_copy(
            src, dst, ssem, rsem, device_id=device, device_id_type=MESH)

    def block(self, i, j, k):
        z, y, core = self.pos
        return self.out.at[flip(z, i), flip(y, j), flip(core, k)]

    def held(self, i, j):
        return self.src if i == 0 and j == 0 else self.block(i, j, 0)

    def z_copy(self, i, arriving):
        z, y, core = self.pos
        return self.copy(self.src, self.block(i if arriving else 0, 0, 0), self.sz.at[i],
                         self.rz.at[i], at(flip(z, i), y, core, self.ys))

    def y_copy(self, j, i, arriving):
        z, y, core = self.pos
        return self.copy(self.held(i, 0), self.block(i, j if arriving else 0, 0), self.sy.at[j, i],
                         self.ry.at[j, i], at(z, flip(y, j), core, self.ys))

    def core_copy(self, j, i, arriving):
        z, y, core = self.pos
        return self.copy(self.held(i, j), self.block(i, j, 1 if arriving else 0), self.sc.at[j, i],
                         self.rc.at[j, i], at(z, y, 1 - core, self.ys))

    def start(self):
        for i in reversed(range(1, self.zs)):
            self.z_copy(i, False).start()
        for j in range(1, self.ys):
            self.y_copy(j, 0, False).start()
        self.core_copy(0, 0, False).start()
        z, y, core = self.pos
        self.out[z, y, core] = self.src[...]

    def forward_z(self, i):
        self.z_copy(i, True).wait_recv()
        for j in range(1, self.ys):
            self.y_copy(j, i, False).start()
        self.core_copy(0, i, False).start()

    def forward_y(self, i):
        for j in range(1, self.ys):
            self.y_copy(j, i, True).wait_recv()
            self.core_copy(j, i, False).start()

    def finish(self):
        for i in range(self.zs):
            for j in range(self.ys):
                self.core_copy(j, i, True).wait_recv()

    def drain(self):
        for i in range(self.zs):
            if i:
                self.z_copy(i, False).wait_send()
            for j in range(self.ys):
                if j:
                    self.y_copy(j, i, False).wait_send()
                self.core_copy(j, i, False).wait_send()


class Sum:
    def __init__(self, pos, zs, ys, terms, bufs, sems):
        self.pos, self.zs, self.ys, self.terms = pos, zs, ys, terms
        self.s1, self.s2, self.bufc, self.bufy, self.bufz = bufs
        self.sc, self.rc, self.sy, self.ry, self.sz, self.rz = sems
        self.zorder = list(range(1, zs)) + [0]
        self.yorder = list(range(1, ys)) + [0]

    def zi(self, i):
        return lax.rem(self.pos[0] + i, self.zs)

    def yi(self, j):
        return lax.rem(self.pos[1] + j, self.ys)

    def copy(self, src, dst, ssem, rsem, device):
        return pltpu.make_async_remote_copy(
            src, dst, ssem, rsem, device_id=device, device_id_type=MESH)

    def core_copy(self, j, i):
        z, y, core = self.pos
        return self.copy(self.terms.at[self.zi(i), self.yi(j), 1 - core], self.bufc.at[j, i],
                         self.sc.at[j, i], self.rc.at[j, i], at(z, y, 1 - core, self.ys))

    def y_copy(self, j, i):
        z, y, core = self.pos
        return self.copy(self.s1.at[j, i], self.bufy.at[j, i], self.sy.at[j, i],
                         self.ry.at[j, i], at(z, self.yi(j), core, self.ys))

    def z_copy(self, i):
        z, y, core = self.pos
        return self.copy(self.s2.at[i], self.bufz.at[i], self.sz.at[i], self.rz.at[i],
                         at(self.zi(i), y, core, self.ys))

    def start(self):
        for j in self.yorder:
            for i in self.zorder:
                self.core_copy(j, i).start()

    def pair(self):
        core = self.pos[2]
        for j in self.yorder:
            for i in self.zorder:
                self.core_copy(j, i).wait_recv()
                both = self.terms[self.zi(i), self.yi(j), core].astype(F32)
                self.s1[j, i] = (both + self.bufc[j, i].astype(F32)).astype(BF16)
                if j:
                    self.y_copy(j, i).start()

    def along_y(self, begin, end):
        for i in self.zorder[begin:end]:
            total = self.s1[0, i].astype(F32)
            for j in range(1, self.ys):
                self.y_copy(j, i).wait_recv()
                total = total + self.bufy[j, i].astype(F32)
            if i:
                self.s2[i] = total.astype(BF16)
                self.z_copy(i).start()
            else:
                self.own = total

    def along_z(self):
        total = self.own
        for i in range(1, self.zs):
            self.z_copy(i).wait_recv()
            total = total + self.bufz[i].astype(F32)
        return total

    def drain(self):
        for j in self.yorder:
            for i in self.zorder:
                self.core_copy(j, i).wait_send()
                if j:
                    self.y_copy(j, i).wait_send()
        for i in range(1, self.zs):
            self.z_copy(i).wait_send()


def tap(t):
    return slice(t * LANES, (t + 1) * LANES)


def conv_taps(ref, w, start, step, count):
    total = None
    for kx in range(3):
        rhs = jnp.concatenate([w[:, tap(3 * ky + kx)] for ky in range(3)], axis=1)
        term = lax.dot_general(ref[pl.ds(start + kx * step, count), :], rhs,
                               (((1,), (1,)), ((), ())), preferred_element_type=F32)
        total = term if total is None else total + term
    return total


def join_rows(prod, d, height, kx):
    up = from_below(prod[:, tap(kx)], d, height)
    down = from_above(prod[:, tap(6 + kx)], d, height)
    return up + prod[:, tap(3 + kx)] + down


def put_terms(ref, place, value):
    zs, ys = ref.shape[0], ref.shape[1]
    (first, count), t = place
    ref[:, :, :, first : first + count, tap(t)] = value.reshape(zs, ys, 2, count, LANES).astype(BF16)


def grad_taps(ref, places, slope_f32, acts, start, step):
    count = slope_f32.shape[0]
    turned = slope_f32.T.astype(BF16)
    for kx in range(3):
        prod = jnp.dot(turned, acts[pl.ds(start + kx * step, count), :],
                       preferred_element_type=F32)
        for ky in range(3):
            put_terms(ref, places[3 * ky + kx], prod[:, tap(ky)])


def fused_kernel(
    n, zs, ys, height, breadth, rl, rm, rf,
    x_ref, t_ref, wl_ref, wm_ref, wf_ref, o1_ref, o2_ref, o3_ref,
    xv, tv, wlv, wmv, wfv,
    pa, ga, gb, ta, tb, xh, xs, x9, x3f, x3s, pre1, pre2, acc, send, recv, tf, tn,
    a1, a2, a3, a4, a5, b1, b2, b3, b4, b5, lsem, sx, rx, ssem, rsem, *sems,
):
    me, z, y, core = place(n, zs, ys)
    pos = (z, y, core)
    h, b = height, breadth
    depth = wf_ref.shape[1] // 9
    left, right = lax.rem(me + n - 1, n), lax.rem(me + 1, n)
    loads = [pltpu.make_async_copy(src, dst, lsem.at[i]) for i, (src, dst) in enumerate(
        ((wm_ref, wmv), (wf_ref, wfv), (x_ref, xv), (wl_ref, wlv), (t_ref, tv)))]
    for load in loads:
        load.start()
    peers = (
        [at(flip(z, i), y, core, ys) for i in range(1, zs)]
        + [at(z, flip(y, j), core, ys) for j in range(1, ys)]
        + [at(z, y, 1 - core, ys), {"cols": left}, {"cols": right}]
    )
    call(peers)
    middle = [((0, rm), t) if t < 7 else ((rm, rf), t - 7) for t in range(9)]
    first = [((rm, rf), t + 2) for t in range(5)]
    low = Star(pos, zs, ys, pa, ga, sems[0:6])
    cut = rl // 16 * 8
    parts = ((0, cut), (cut, rl - cut)) if cut else ((0, rl),)
    high = [Line(pos, zs, ys, wlv, gb, begin, rows, sems[8 * i + 6 : 8 * i + 14])
            for i, (begin, rows) in enumerate(parts)]
    sum_a = Sum(pos, zs, ys, ta, (a1, a2, a3, a4, a5), sems[22:28])
    sum_b = Sum(pos, zs, ys, tb, (b1, b2, b3, b4, b5), sems[28:34])
    loads[0].wait()
    loads[1].wait()
    pa[0:rm, :] = wmv[:, 0 : 7 * LANES]
    pa[rm : rm + rf, 0 : 2 * LANES] = wmv[:, 7 * LANES : 9 * LANES]
    pa[rm : rm + rf, 6 * LANES : 7 * LANES] = jnp.zeros((rf, LANES), BF16)
    pa[rm : rm + rf, 2 * LANES : 2 * LANES + 9 * depth] = wfv[...]
    hear(peers)
    low.start()
    loads[2].wait()
    edge = 14 * depth
    halo = []
    for side, peer, begin in ((0, right, b * depth - edge), (1, left, 0)):
        copy = pltpu.make_async_remote_copy(
            xv.at[:, pl.ds(begin, edge)], xh.at[side], sx.at[side], rx.at[side],
            device_id={"cols": peer}, device_id_type=MESH)
        copy.start()
        halo.append(copy)
    loads[3].wait()
    for line in high:
        line.start()

    loads[4].wait()
    target = tv[...].astype(F32)
    t_norm = jnp.sqrt(jnp.sum(target * target, -1, keepdims=True) + epsilon)
    target = target / t_norm
    for q in range(tf.shape[0]):
        tf[q] = target[:, tap(q)]
    for i in reversed(range(1, zs)):
        low.forward_z(i)
    for c in range(b):
        for q in range(tf.shape[0]):
            tn[pl.ds(c * h, h), tap(q)] = tf[q, pl.ds(c, h, stride=b), :]
    for line in high:
        line.forward_z(1)

    first_col = me * b
    width = n * b

    def inside(v, first):
        cols = column_of(v.shape[0], h, first_col + first)
        return jnp.where((cols >= 0) & (cols < width), v, 0.0)

    for copy in halo:
        copy.wait()
    half = lax.broadcasted_iota(jnp.int32, (h, LANES), 1) < depth
    at_col = 0
    for part, pairs in ((xh[0], 7), (xv[...], b // 2), (xh[1], 7)):
        part = part.astype(F32)
        for q in range(pairs):
            both = part[:, tap(q)]
            turned = pltpu.roll(both, depth, 1)
            xs[pl.ds(at_col * h, h), :] = jnp.where(half, both, turned)
            xs[pl.ds((at_col + 1) * h, h), :] = jnp.where(half, turned, both)
            at_col += 2
    for i in [0] + list(reversed(range(1, zs))):
        low.forward_y(i)
    for line in high:
        line.forward_z(2)
    wide_x = inside(xs[...], -14)
    count1 = (b + 24) * h
    rows3 = (from_above(wide_x, 2, h), wide_x, from_below(wide_x, 2, h))

    def piece(t):
        ky, kx = t // 3, t % 3
        return rows3[ky][kx * 2 * h : kx * 2 * h + count1]

    lower = lax.broadcasted_iota(jnp.int32, (count1, LANES), 1) < depth
    for q in range(5):
        odd = piece(2 * q + 1) if q < 4 else 0.0
        x9[:, tap(q)] = jnp.where(lower, piece(2 * q), odd).astype(BF16)
    for s in range(3, zs):
        for line in high:
            line.forward_z(s)
    low.finish()
    w1 = ga[:, :, :, rm : rm + rf, 2 * LANES : 7 * LANES].reshape(n * rf, 5 * LANES)
    v = lax.dot_general(x9[...], w1, (((1,), (1,)), ((), ())), preferred_element_type=F32)
    pre1[...] = v
    act = inside(v * sigmoid(v), -12).astype(BF16).astype(F32)
    spread_rows(x3f, act, 4, h)
    for line in high:
        for s in range(zs - 1):
            line.forward_y(s)
    w2 = jnp.concatenate([
        ga[:, :, :, 0:rm, :].reshape(n * rm, 7 * LANES),
        ga[:, :, :, rm : rm + rf, 0 : 2 * LANES].reshape(n * rm, 2 * LANES)], axis=1)
    v = conv_taps(x3f, w2, 0, 4 * h, (b + 16) * h)
    pre2[...] = v
    act = inside(v * sigmoid(v), -8).astype(BF16).astype(F32)
    spread_rows(x3s, act, 8, h)
    for line in high:
        line.forward_y(zs - 1)
    for line in high:
        line.finish()
    w3 = gb[...].reshape(n * rl, 9 * LANES)
    student = conv_taps(x3s, w3, 0, 8 * h, b * h)
    s_norm = jnp.sqrt(jnp.sum(student * student, -1, keepdims=True) + epsilon)
    s_unit = student / s_norm
    differ = s_unit - tn[...]
    slope = (differ - s_unit * jnp.sum(s_unit * differ, -1, keepdims=True)) / s_norm

    prod = jnp.dot(slope.astype(BF16), w3, preferred_element_type=F32)
    e = 8 * h
    m = b * h
    acc[pl.ds(0, m), :] = join_rows(prod, 8, h, 0)
    acc[pl.ds(m, 2 * e), :] = jnp.zeros((2 * e, LANES), F32)
    acc[pl.ds(e, m), :] += join_rows(prod, 8, h, 1)
    acc[pl.ds(2 * e, m), :] += join_rows(prod, 8, h, 2)
    part = 12 * h
    send[0] = acc[pl.ds(m + 2 * e - part, part), :].astype(BF16)
    send[1] = acc[pl.ds(0, part), :].astype(BF16)
    copies = []
    for side, peer in ((0, right), (1, left)):
        copy = pltpu.make_async_remote_copy(
            send.at[side], recv.at[side], ssem.at[side], rsem.at[side],
            device_id={"cols": peer}, device_id_type=MESH)
        copy.start()
        copies.append(copy)
    grad_taps(tb, [((0, rl), t) for t in range(9)], slope, x3s, 0, 8 * h)
    sum_b.start()
    sum_b.pair()
    for copy in copies:
        copy.wait()
    inner = (b + 8) * h
    split = inner - part
    from_left = jnp.where(me > 0, recv[0].astype(F32), 0.0)
    from_right = jnp.where(me < n - 1, recv[1].astype(F32), 0.0)
    acc[pl.ds(4 * h, part), :] += from_left
    acc[pl.ds(4 * h + split, part), :] += from_right
    back = acc[pl.ds(4 * h, inner), :]
    slope2 = inside(back * silu_slope(pre2[pl.ds(4 * h, inner), :]), -4).astype(BF16)
    prod = jnp.dot(slope2, w2, preferred_element_type=F32)
    back = (
        join_rows(prod, 4, h, 0)[8 * h : 8 * h + m]
        + join_rows(prod, 4, h, 1)[4 * h : 4 * h + m]
        + join_rows(prod, 4, h, 2)[0:m]
    )
    grad_taps(ta, middle, slope2.astype(F32)[4 * h : 4 * h + m], x3f, 8 * h, 4 * h)
    slope1 = back * silu_slope(pre1[pl.ds(12 * h, m), :])
    prod = jnp.dot(slope1.T.astype(BF16), x9[pl.ds(12 * h, m), :], preferred_element_type=F32)
    for q in range(5):
        put_terms(ta, first[q], prod[:, tap(q)])
    sum_a.start()
    sum_b.along_y(0, 1)
    sum_a.pair()
    sum_b.along_y(1, zs)
    sum_a.along_y(0, zs)
    o3_ref[...] = sum_b.along_z()
    total = sum_a.along_z()
    o2_ref[:, 0 : 7 * LANES] = total[0:rm]
    o2_ref[:, 7 * LANES : 9 * LANES] = total[rm : rm + rf, 0 : 2 * LANES]
    o1_ref[...] = total[rm : rm + rf, 2 * LANES : 2 * LANES + 9 * depth]
    for each in (low, *high, sum_a, sum_b):
        each.drain()


def hand_over_kernel(a_ref, b_ref, c_ref, x_ref, y_ref, z_ref):
    x_ref[...] = a_ref[...]
    y_ref[...] = b_ref[...]
    z_ref[...] = c_ref[...]


def hand_over(arrays):
    vmem = pl.BlockSpec(memory_space=pltpu.VMEM)
    return pl.pallas_call(
        hand_over_kernel,
        out_shape=tuple(jax.ShapeDtypeStruct(a.shape, a.dtype) for a in arrays),
        in_specs=[vmem] * 3,
        out_specs=(vmem,) * 3,
        name="hand_over",
    )(*(pltpu.with_memory_space_constraint(a, pltpu.VMEM) for a in arrays))


def fused(n, height, breadth, x, t, wl, wm, wf):
    zs, ys = split_axis(n)
    sem = pltpu.SemaphoreType.DMA
    vmem = pl.BlockSpec(memory_space=pltpu.VMEM)
    h, b = height, breadth
    rl, rm, rf = wl.shape[0], wm.shape[0], wf.shape[0]
    wide = wl.shape[1]
    low, high = (rm + rf, 7 * LANES), (rl, wide)
    channels = t.shape[1]

    def sum_bufs(block):
        return [
            pltpu.VMEM((ys, zs) + block, BF16), pltpu.VMEM((zs,) + block, BF16),
            pltpu.VMEM((ys, zs) + block, BF16), pltpu.VMEM((ys, zs) + block, BF16),
            pltpu.VMEM((zs,) + block, BF16),
        ]

    star_sems = [sem((zs,))] * 2 + [sem((ys, zs))] * 4
    line_sems = [sem((zs,))] * 4 + [sem((ys, zs))] * 4
    sum_sems = [sem((ys, zs))] * 4 + [sem((zs,))] * 2
    return pl.pallas_call(
        functools.partial(fused_kernel, n, zs, ys, h, b, rl, rm, rf),
        out_shape=tuple(pltpu.VMEM(w.shape, F32) for w in (wf, wm, wl)),
        in_specs=[pl.BlockSpec(memory_space=pltpu.HBM)] * 5,
        out_specs=(vmem,) * 3,
        scratch_shapes=[pltpu.VMEM(w.shape, BF16) for w in (x, t, wl, wm, wf)] + [
            pltpu.VMEM(low, BF16),
            pltpu.VMEM((zs, ys, 2) + low, BF16),
            pltpu.VMEM((zs, ys, 2) + high, BF16),
            pltpu.VMEM((zs, ys, 2) + low, BF16),
            pltpu.VMEM((zs, ys, 2) + high, BF16),
            pltpu.VMEM((2, h, 14 * wf.shape[1] // 9), BF16),
            pltpu.VMEM(((b + 28) * h, LANES), F32),
            pltpu.VMEM(((b + 24) * h, 5 * LANES), BF16),
            pltpu.VMEM(((b + 24) * h, 3 * LANES), BF16),
            pltpu.VMEM(((b + 16) * h, 3 * LANES), BF16),
            pltpu.VMEM(((b + 24) * h, LANES), F32),
            pltpu.VMEM(((b + 16) * h, LANES), F32),
            pltpu.VMEM(((b + 16) * h, LANES), F32),
            pltpu.VMEM((2, 12 * h, LANES), BF16),
            pltpu.VMEM((2, 12 * h, LANES), BF16),
            pltpu.VMEM((channels // LANES, b * h, LANES), F32),
            pltpu.VMEM((b * h, channels), F32),
        ]
        + sum_bufs(low) + sum_bufs(high)
        + [sem((5,))] + [sem((2,))] * 4 + star_sems + line_sems * 2 + sum_sems * 2,
        compiler_params=pltpu.CompilerParams(
            collective_id=3, has_side_effects=True, vmem_limit_bytes=56 << 20),
        name="fused_step",
    )(x, t, wl, wm, wf)


def on_device(n, image_feats, teacher, w_first, w_middle, w_last):
    height, breadth, channels = teacher.shape
    in_depth = w_first.shape[1] // 9
    rl, rm, rf = w_last.shape[0], w_middle.shape[0], w_first.shape[0]
    if (split_axis(n)[0] > 2 and n & (n - 1) == 0 and rm == rf and all(r % 8 == 0 for r in (rl, rm, rf))
            and breadth % 8 == 0 and 2 * in_depth == LANES):
        return hand_over(fused(n, height, breadth, image_feats,
                               teacher.reshape(height * breadth, channels), w_last, w_middle, w_first))
    packed = jnp.concatenate([taps_by_column(w) for w in (w_last, w_middle, w_first)], axis=0)
    x = image_feats.reshape(height, breadth, in_depth).transpose(1, 0, 2)
    x = jnp.pad(x, ((0, 0), (0, 0), (0, LANES - in_depth)))
    x_cells = x.reshape(breadth * height, LANES)
    t_cells = teacher.transpose(1, 0, 2).reshape(breadth * height, channels)
    gathered, x_edges = gather(n, packed, x_cells, 14 * height)
    g = gathered.reshape((n,) + packed.shape)
    w3 = g[:, :rl].reshape(n * rl, -1)
    w2 = g[:, rl : rl + rm].reshape(n * rm, -1)
    w1 = g[:, rl + rm :].reshape(n * rf, -1)
    g1, g2, g3 = local_step(n, height, breadth, x_cells, x_edges, t_cells, w1, w2, w3)
    terms = jnp.concatenate(
        [g3.reshape(n, rl, -1), g2.reshape(n, rm, -1), g1.reshape(n, rf, -1)], axis=1)
    out = scatter(n, terms.reshape(gathered.shape))
    return (
        taps_by_row(out[rl + rm :], in_depth),
        taps_by_row(out[rl : rl + rm], LANES),
        taps_by_row(out[:rl], LANES),
    )


def solution(mesh):
    placed = (
        P("groups", "cols"),
        P("groups", "cols", None),
        P("cols", None),
        P("cols", None),
        P("cols", None),
    )
    return jax.shard_map(
        functools.partial(on_device, mesh.shape["cols"]),
        mesh=mesh,
        in_specs=placed,
        out_specs=(P(("groups", "cols"), None),) * 3,
        check_vma=False,
    )
```

```python
import functools

import jax
import jax.numpy as jnp
from jax import lax
from jax.experimental import pallas as pl
from jax.experimental.pallas import tpu as pltpu
from jax.sharding import PartitionSpec as P

epsilon = 1e-06
MESH = pl.DeviceIdType.MESH
LANES = 128
F32 = jnp.float32
BF16 = jnp.bfloat16


def split_axis(n):
    half = n // 2
    y = 1
    while 4 * y * y <= half:
        y *= 2
    return half // y, y


def place(n, z_size, y_size):
    me = lax.axis_index("cols")
    core = lax.rem(me, 2)
    y = lax.rem(me // 2, y_size)
    z = me // (2 * y_size)
    return me, z, y, core


def at(z, y, core, y_size):
    return {"cols": (z * y_size + y) * 2 + core}


def call(peers):
    barrier = pltpu.get_barrier_semaphore()
    for peer in peers:
        pl.semaphore_signal(barrier, inc=1, device_id=peer, device_id_type=MESH)


def hear(peers):
    pl.semaphore_wait(pltpu.get_barrier_semaphore(), len(peers))


def greet(peers):
    call(peers)
    hear(peers)


def gather_kernel(n, zs, ys, edge, p_ref, x_ref, g_ref, xh_ref, sz, rz, sy, ry, sc, rc, sx, rx):
    me, z, y, core = place(n, zs, ys)
    other = 1 - core
    zmod = [lax.rem(z + i, zs) for i in range(zs)]
    zback = [lax.rem(z + zs - i, zs) for i in range(zs)]
    ymod = [lax.rem(y + i, ys) for i in range(ys)]
    yback = [lax.rem(y + ys - i, ys) for i in range(ys)]
    left, right = lax.rem(me + n - 1, n), lax.rem(me + 1, n)
    greet(
        [at(zmod[i], y, core, ys) for i in range(1, zs)]
        + [at(z, ymod[j], core, ys) for j in range(1, ys)]
        + [at(z, y, other, ys), {"cols": left}, {"cols": right}]
    )

    def block(zi, yi, c):
        return g_ref.at[zi, yi, c]

    def to_z(i):
        return pltpu.make_async_remote_copy(
            p_ref, block(z, y, core), sz.at[i], rz.at[i],
            device_id=at(zmod[i], y, core, ys), device_id_type=MESH)

    def from_z(i):
        return pltpu.make_async_remote_copy(
            p_ref, block(zback[i], y, core), sz.at[i], rz.at[i],
            device_id=at(zmod[i], y, core, ys), device_id_type=MESH)

    def to_y(j, i):
        src = p_ref if i == 0 else block(zback[i], y, core)
        return pltpu.make_async_remote_copy(
            src, block(zback[i], y, core), sy.at[j, i], ry.at[j, i],
            device_id=at(z, ymod[j], core, ys), device_id_type=MESH)

    def from_y(j, i):
        return pltpu.make_async_remote_copy(
            p_ref, block(zback[i], yback[j], core), sy.at[j, i], ry.at[j, i],
            device_id=at(z, ymod[j], core, ys), device_id_type=MESH)

    def to_core(j, i):
        src = p_ref if i == 0 and j == 0 else block(zback[i], yback[j], core)
        return pltpu.make_async_remote_copy(
            src, block(zback[i], yback[j], core), sc.at[j, i], rc.at[j, i],
            device_id=at(z, y, other, ys), device_id_type=MESH)

    def from_core(j, i):
        return pltpu.make_async_remote_copy(
            p_ref, block(zback[i], yback[j], other), sc.at[j, i], rc.at[j, i],
            device_id=at(z, y, other, ys), device_id_type=MESH)

    cells = x_ref.shape[0]
    to_right = pltpu.make_async_remote_copy(
        x_ref.at[pl.ds(cells - edge, edge)], xh_ref.at[0], sx.at[0], rx.at[0],
        device_id={"cols": right}, device_id_type=MESH)
    to_left = pltpu.make_async_remote_copy(
        x_ref.at[pl.ds(0, edge)], xh_ref.at[1], sx.at[1], rx.at[1],
        device_id={"cols": left}, device_id_type=MESH)
    started = []

    def go(copy):
        copy.start()
        started.append(copy)

    for i in range(1, zs):
        go(to_z(i))
    for j in range(1, ys):
        go(to_y(j, 0))
    go(to_right)
    go(to_left)
    go(to_core(0, 0))
    g_ref[z, y, core] = p_ref[...]
    for i in range(1, zs):
        from_z(i).wait_recv()
        for j in range(1, ys):
            go(to_y(j, i))
        go(to_core(0, i))
    for i in range(zs):
        for j in range(1, ys):
            from_y(j, i).wait_recv()
            go(to_core(j, i))
    to_right.wait_recv()
    to_left.wait_recv()
    for i in range(zs):
        for j in range(ys):
            from_core(j, i).wait_recv()
    for copy in started:
        copy.wait_send()


def gather(n, packed, x_cells, edge):
    zs, ys = split_axis(n)
    sem = pltpu.SemaphoreType.DMA
    vmem = pl.BlockSpec(memory_space=pltpu.VMEM)
    return pl.pallas_call(
        functools.partial(gather_kernel, n, zs, ys, edge),
        out_shape=(
            jax.ShapeDtypeStruct((zs, ys, 2) + packed.shape, BF16),
            jax.ShapeDtypeStruct((2, edge, x_cells.shape[1]), BF16),
        ),
        in_specs=[vmem, vmem],
        out_specs=(vmem, vmem),
        scratch_shapes=[
            sem((zs,)), sem((zs,)), sem((ys, zs)), sem((ys, zs)), sem((ys, zs)), sem((ys, zs)),
            sem((2,)), sem((2,)),
        ],
        compiler_params=pltpu.CompilerParams(
            collective_id=0, has_side_effects=True, vmem_limit_bytes=48 << 20),
        name="gather_weights",
    )(packed, x_cells)


def scatter_kernel(n, zs, ys, t_ref, out_ref, s1, s2, bufc, bufy, bufz, sc, rc, sy, ry, sz, rz):
    me, z, y, core = place(n, zs, ys)
    other = 1 - core
    zmod = [lax.rem(z + i, zs) for i in range(zs)]
    ymod = [lax.rem(y + i, ys) for i in range(ys)]
    greet(
        [at(zmod[i], y, core, ys) for i in range(1, zs)]
        + [at(z, ymod[j], core, ys) for j in range(1, ys)]
        + [at(z, y, other, ys)]
    )
    zorder = list(range(1, zs)) + [0]
    yorder = list(range(1, ys)) + [0]

    def core_copy(j, i):
        return pltpu.make_async_remote_copy(
            t_ref.at[zmod[i], ymod[j], other], bufc.at[j, i], sc.at[j, i], rc.at[j, i],
            device_id=at(z, y, other, ys), device_id_type=MESH)

    def y_copy(j, i):
        return pltpu.make_async_remote_copy(
            s1.at[j, i], bufy.at[j, i], sy.at[j, i], ry.at[j, i],
            device_id=at(z, ymod[j], core, ys), device_id_type=MESH)

    def z_copy(i):
        return pltpu.make_async_remote_copy(
            s2.at[i], bufz.at[i], sz.at[i], rz.at[i],
            device_id=at(zmod[i], y, core, ys), device_id_type=MESH)

    started = []

    def go(copy):
        copy.start()
        started.append(copy)

    for j in yorder:
        for i in zorder:
            go(core_copy(j, i))
    for j in yorder:
        for i in zorder:
            core_copy(j, i).wait_recv()
            both = t_ref[zmod[i], ymod[j], core].astype(F32) + bufc[j, i].astype(F32)
            s1[j, i] = both.astype(BF16)
            if j:
                go(y_copy(j, i))
    for i in zorder:
        total = s1[0, i].astype(F32)
        for j in range(1, ys):
            y_copy(j, i).wait_recv()
            total = total + bufy[j, i].astype(F32)
        if i:
            s2[i] = total.astype(BF16)
            go(z_copy(i))
        else:
            out_ref[...] = total
    for i in range(1, zs):
        z_copy(i).wait_recv()
        out_ref[...] = out_ref[...] + bufz[i].astype(F32)
    for copy in started:
        copy.wait_send()


def scatter(n, terms):
    zs, ys = split_axis(n)
    sem = pltpu.SemaphoreType.DMA
    block = terms.shape[3:]
    vmem = pl.BlockSpec(memory_space=pltpu.VMEM)
    return pl.pallas_call(
        functools.partial(scatter_kernel, n, zs, ys),
        out_shape=jax.ShapeDtypeStruct(block, F32),
        in_specs=[vmem],
        out_specs=vmem,
        scratch_shapes=[
            pltpu.VMEM((ys, zs) + block, BF16),
            pltpu.VMEM((zs,) + block, BF16),
            pltpu.VMEM((ys, zs) + block, BF16),
            pltpu.VMEM((ys, zs) + block, BF16),
            pltpu.VMEM((zs,) + block, BF16),
            sem((ys, zs)), sem((ys, zs)), sem((ys, zs)), sem((ys, zs)), sem((zs,)), sem((zs,)),
        ],
        compiler_params=pltpu.CompilerParams(
            collective_id=2, has_side_effects=True, vmem_limit_bytes=48 << 20),
        name="scatter_terms",
    )(terms)


def row_of(count, height):
    return lax.rem(lax.broadcasted_iota(jnp.int32, (count, LANES), 0), height)


def column_of(count, height, first):
    return lax.broadcasted_iota(jnp.int32, (count, LANES), 0) // height + first


def from_above(v, d, height):
    return jnp.where(row_of(v.shape[0], height) >= d, pltpu.roll(v, d, 0), 0.0)


def from_below(v, d, height):
    count = v.shape[0]
    return jnp.where(row_of(count, height) < height - d, pltpu.roll(v, count - d, 0), 0.0)


def spread_rows(ref, v, d, height):
    ref[:, 0:LANES] = from_above(v, d, height).astype(BF16)
    ref[:, LANES : 2 * LANES] = v.astype(BF16)
    ref[:, 2 * LANES : 3 * LANES] = from_below(v, d, height).astype(BF16)


def sigmoid(v):
    return 1.0 / (1.0 + jnp.exp(-v))


def silu_slope(pre):
    sigma = sigmoid(pre)
    return sigma * (1.0 + pre * (1.0 - sigma))


def conv(ref, w_ref, start, step, count):
    total = None
    for kx in range(3):
        term = lax.dot_general(
            ref[pl.ds(start + kx * step, count), :],
            w_ref[:, kx * 3 * LANES : (kx + 1) * 3 * LANES],
            (((1,), (1,)), ((), ())),
            preferred_element_type=F32,
        )
        total = term if total is None else total + term
    return total


def gather_rows(prod, d, height, kx):
    base = kx * 3 * LANES
    up = from_below(prod[:, base : base + LANES], d, height)
    same = prod[:, base + LANES : base + 2 * LANES]
    down = from_above(prod[:, base + 2 * LANES : base + 3 * LANES], d, height)
    return up + same + down


def weight_grad(out_ref, slope_f32, ref, start, step):
    count = slope_f32.shape[0]
    turned = slope_f32.T.astype(BF16)
    for kx in range(3):
        out_ref[:, kx * 3 * LANES : (kx + 1) * 3 * LANES] = jnp.dot(
            turned, ref[pl.ds(start + kx * step, count), :], preferred_element_type=F32
        ).astype(BF16)


def step_kernel(
    n, height, breadth,
    x_ref, xh_ref, t_ref, w1_ref, w2_ref, w3_ref, g1_ref, g2_ref, g3_ref,
    x3x, x3f, x3s, pre1, pre2, acc, send, recv, ssem, rsem,
):
    me = lax.axis_index("cols")
    left, right = lax.rem(me + n - 1, n), lax.rem(me + 1, n)
    greet([{"cols": left}, {"cols": right}])
    h, b = height, breadth
    first_col = me * b
    width = n * b

    def inside(v, first):
        cols = column_of(v.shape[0], h, first_col + first)
        return jnp.where((cols >= 0) & (cols < width), v, 0.0)

    wide_x = jnp.concatenate([xh_ref[0], x_ref[...], xh_ref[1]], axis=0).astype(F32)
    spread_rows(x3x, inside(wide_x, -14), 2, h)
    v = conv(x3x, w1_ref, 0, 2 * h, (b + 24) * h)
    pre1[...] = v
    act = inside(v * sigmoid(v), -12).astype(BF16).astype(F32)
    spread_rows(x3f, act, 4, h)
    v = conv(x3f, w2_ref, 0, 4 * h, (b + 16) * h)
    pre2[...] = v
    act = inside(v * sigmoid(v), -8).astype(BF16).astype(F32)
    spread_rows(x3s, act, 8, h)
    student = conv(x3s, w3_ref, 0, 8 * h, b * h)
    s_norm = jnp.sqrt(jnp.sum(student * student, -1, keepdims=True) + epsilon)
    target = t_ref[...].astype(F32)
    t_norm = jnp.sqrt(jnp.sum(target * target, -1, keepdims=True) + epsilon)
    s_unit = student / s_norm
    differ = s_unit - target / t_norm
    slope = (differ - s_unit * jnp.sum(s_unit * differ, -1, keepdims=True)) / s_norm
    slope_b = slope.astype(BF16)

    prod = jnp.dot(slope_b, w3_ref[...], preferred_element_type=F32)
    u0 = gather_rows(prod, 8, h, 0)
    u1 = gather_rows(prod, 8, h, 1)
    u2 = gather_rows(prod, 8, h, 2)
    e = 8 * h
    m = b * h
    acc[pl.ds(0, m), :] = u0
    acc[pl.ds(m, 2 * e), :] = jnp.zeros((2 * e, LANES), F32)
    acc[pl.ds(e, m), :] += u1
    acc[pl.ds(2 * e, m), :] += u2
    part = 12 * h
    send[0] = acc[pl.ds(m + 2 * e - part, part), :].astype(BF16)
    send[1] = acc[pl.ds(0, part), :].astype(BF16)
    copies = []
    for side, target_id in ((0, right), (1, left)):
        copy = pltpu.make_async_remote_copy(
            send.at[side], recv.at[side], ssem.at[side], rsem.at[side],
            device_id={"cols": target_id}, device_id_type=MESH)
        copy.start()
        copies.append(copy)
    weight_grad(g3_ref, slope, x3s, 0, 8 * h)
    for copy in copies:
        copy.wait()
    inner = (b + 8) * h
    split = inner - part
    from_left = jnp.where(me > 0, recv[0].astype(F32), 0.0)
    from_right = jnp.where(me < n - 1, recv[1].astype(F32), 0.0)
    acc[pl.ds(4 * h, part), :] += from_left
    acc[pl.ds(4 * h + split, part), :] += from_right
    back = acc[pl.ds(4 * h, inner), :]
    slope2 = inside(back * silu_slope(pre2[pl.ds(4 * h, inner), :]), -4).astype(BF16)
    prod = jnp.dot(slope2, w2_ref[...], preferred_element_type=F32)
    back = (
        gather_rows(prod, 4, h, 0)[8 * h : 8 * h + m]
        + gather_rows(prod, 4, h, 1)[4 * h : 4 * h + m]
        + gather_rows(prod, 4, h, 2)[0:m]
    )
    weight_grad(g2_ref, slope2.astype(F32)[4 * h : 4 * h + m], x3f, 8 * h, 4 * h)
    slope1 = back * silu_slope(pre1[pl.ds(12 * h, m), :])
    weight_grad(g1_ref, slope1, x3x, 12 * h, 2 * h)


def local_step(n, height, breadth, x_cells, x_edges, teacher, w1, w2, w3):
    sem = pltpu.SemaphoreType.DMA
    vmem = pl.BlockSpec(memory_space=pltpu.VMEM)
    h, b = height, breadth
    return pl.pallas_call(
        functools.partial(step_kernel, n, h, b),
        out_shape=tuple(jax.ShapeDtypeStruct(w.shape, BF16) for w in (w1, w2, w3)),
        in_specs=[vmem] * 6,
        out_specs=(vmem,) * 3,
        scratch_shapes=[
            pltpu.VMEM(((b + 28) * h, 3 * LANES), BF16),
            pltpu.VMEM(((b + 24) * h, 3 * LANES), BF16),
            pltpu.VMEM(((b + 16) * h, 3 * LANES), BF16),
            pltpu.VMEM(((b + 24) * h, LANES), F32),
            pltpu.VMEM(((b + 16) * h, LANES), F32),
            pltpu.VMEM(((b + 16) * h, LANES), F32),
            pltpu.VMEM((2, 12 * h, LANES), BF16),
            pltpu.VMEM((2, 12 * h, LANES), BF16),
            sem((2,)), sem((2,)),
        ],
        compiler_params=pltpu.CompilerParams(
            collective_id=1, has_side_effects=True, vmem_limit_bytes=56 << 20),
        name="student_step",
    )(x_cells, x_edges, teacher, w1, w2, w3)


def taps_by_column(w):
    rows, depth = w.shape[0], w.shape[1] // 9
    w = w.reshape(rows, 3, 3, depth).transpose(0, 2, 1, 3)
    w = jnp.pad(w, ((0, 0), (0, 0), (0, 0), (0, LANES - depth)))
    return w.reshape(rows, 9 * LANES)


def taps_by_row(g, depth):
    rows = g.shape[0]
    g = g.reshape(rows, 3, 3, LANES)[..., :depth].transpose(0, 2, 1, 3)
    return g.reshape(rows, 9 * depth)


class Line:
    def __init__(self, pos, zs, ys, src, out, first, rows, sems):
        self.pos, self.zs, self.ys = pos, zs, ys
        self.rows = pl.ds(first, rows)
        self.src, self.out = src.at[self.rows], out
        self.szr, self.rzr, self.szl, self.rzl, self.sy, self.ry, self.sc, self.rc = sems

    def copy(self, src, dst, ssem, rsem, device):
        return pltpu.make_async_remote_copy(
            src, dst, ssem, rsem, device_id=device, device_id_type=MESH)

    def block(self, zi, yi, c):
        return self.out.at[zi, yi, c, self.rows]

    def hop(self, way, s):
        z, y, core = self.pos
        zi = z - way * s
        src = self.src if s == 0 else self.block(zi, y, core)
        ss, rs = (self.szr, self.rzr) if way > 0 else (self.szl, self.rzl)
        ok = (zi >= 0) & (zi < self.zs) & (z + way >= 0) & (z + way < self.zs)
        return ok, self.copy(
            src, self.block(zi, y, core), ss.at[s], rs.at[s + 1], at(z + way, y, core, self.ys))

    def arrived(self, way, s):
        z, y, core = self.pos
        zi = z - way * s
        ss, rs = (self.szr, self.rzr) if way > 0 else (self.szl, self.rzl)
        ok = (zi >= 0) & (zi < self.zs)
        return ok, zi, self.copy(
            self.src, self.block(zi, y, core), ss.at[0], rs.at[s], at(z, y, 1 - core, self.ys))

    def to_y(self, j, zi, own):
        z, y, core = self.pos
        src = self.src if own else self.block(zi, y, core)
        return self.copy(src, self.block(zi, y, core), self.sy.at[j, zi], self.ry.at[j, zi],
                         at(z, lax.rem(y + j, self.ys), core, self.ys))

    def from_y(self, j, zi):
        z, y, core = self.pos
        yi = lax.rem(y + self.ys - j, self.ys)
        return self.copy(self.src, self.block(zi, yi, core), self.sy.at[j, zi], self.ry.at[j, zi],
                         at(z, lax.rem(y + j, self.ys), core, self.ys))

    def to_core(self, j, zi, own):
        z, y, core = self.pos
        yi = lax.rem(y + self.ys - j, self.ys)
        src = self.src if own else self.block(zi, yi, core)
        return self.copy(src, self.block(zi, yi, core), self.sc.at[j, zi], self.rc.at[j, zi],
                         at(z, y, 1 - core, self.ys))

    def from_core(self, j, zi):
        z, y, core = self.pos
        yi = lax.rem(y + self.ys - j, self.ys)
        return self.copy(self.src, self.block(zi, yi, 1 - core), self.sc.at[j, zi],
                         self.rc.at[j, zi], at(z, y, 1 - core, self.ys))

    def start(self):
        z, y, core = self.pos
        for way in (1, -1):
            ok, copy = self.hop(way, 0)
            pl.when(ok)(copy.start)
        for j in range(1, self.ys):
            self.to_y(j, z, True).start()
        self.to_core(0, z, True).start()
        self.out[z, y, core, self.rows] = self.src[...]

    def forward_z(self, s):
        for way in (1, -1):
            ok, zi, here = self.arrived(way, s)

            @pl.when(ok)
            def _():
                here.wait_recv()
                for j in range(1, self.ys):
                    self.to_y(j, zi, False).start()

            if s < self.zs - 1:
                more, on = self.hop(way, s)
                pl.when(more)(on.start)

            @pl.when(ok)
            def _():
                self.to_core(0, zi, False).start()

    def forward_y(self, s):
        z = self.pos[0]
        todo = [(None, z)] if s == 0 else [
            ((z - way * s >= 0) & (z - way * s < self.zs), z - way * s) for way in (1, -1)]
        for ok, zi in todo:

            def step(zi=zi):
                for j in range(1, self.ys):
                    self.from_y(j, zi).wait_recv()
                    self.to_core(j, zi, False).start()

            step() if ok is None else pl.when(ok)(step)

    def finish(self):
        for zi in range(self.zs):
            for j in range(self.ys):
                self.from_core(j, zi).wait_recv()

    def drain(self):
        for s in range(self.zs - 1):
            for way in (1, -1):
                ok, copy = self.hop(way, s)
                pl.when(ok)(copy.wait_send)
        for zi in range(self.zs):
            for j in range(self.ys):
                if j:
                    self.to_y(j, zi, False).wait_send()
                self.to_core(j, zi, False).wait_send()


def flip(v, i):
    bit = 1
    while bit <= i:
        if i & bit:
            v = v + bit - 2 * bit * lax.rem(v // bit, 2)
        bit *= 2
    return v


class Star:
    def __init__(self, pos, zs, ys, src, out, sems):
        self.pos, self.zs, self.ys, self.src, self.out = pos, zs, ys, src, out
        self.sz, self.rz, self.sy, self.ry, self.sc, self.rc = sems

    def copy(self, src, dst, ssem, rsem, device):
        return pltpu.make_async_remote_copy(
            src, dst, ssem, rsem, device_id=device, device_id_type=MESH)

    def block(self, i, j, k):
        z, y, core = self.pos
        return self.out.at[flip(z, i), flip(y, j), flip(core, k)]

    def held(self, i, j):
        return self.src if i == 0 and j == 0 else self.block(i, j, 0)

    def z_copy(self, i, arriving):
        z, y, core = self.pos
        return self.copy(self.src, self.block(i if arriving else 0, 0, 0), self.sz.at[i],
                         self.rz.at[i], at(flip(z, i), y, core, self.ys))

    def y_copy(self, j, i, arriving):
        z, y, core = self.pos
        return self.copy(self.held(i, 0), self.block(i, j if arriving else 0, 0), self.sy.at[j, i],
                         self.ry.at[j, i], at(z, flip(y, j), core, self.ys))

    def core_copy(self, j, i, arriving):
        z, y, core = self.pos
        return self.copy(self.held(i, j), self.block(i, j, 1 if arriving else 0), self.sc.at[j, i],
                         self.rc.at[j, i], at(z, y, 1 - core, self.ys))

    def start(self):
        for i in reversed(range(1, self.zs)):
            self.z_copy(i, False).start()
        for j in range(1, self.ys):
            self.y_copy(j, 0, False).start()
        self.core_copy(0, 0, False).start()
        z, y, core = self.pos
        self.out[z, y, core] = self.src[...]

    def forward_z(self, i):
        self.z_copy(i, True).wait_recv()
        for j in range(1, self.ys):
            self.y_copy(j, i, False).start()
        self.core_copy(0, i, False).start()

    def forward_y(self, i):
        for j in range(1, self.ys):
            self.y_copy(j, i, True).wait_recv()
            self.core_copy(j, i, False).start()

    def finish(self):
        for i in range(self.zs):
            for j in range(self.ys):
                self.core_copy(j, i, True).wait_recv()

    def drain(self):
        for i in range(self.zs):
            if i:
                self.z_copy(i, False).wait_send()
            for j in range(self.ys):
                if j:
                    self.y_copy(j, i, False).wait_send()
                self.core_copy(j, i, False).wait_send()


class Pair:
    def __init__(self, me, n, sides):
        self.has_right, self.has_left = me < n - 1, me > 0
        self.copies = [pltpu.make_async_remote_copy(
            src, dst, ssem, rsem, device_id={"cols": peer}, device_id_type=MESH)
            for (src, dst, ssem, rsem), peer in zip(
                sides, (lax.rem(me + 1, n), lax.rem(me + n - 1, n)))]

    def start(self):
        pl.when(self.has_right)(self.copies[0].start)
        pl.when(self.has_left)(self.copies[1].start)

    def wait(self):
        pl.when(self.has_left)(self.copies[0].wait_recv)
        pl.when(self.has_right)(self.copies[1].wait_recv)
        pl.when(self.has_right)(self.copies[0].wait_send)
        pl.when(self.has_left)(self.copies[1].wait_send)


class Sum:
    def __init__(self, pos, zs, ys, terms, bufs, sems):
        self.pos, self.zs, self.ys, self.terms = pos, zs, ys, terms
        self.s1, self.s2, self.bufc, self.bufy, self.bufz = bufs
        self.sc, self.rc, self.sy, self.ry, self.sz, self.rz = sems
        self.zorder = list(range(1, zs)) + [0]
        self.yorder = list(range(1, ys)) + [0]

    def zi(self, i):
        return lax.rem(self.pos[0] + i, self.zs)

    def yi(self, j):
        return lax.rem(self.pos[1] + j, self.ys)

    def copy(self, src, dst, ssem, rsem, device):
        return pltpu.make_async_remote_copy(
            src, dst, ssem, rsem, device_id=device, device_id_type=MESH)

    def core_copy(self, j, i):
        z, y, core = self.pos
        return self.copy(self.terms.at[self.zi(i), self.yi(j), 1 - core], self.bufc.at[j, i],
                         self.sc.at[j, i], self.rc.at[j, i], at(z, y, 1 - core, self.ys))

    def y_copy(self, j, i):
        z, y, core = self.pos
        return self.copy(self.s1.at[j, i], self.bufy.at[j, i], self.sy.at[j, i],
                         self.ry.at[j, i], at(z, self.yi(j), core, self.ys))

    def z_copy(self, i):
        z, y, core = self.pos
        return self.copy(self.s2.at[i], self.bufz.at[i], self.sz.at[i], self.rz.at[i],
                         at(self.zi(i), y, core, self.ys))

    def start(self):
        for j in self.yorder:
            for i in self.zorder:
                self.core_copy(j, i).start()

    def pair(self):
        core = self.pos[2]
        for j in self.yorder:
            for i in self.zorder:
                self.core_copy(j, i).wait_recv()
                both = self.terms[self.zi(i), self.yi(j), core].astype(F32)
                self.s1[j, i] = (both + self.bufc[j, i].astype(F32)).astype(BF16)
                if j:
                    self.y_copy(j, i).start()

    def along_y(self, begin, end):
        for i in self.zorder[begin:end]:
            total = self.s1[0, i].astype(F32)
            for j in range(1, self.ys):
                self.y_copy(j, i).wait_recv()
                total = total + self.bufy[j, i].astype(F32)
            if i:
                self.s2[i] = total.astype(BF16)
                self.z_copy(i).start()
            else:
                self.own = total

    def along_z(self):
        total = self.own
        for i in range(1, self.zs):
            self.z_copy(i).wait_recv()
            total = total + self.bufz[i].astype(F32)
        return total

    def drain(self):
        for j in self.yorder:
            for i in self.zorder:
                self.core_copy(j, i).wait_send()
                if j:
                    self.y_copy(j, i).wait_send()
        for i in range(1, self.zs):
            self.z_copy(i).wait_send()


class Sum2:
    def __init__(self, pos, zs, ys, terms, cut, bufs, sems):
        self.pos, self.zs, self.ys, self.terms = pos, zs, ys, terms
        self.s1, self.bufc, self.bufy, self.s2a, self.bufz, self.bufw, self.s2b, self.bufv = bufs
        self.sc, self.rc, self.sy, self.ry, self.sz, self.rz, self.sw, self.rw, self.sv, self.rv = sems
        self.cut, width = cut, terms.shape[-1]
        self.lanes_a, self.lanes_b = pl.ds(0, cut), pl.ds(cut, width - cut)
        self.zorder = list(range(1, zs)) + [0]
        self.yorder = list(range(1, ys)) + [0]

    def zi(self, i):
        return lax.rem(self.pos[0] + i, self.zs)

    def yi(self, j):
        return lax.rem(self.pos[1] + j, self.ys)

    def y_peer(self, j):
        return at(self.pos[0], self.yi(j), self.pos[2], self.ys)

    def z_peer(self, i):
        return at(self.zi(i), self.pos[1], self.pos[2], self.ys)

    def copy(self, src, dst, ssem, rsem, device):
        return pltpu.make_async_remote_copy(
            src, dst, ssem, rsem, device_id=device, device_id_type=MESH)

    def core_copy(self, j, i):
        z, y, core = self.pos
        return self.copy(self.terms.at[self.zi(i), self.yi(j), 1 - core], self.bufc.at[j, i],
                         self.sc.at[j, i], self.rc.at[j, i], at(z, y, 1 - core, self.ys))

    def y_copies(self, j):
        return [self.copy(self.s1.at[j, i, :, self.lanes_a], self.bufy.at[j, i], self.sy.at[j, i],
                          self.ry.at[j, i], self.y_peer(j)) for i in self.zorder]

    def w_copy(self, i):
        return self.copy(self.s1.at[:, i, :, self.lanes_b], self.bufw.at[i], self.sw.at[i],
                         self.rw.at[i], self.z_peer(i))

    def z_copy(self, i):
        return self.copy(self.s2a.at[i], self.bufz.at[i], self.sz.at[i], self.rz.at[i], self.z_peer(i))

    def v_copy(self, j):
        return self.copy(self.s2b.at[j], self.bufv.at[j], self.sv.at[j], self.rv.at[j], self.y_peer(j))

    def start(self):
        for j in self.yorder:
            for i in self.zorder:
                self.core_copy(j, i).start()

    def pair(self):
        core = self.pos[2]
        for j in self.yorder:
            for i in self.zorder:
                self.core_copy(j, i).wait_recv()
                both = self.terms[self.zi(i), self.yi(j), core].astype(F32)
                self.s1[j, i] = (both + self.bufc[j, i].astype(F32)).astype(BF16)
            if j:
                for copy in self.y_copies(j):
                    copy.start()
        for i in self.zorder[:-1]:
            self.w_copy(i).start()

    def second_b(self):
        for i in self.zorder[:-1]:
            self.w_copy(i).wait_recv()
        for j in self.yorder:
            total = self.s1[j, 0, :, self.lanes_b].astype(F32)
            for i in self.zorder[:-1]:
                total = total + self.bufw[i, j].astype(F32)
            if j:
                self.s2b[j] = total.astype(BF16)
                self.v_copy(j).start()
            else:
                self.own_b = total

    def second_a(self, begin, end):
        for i in self.zorder[begin:end]:
            total = self.s1[0, i, :, self.lanes_a].astype(F32)
            for j in range(1, self.ys):
                copies = self.y_copies(j)
                if len(copies) > 1:
                    copies[self.zorder.index(i)].wait_recv()
                elif i == self.zorder[0]:
                    copies[0].wait_recv()
                total = total + self.bufy[j, i].astype(F32)
            if i:
                self.s2a[i] = total.astype(BF16)
                self.z_copy(i).start()
            else:
                self.own_a = total

    def last_b(self):
        total = self.own_b
        for j in range(1, self.ys):
            self.v_copy(j).wait_recv()
            total = total + self.bufv[j].astype(F32)
        return total

    def last_a(self):
        total = self.own_a
        for i in range(1, self.zs):
            self.z_copy(i).wait_recv()
            total = total + self.bufz[i].astype(F32)
        return total

    def drain(self):
        for j in self.yorder:
            for i in self.zorder:
                self.core_copy(j, i).wait_send()
            if j:
                for copy in self.y_copies(j):
                    copy.wait_send()
                self.v_copy(j).wait_send()
        for i in range(1, self.zs):
            self.w_copy(i).wait_send()
            self.z_copy(i).wait_send()


def tap(t):
    return slice(t * LANES, (t + 1) * LANES)


def conv_taps(ref, w, start, step, count):
    total = None
    for kx in range(3):
        rhs = jnp.concatenate([w[:, tap(3 * ky + kx)] for ky in range(3)], axis=1)
        term = lax.dot_general(ref[pl.ds(start + kx * step, count), :], rhs,
                               (((1,), (1,)), ((), ())), preferred_element_type=F32)
        total = term if total is None else total + term
    return total


def join_rows(prod, d, height, kx):
    up = from_below(prod[:, tap(kx)], d, height)
    down = from_above(prod[:, tap(6 + kx)], d, height)
    return up + prod[:, tap(3 + kx)] + down


def put_terms(ref, place, value):
    zs, ys = ref.shape[0], ref.shape[1]
    (first, count), t = place
    ref[:, :, :, first : first + count, tap(t)] = value.reshape(zs, ys, 2, count, LANES).astype(BF16)


def grad_taps(ref, places, slope_f32, acts, start, step):
    count = slope_f32.shape[0]
    turned = slope_f32.T.astype(BF16)
    for kx in range(3):
        prod = jnp.dot(turned, acts[pl.ds(start + kx * step, count), :],
                       preferred_element_type=F32)
        for ky in range(3):
            put_terms(ref, places[3 * ky + kx], prod[:, tap(ky)])


def fused_kernel(
    n, zs, ys, height, breadth, rl, rm, rf,
    x_ref, t_ref, wl_ref, wm_ref, wf_ref, o1_ref, o2_ref, o3_ref,
    xv, tv, wlv, wmv, wfv,
    pa, ga, gb, ta, tb, xh, xs, x9, x3f, x3s, pre1, pre2, acc, send, recv, tf, tn,
    a1, a2, a3, a4, a5, b1, b2, b3, b4, b5, b6, b7, b8, lsem, sx, rx, ssem, rsem, *sems,
):
    me, z, y, core = place(n, zs, ys)
    pos = (z, y, core)
    h, b = height, breadth
    depth = wf_ref.shape[1] // 9
    left, right = lax.rem(me + n - 1, n), lax.rem(me + 1, n)
    loads = [pltpu.make_async_copy(src, dst, lsem.at[i]) for i, (src, dst) in enumerate(
        ((wm_ref, wmv), (wf_ref, wfv), (x_ref, xv), (wl_ref, wlv), (t_ref, tv)))]
    for load in loads:
        load.start()
    peers = (
        [at(flip(z, i), y, core, ys) for i in range(1, zs)]
        + [at(z, flip(y, j), core, ys) for j in range(1, ys)]
        + [at(z, y, 1 - core, ys), {"cols": left}, {"cols": right}]
    )
    call(peers)
    middle = [((0, rm), t) if t < 7 else ((rm, rf), t - 7) for t in range(9)]
    first = [((rm, rf), t + 2) for t in range(5)]
    low = Star(pos, zs, ys, pa, ga, sems[0:6])
    cut = rl // 16 * 8
    parts = ((0, cut), (cut, rl - cut)) if cut else ((0, rl),)
    high = [Line(pos, zs, ys, wlv, gb, begin, rows, sems[8 * i + 6 : 8 * i + 14])
            for i, (begin, rows) in enumerate(parts)]
    sum_a = Sum(pos, zs, ys, ta, (a1, a2, a3, a4, a5), sems[22:28])
    sum_b = Sum2(pos, zs, ys, tb, 6 * LANES, (b1, b2, b3, b4, b5, b6, b7, b8), sems[28:38])
    loads[0].wait()
    loads[1].wait()
    pa[0:rm, :] = wmv[:, 0 : 7 * LANES]
    pa[rm : rm + rf, 0 : 2 * LANES] = wmv[:, 7 * LANES : 9 * LANES]
    pa[rm : rm + rf, 6 * LANES : 7 * LANES] = jnp.zeros((rf, LANES), BF16)
    pa[rm : rm + rf, 2 * LANES : 2 * LANES + 9 * depth] = wfv[...]
    hear(peers)
    low.start()
    loads[2].wait()
    edge = 14 * depth
    halo = Pair(me, n, [(xv.at[:, pl.ds(b * depth - edge, edge)], xh.at[0], sx.at[0], rx.at[0]),
                        (xv.at[:, pl.ds(0, edge)], xh.at[1], sx.at[1], rx.at[1])])
    halo.start()
    loads[3].wait()
    for line in high:
        line.start()

    loads[4].wait()
    target = tv[...].astype(F32)
    t_norm = jnp.sqrt(jnp.sum(target * target, -1, keepdims=True) + epsilon)
    target = target / t_norm
    for q in range(tf.shape[0]):
        tf[q] = target[:, tap(q)]
    for i in reversed(range(1, zs)):
        low.forward_z(i)
    for c in range(b):
        for q in range(tf.shape[0]):
            tn[pl.ds(c * h, h), tap(q)] = tf[q, pl.ds(c, h, stride=b), :]
    for line in high:
        line.forward_z(1)

    first_col = me * b
    width = n * b

    def inside(v, first):
        cols = column_of(v.shape[0], h, first_col + first)
        return jnp.where((cols >= 0) & (cols < width), v, 0.0)

    halo.wait()
    half = lax.broadcasted_iota(jnp.int32, (h, LANES), 1) < depth
    at_col = 0
    for part, pairs in ((xh[0], 7), (xv[...], b // 2), (xh[1], 7)):
        part = part.astype(F32)
        for q in range(pairs):
            both = part[:, tap(q)]
            turned = pltpu.roll(both, depth, 1)
            xs[pl.ds(at_col * h, h), :] = jnp.where(half, both, turned)
            xs[pl.ds((at_col + 1) * h, h), :] = jnp.where(half, turned, both)
            at_col += 2
    for i in [0] + list(reversed(range(1, zs))):
        low.forward_y(i)
    for line in high:
        line.forward_z(2)
    wide_x = inside(xs[...], -14)
    count1 = (b + 24) * h
    rows3 = (from_above(wide_x, 2, h), wide_x, from_below(wide_x, 2, h))

    def piece(t):
        ky, kx = t // 3, t % 3
        return rows3[ky][kx * 2 * h : kx * 2 * h + count1]

    lower = lax.broadcasted_iota(jnp.int32, (count1, LANES), 1) < depth
    for q in range(5):
        odd = piece(2 * q + 1) if q < 4 else 0.0
        x9[:, tap(q)] = jnp.where(lower, piece(2 * q), odd).astype(BF16)
    for s in range(3, zs):
        for line in high:
            line.forward_z(s)
    low.finish()
    w1 = ga[:, :, :, rm : rm + rf, 2 * LANES : 7 * LANES].reshape(n * rf, 5 * LANES)
    v = lax.dot_general(x9[...], w1, (((1,), (1,)), ((), ())), preferred_element_type=F32)
    pre1[...] = v
    act = inside(v * sigmoid(v), -12).astype(BF16).astype(F32)
    spread_rows(x3f, act, 4, h)
    for line in high:
        for s in range(zs - 1):
            line.forward_y(s)
    w2 = jnp.concatenate([
        ga[:, :, :, 0:rm, :].reshape(n * rm, 7 * LANES),
        ga[:, :, :, rm : rm + rf, 0 : 2 * LANES].reshape(n * rm, 2 * LANES)], axis=1)
    v = conv_taps(x3f, w2, 0, 4 * h, (b + 16) * h)
    pre2[...] = v
    act = inside(v * sigmoid(v), -8).astype(BF16).astype(F32)
    spread_rows(x3s, act, 8, h)
    for line in high:
        line.forward_y(zs - 1)
    for line in high:
        line.finish()
    w3 = gb[...].reshape(n * rl, 9 * LANES)
    student = conv_taps(x3s, w3, 0, 8 * h, b * h)
    s_norm = jnp.sqrt(jnp.sum(student * student, -1, keepdims=True) + epsilon)
    s_unit = student / s_norm
    differ = s_unit - tn[...]
    slope = (differ - s_unit * jnp.sum(s_unit * differ, -1, keepdims=True)) / s_norm

    prod = jnp.dot(slope.astype(BF16), w3, preferred_element_type=F32)
    e = 8 * h
    m = b * h
    acc[pl.ds(0, m), :] = join_rows(prod, 8, h, 0)
    acc[pl.ds(m, 2 * e), :] = jnp.zeros((2 * e, LANES), F32)
    acc[pl.ds(e, m), :] += join_rows(prod, 8, h, 1)
    acc[pl.ds(2 * e, m), :] += join_rows(prod, 8, h, 2)
    part = 12 * h
    send[0] = acc[pl.ds(m + 2 * e - part, part), :].astype(BF16)
    send[1] = acc[pl.ds(0, part), :].astype(BF16)
    copies = Pair(me, n, [(send.at[side], recv.at[side], ssem.at[side], rsem.at[side])
                          for side in range(2)])
    copies.start()
    grad_taps(tb, [((0, rl), t) for t in range(9)], slope, x3s, 0, 8 * h)
    sum_b.start()
    sum_b.pair()
    copies.wait()
    inner = (b + 8) * h
    split = inner - part
    from_left = jnp.where(me > 0, recv[0].astype(F32), 0.0)
    from_right = jnp.where(me < n - 1, recv[1].astype(F32), 0.0)
    acc[pl.ds(4 * h, part), :] += from_left
    acc[pl.ds(4 * h + split, part), :] += from_right
    back = acc[pl.ds(4 * h, inner), :]
    slope2 = inside(back * silu_slope(pre2[pl.ds(4 * h, inner), :]), -4).astype(BF16)
    prod = jnp.dot(slope2, w2, preferred_element_type=F32)
    back = (
        join_rows(prod, 4, h, 0)[8 * h : 8 * h + m]
        + join_rows(prod, 4, h, 1)[4 * h : 4 * h + m]
        + join_rows(prod, 4, h, 2)[0:m]
    )
    grad_taps(ta, middle, slope2.astype(F32)[4 * h : 4 * h + m], x3f, 8 * h, 4 * h)
    slope1 = back * silu_slope(pre1[pl.ds(12 * h, m), :])
    prod = jnp.dot(slope1.T.astype(BF16), x9[pl.ds(12 * h, m), :], preferred_element_type=F32)
    for q in range(5):
        put_terms(ta, first[q], prod[:, tap(q)])
    sum_a.start()
    sum_b.second_a(0, 1)
    sum_a.pair()
    sum_b.second_a(1, 2)
    sum_b.second_b()
    sum_b.second_a(2, zs)
    sum_a.along_y(0, zs)
    o3_ref[:, sum_b.lanes_a] = sum_b.last_a()
    o3_ref[:, sum_b.lanes_b] = sum_b.last_b()
    total = sum_a.along_z()
    o2_ref[:, 0 : 7 * LANES] = total[0:rm]
    o2_ref[:, 7 * LANES : 9 * LANES] = total[rm : rm + rf, 0 : 2 * LANES]
    o1_ref[...] = total[rm : rm + rf, 2 * LANES : 2 * LANES + 9 * depth]
    for each in (low, *high, sum_a, sum_b):
        each.drain()


def hand_over_kernel(a_ref, b_ref, c_ref, x_ref, y_ref, z_ref):
    x_ref[...] = a_ref[...]
    y_ref[...] = b_ref[...]
    z_ref[...] = c_ref[...]


def hand_over(arrays):
    vmem = pl.BlockSpec(memory_space=pltpu.VMEM)
    return pl.pallas_call(
        hand_over_kernel,
        out_shape=tuple(jax.ShapeDtypeStruct(a.shape, a.dtype) for a in arrays),
        in_specs=[vmem] * 3,
        out_specs=(vmem,) * 3,
        name="hand_over",
    )(*(pltpu.with_memory_space_constraint(a, pltpu.VMEM) for a in arrays))


def fused(n, height, breadth, x, t, wl, wm, wf):
    zs, ys = split_axis(n)
    sem = pltpu.SemaphoreType.DMA
    vmem = pl.BlockSpec(memory_space=pltpu.VMEM)
    h, b = height, breadth
    rl, rm, rf = wl.shape[0], wm.shape[0], wf.shape[0]
    wide = wl.shape[1]
    low, high = (rm + rf, 7 * LANES), (rl, wide)
    channels = t.shape[1]

    def sum_bufs(block):
        return [
            pltpu.VMEM((ys, zs) + block, BF16), pltpu.VMEM((zs,) + block, BF16),
            pltpu.VMEM((ys, zs) + block, BF16), pltpu.VMEM((ys, zs) + block, BF16),
            pltpu.VMEM((zs,) + block, BF16),
        ]

    def sum2_bufs(block, cut):
        rows, width = block
        part_a, part_b = (rows, cut), (rows, width - cut)
        return [
            pltpu.VMEM((ys, zs) + block, BF16), pltpu.VMEM((ys, zs) + block, BF16),
            pltpu.VMEM((ys, zs) + part_a, BF16), pltpu.VMEM((zs,) + part_a, BF16),
            pltpu.VMEM((zs,) + part_a, BF16), pltpu.VMEM((zs, ys) + part_b, BF16),
            pltpu.VMEM((ys,) + part_b, BF16), pltpu.VMEM((ys,) + part_b, BF16),
        ]

    star_sems = [sem((zs,))] * 2 + [sem((ys, zs))] * 4
    line_sems = [sem((zs,))] * 4 + [sem((ys, zs))] * 4
    sum_sems = [sem((ys, zs))] * 4 + [sem((zs,))] * 2
    sum2_sems = [sem((ys, zs))] * 4 + [sem((zs,))] * 4 + [sem((ys,))] * 2
    return pl.pallas_call(
        functools.partial(fused_kernel, n, zs, ys, h, b, rl, rm, rf),
        out_shape=tuple(pltpu.VMEM(w.shape, F32) for w in (wf, wm, wl)),
        in_specs=[pl.BlockSpec(memory_space=pltpu.HBM)] * 5,
        out_specs=(vmem,) * 3,
        scratch_shapes=[pltpu.VMEM(w.shape, BF16) for w in (x, t, wl, wm, wf)] + [
            pltpu.VMEM(low, BF16),
            pltpu.VMEM((zs, ys, 2) + low, BF16),
            pltpu.VMEM((zs, ys, 2) + high, BF16),
            pltpu.VMEM((zs, ys, 2) + low, BF16),
            pltpu.VMEM((zs, ys, 2) + high, BF16),
            pltpu.VMEM((2, h, 14 * wf.shape[1] // 9), BF16),
            pltpu.VMEM(((b + 28) * h, LANES), F32),
            pltpu.VMEM(((b + 24) * h, 5 * LANES), BF16),
            pltpu.VMEM(((b + 24) * h, 3 * LANES), BF16),
            pltpu.VMEM(((b + 16) * h, 3 * LANES), BF16),
            pltpu.VMEM(((b + 24) * h, LANES), F32),
            pltpu.VMEM(((b + 16) * h, LANES), F32),
            pltpu.VMEM(((b + 16) * h, LANES), F32),
            pltpu.VMEM((2, 12 * h, LANES), BF16),
            pltpu.VMEM((2, 12 * h, LANES), BF16),
            pltpu.VMEM((channels // LANES, b * h, LANES), F32),
            pltpu.VMEM((b * h, channels), F32),
        ]
        + sum_bufs(low) + sum2_bufs(high, 6 * LANES)
        + [sem((5,))] + [sem((2,))] * 4 + star_sems + line_sems * 2 + sum_sems + sum2_sems,
        compiler_params=pltpu.CompilerParams(
            collective_id=3, has_side_effects=True, vmem_limit_bytes=56 << 20),
        name="fused_step",
    )(x, t, wl, wm, wf)


def on_device(n, image_feats, teacher, w_first, w_middle, w_last):
    height, breadth, channels = teacher.shape
    in_depth = w_first.shape[1] // 9
    rl, rm, rf = w_last.shape[0], w_middle.shape[0], w_first.shape[0]
    if (split_axis(n)[0] > 2 and n & (n - 1) == 0 and rm == rf and all(r % 8 == 0 for r in (rl, rm, rf))
            and breadth % 8 == 0 and 2 * in_depth == LANES):
        return hand_over(fused(n, height, breadth, image_feats,
                               teacher.reshape(height * breadth, channels), w_last, w_middle, w_first))
    packed = jnp.concatenate([taps_by_column(w) for w in (w_last, w_middle, w_first)], axis=0)
    x = image_feats.reshape(height, breadth, in_depth).transpose(1, 0, 2)
    x = jnp.pad(x, ((0, 0), (0, 0), (0, LANES - in_depth)))
    x_cells = x.reshape(breadth * height, LANES)
    t_cells = teacher.transpose(1, 0, 2).reshape(breadth * height, channels)
    gathered, x_edges = gather(n, packed, x_cells, 14 * height)
    g = gathered.reshape((n,) + packed.shape)
    w3 = g[:, :rl].reshape(n * rl, -1)
    w2 = g[:, rl : rl + rm].reshape(n * rm, -1)
    w1 = g[:, rl + rm :].reshape(n * rf, -1)
    g1, g2, g3 = local_step(n, height, breadth, x_cells, x_edges, t_cells, w1, w2, w3)
    terms = jnp.concatenate(
        [g3.reshape(n, rl, -1), g2.reshape(n, rm, -1), g1.reshape(n, rf, -1)], axis=1)
    out = scatter(n, terms.reshape(gathered.shape))
    return (
        taps_by_row(out[rl + rm :], in_depth),
        taps_by_row(out[rl : rl + rm], LANES),
        taps_by_row(out[:rl], LANES),
    )


def solution(mesh):
    placed = (
        P("groups", "cols"),
        P("groups", "cols", None),
        P("cols", None),
        P("cols", None),
        P("cols", None),
    )
    return jax.shard_map(
        functools.partial(on_device, mesh.shape["cols"]),
        mesh=mesh,
        in_specs=placed,
        out_specs=(P(("groups", "cols"), None),) * 3,
        check_vma=False,
    )
```

```python
import functools

import jax
import jax.numpy as jnp
from jax import lax
from jax.experimental import pallas as pl
from jax.experimental.pallas import tpu as pltpu
from jax.sharding import PartitionSpec as P

epsilon = 1e-06
MESH = pl.DeviceIdType.MESH
LANES = 128
F32 = jnp.float32
BF16 = jnp.bfloat16


def split_axis(n):
    half = n // 2
    y = 1
    while 4 * y * y <= half:
        y *= 2
    return half // y, y


def place(n, z_size, y_size):
    me = lax.axis_index("cols")
    core = lax.rem(me, 2)
    y = lax.rem(me // 2, y_size)
    z = me // (2 * y_size)
    return me, z, y, core


def at(z, y, core, y_size):
    return {"cols": (z * y_size + y) * 2 + core}


def call(peers):
    barrier = pltpu.get_barrier_semaphore()
    for peer in peers:
        pl.semaphore_signal(barrier, inc=1, device_id=peer, device_id_type=MESH)


def hear(peers):
    pl.semaphore_wait(pltpu.get_barrier_semaphore(), len(peers))


def greet(peers):
    call(peers)
    hear(peers)


def gather_kernel(n, zs, ys, edge, p_ref, x_ref, g_ref, xh_ref, sz, rz, sy, ry, sc, rc, sx, rx):
    me, z, y, core = place(n, zs, ys)
    other = 1 - core
    zmod = [lax.rem(z + i, zs) for i in range(zs)]
    zback = [lax.rem(z + zs - i, zs) for i in range(zs)]
    ymod = [lax.rem(y + i, ys) for i in range(ys)]
    yback = [lax.rem(y + ys - i, ys) for i in range(ys)]
    left, right = lax.rem(me + n - 1, n), lax.rem(me + 1, n)
    greet(
        [at(zmod[i], y, core, ys) for i in range(1, zs)]
        + [at(z, ymod[j], core, ys) for j in range(1, ys)]
        + [at(z, y, other, ys), {"cols": left}, {"cols": right}]
    )

    def block(zi, yi, c):
        return g_ref.at[zi, yi, c]

    def to_z(i):
        return pltpu.make_async_remote_copy(
            p_ref, block(z, y, core), sz.at[i], rz.at[i],
            device_id=at(zmod[i], y, core, ys), device_id_type=MESH)

    def from_z(i):
        return pltpu.make_async_remote_copy(
            p_ref, block(zback[i], y, core), sz.at[i], rz.at[i],
            device_id=at(zmod[i], y, core, ys), device_id_type=MESH)

    def to_y(j, i):
        src = p_ref if i == 0 else block(zback[i], y, core)
        return pltpu.make_async_remote_copy(
            src, block(zback[i], y, core), sy.at[j, i], ry.at[j, i],
            device_id=at(z, ymod[j], core, ys), device_id_type=MESH)

    def from_y(j, i):
        return pltpu.make_async_remote_copy(
            p_ref, block(zback[i], yback[j], core), sy.at[j, i], ry.at[j, i],
            device_id=at(z, ymod[j], core, ys), device_id_type=MESH)

    def to_core(j, i):
        src = p_ref if i == 0 and j == 0 else block(zback[i], yback[j], core)
        return pltpu.make_async_remote_copy(
            src, block(zback[i], yback[j], core), sc.at[j, i], rc.at[j, i],
            device_id=at(z, y, other, ys), device_id_type=MESH)

    def from_core(j, i):
        return pltpu.make_async_remote_copy(
            p_ref, block(zback[i], yback[j], other), sc.at[j, i], rc.at[j, i],
            device_id=at(z, y, other, ys), device_id_type=MESH)

    cells = x_ref.shape[0]
    to_right = pltpu.make_async_remote_copy(
        x_ref.at[pl.ds(cells - edge, edge)], xh_ref.at[0], sx.at[0], rx.at[0],
        device_id={"cols": right}, device_id_type=MESH)
    to_left = pltpu.make_async_remote_copy(
        x_ref.at[pl.ds(0, edge)], xh_ref.at[1], sx.at[1], rx.at[1],
        device_id={"cols": left}, device_id_type=MESH)
    started = []

    def go(copy):
        copy.start()
        started.append(copy)

    for i in range(1, zs):
        go(to_z(i))
    for j in range(1, ys):
        go(to_y(j, 0))
    go(to_right)
    go(to_left)
    go(to_core(0, 0))
    g_ref[z, y, core] = p_ref[...]
    for i in range(1, zs):
        from_z(i).wait_recv()
        for j in range(1, ys):
            go(to_y(j, i))
        go(to_core(0, i))
    for i in range(zs):
        for j in range(1, ys):
            from_y(j, i).wait_recv()
            go(to_core(j, i))
    to_right.wait_recv()
    to_left.wait_recv()
    for i in range(zs):
        for j in range(ys):
            from_core(j, i).wait_recv()
    for copy in started:
        copy.wait_send()


def gather(n, packed, x_cells, edge):
    zs, ys = split_axis(n)
    sem = pltpu.SemaphoreType.DMA
    vmem = pl.BlockSpec(memory_space=pltpu.VMEM)
    return pl.pallas_call(
        functools.partial(gather_kernel, n, zs, ys, edge),
        out_shape=(
            jax.ShapeDtypeStruct((zs, ys, 2) + packed.shape, BF16),
            jax.ShapeDtypeStruct((2, edge, x_cells.shape[1]), BF16),
        ),
        in_specs=[vmem, vmem],
        out_specs=(vmem, vmem),
        scratch_shapes=[
            sem((zs,)), sem((zs,)), sem((ys, zs)), sem((ys, zs)), sem((ys, zs)), sem((ys, zs)),
            sem((2,)), sem((2,)),
        ],
        compiler_params=pltpu.CompilerParams(
            collective_id=0, has_side_effects=True, vmem_limit_bytes=48 << 20),
        name="gather_weights",
    )(packed, x_cells)


def scatter_kernel(n, zs, ys, t_ref, out_ref, s1, s2, bufc, bufy, bufz, sc, rc, sy, ry, sz, rz):
    me, z, y, core = place(n, zs, ys)
    other = 1 - core
    zmod = [lax.rem(z + i, zs) for i in range(zs)]
    ymod = [lax.rem(y + i, ys) for i in range(ys)]
    greet(
        [at(zmod[i], y, core, ys) for i in range(1, zs)]
        + [at(z, ymod[j], core, ys) for j in range(1, ys)]
        + [at(z, y, other, ys)]
    )
    zorder = list(range(1, zs)) + [0]
    yorder = list(range(1, ys)) + [0]

    def core_copy(j, i):
        return pltpu.make_async_remote_copy(
            t_ref.at[zmod[i], ymod[j], other], bufc.at[j, i], sc.at[j, i], rc.at[j, i],
            device_id=at(z, y, other, ys), device_id_type=MESH)

    def y_copy(j, i):
        return pltpu.make_async_remote_copy(
            s1.at[j, i], bufy.at[j, i], sy.at[j, i], ry.at[j, i],
            device_id=at(z, ymod[j], core, ys), device_id_type=MESH)

    def z_copy(i):
        return pltpu.make_async_remote_copy(
            s2.at[i], bufz.at[i], sz.at[i], rz.at[i],
            device_id=at(zmod[i], y, core, ys), device_id_type=MESH)

    started = []

    def go(copy):
        copy.start()
        started.append(copy)

    for j in yorder:
        for i in zorder:
            go(core_copy(j, i))
    for j in yorder:
        for i in zorder:
            core_copy(j, i).wait_recv()
            both = t_ref[zmod[i], ymod[j], core].astype(F32) + bufc[j, i].astype(F32)
            s1[j, i] = both.astype(BF16)
            if j:
                go(y_copy(j, i))
    for i in zorder:
        total = s1[0, i].astype(F32)
        for j in range(1, ys):
            y_copy(j, i).wait_recv()
            total = total + bufy[j, i].astype(F32)
        if i:
            s2[i] = total.astype(BF16)
            go(z_copy(i))
        else:
            out_ref[...] = total
    for i in range(1, zs):
        z_copy(i).wait_recv()
        out_ref[...] = out_ref[...] + bufz[i].astype(F32)
    for copy in started:
        copy.wait_send()


def scatter(n, terms):
    zs, ys = split_axis(n)
    sem = pltpu.SemaphoreType.DMA
    block = terms.shape[3:]
    vmem = pl.BlockSpec(memory_space=pltpu.VMEM)
    return pl.pallas_call(
        functools.partial(scatter_kernel, n, zs, ys),
        out_shape=jax.ShapeDtypeStruct(block, F32),
        in_specs=[vmem],
        out_specs=vmem,
        scratch_shapes=[
            pltpu.VMEM((ys, zs) + block, BF16),
            pltpu.VMEM((zs,) + block, BF16),
            pltpu.VMEM((ys, zs) + block, BF16),
            pltpu.VMEM((ys, zs) + block, BF16),
            pltpu.VMEM((zs,) + block, BF16),
            sem((ys, zs)), sem((ys, zs)), sem((ys, zs)), sem((ys, zs)), sem((zs,)), sem((zs,)),
        ],
        compiler_params=pltpu.CompilerParams(
            collective_id=2, has_side_effects=True, vmem_limit_bytes=48 << 20),
        name="scatter_terms",
    )(terms)


def row_of(count, height):
    return lax.rem(lax.broadcasted_iota(jnp.int32, (count, LANES), 0), height)


def column_of(count, height, first):
    return lax.broadcasted_iota(jnp.int32, (count, LANES), 0) // height + first


def from_above(v, d, height):
    return jnp.where(row_of(v.shape[0], height) >= d, pltpu.roll(v, d, 0), 0.0)


def from_below(v, d, height):
    count = v.shape[0]
    return jnp.where(row_of(count, height) < height - d, pltpu.roll(v, count - d, 0), 0.0)


def spread_rows(ref, v, d, height):
    ref[:, 0:LANES] = from_above(v, d, height).astype(BF16)
    ref[:, LANES : 2 * LANES] = v.astype(BF16)
    ref[:, 2 * LANES : 3 * LANES] = from_below(v, d, height).astype(BF16)


def sigmoid(v):
    return 1.0 / (1.0 + jnp.exp(-v))


def silu_slope(pre):
    sigma = sigmoid(pre)
    return sigma * (1.0 + pre * (1.0 - sigma))


def conv(ref, w_ref, start, step, count):
    total = None
    for kx in range(3):
        term = lax.dot_general(
            ref[pl.ds(start + kx * step, count), :],
            w_ref[:, kx * 3 * LANES : (kx + 1) * 3 * LANES],
            (((1,), (1,)), ((), ())),
            preferred_element_type=F32,
        )
        total = term if total is None else total + term
    return total


def gather_rows(prod, d, height, kx):
    base = kx * 3 * LANES
    up = from_below(prod[:, base : base + LANES], d, height)
    same = prod[:, base + LANES : base + 2 * LANES]
    down = from_above(prod[:, base + 2 * LANES : base + 3 * LANES], d, height)
    return up + same + down


def weight_grad(out_ref, slope_f32, ref, start, step):
    count = slope_f32.shape[0]
    turned = slope_f32.T.astype(BF16)
    for kx in range(3):
        out_ref[:, kx * 3 * LANES : (kx + 1) * 3 * LANES] = jnp.dot(
            turned, ref[pl.ds(start + kx * step, count), :], preferred_element_type=F32
        ).astype(BF16)


def step_kernel(
    n, height, breadth,
    x_ref, xh_ref, t_ref, w1_ref, w2_ref, w3_ref, g1_ref, g2_ref, g3_ref,
    x3x, x3f, x3s, pre1, pre2, acc, send, recv, ssem, rsem,
):
    me = lax.axis_index("cols")
    left, right = lax.rem(me + n - 1, n), lax.rem(me + 1, n)
    greet([{"cols": left}, {"cols": right}])
    h, b = height, breadth
    first_col = me * b
    width = n * b

    def inside(v, first):
        cols = column_of(v.shape[0], h, first_col + first)
        return jnp.where((cols >= 0) & (cols < width), v, 0.0)

    wide_x = jnp.concatenate([xh_ref[0], x_ref[...], xh_ref[1]], axis=0).astype(F32)
    spread_rows(x3x, inside(wide_x, -14), 2, h)
    v = conv(x3x, w1_ref, 0, 2 * h, (b + 24) * h)
    pre1[...] = v
    act = inside(v * sigmoid(v), -12).astype(BF16).astype(F32)
    spread_rows(x3f, act, 4, h)
    v = conv(x3f, w2_ref, 0, 4 * h, (b + 16) * h)
    pre2[...] = v
    act = inside(v * sigmoid(v), -8).astype(BF16).astype(F32)
    spread_rows(x3s, act, 8, h)
    student = conv(x3s, w3_ref, 0, 8 * h, b * h)
    s_norm = jnp.sqrt(jnp.sum(student * student, -1, keepdims=True) + epsilon)
    target = t_ref[...].astype(F32)
    t_norm = jnp.sqrt(jnp.sum(target * target, -1, keepdims=True) + epsilon)
    s_unit = student / s_norm
    differ = s_unit - target / t_norm
    slope = (differ - s_unit * jnp.sum(s_unit * differ, -1, keepdims=True)) / s_norm
    slope_b = slope.astype(BF16)

    prod = jnp.dot(slope_b, w3_ref[...], preferred_element_type=F32)
    u0 = gather_rows(prod, 8, h, 0)
    u1 = gather_rows(prod, 8, h, 1)
    u2 = gather_rows(prod, 8, h, 2)
    e = 8 * h
    m = b * h
    acc[pl.ds(0, m), :] = u0
    acc[pl.ds(m, 2 * e), :] = jnp.zeros((2 * e, LANES), F32)
    acc[pl.ds(e, m), :] += u1
    acc[pl.ds(2 * e, m), :] += u2
    part = 12 * h
    send[0] = acc[pl.ds(m + 2 * e - part, part), :].astype(BF16)
    send[1] = acc[pl.ds(0, part), :].astype(BF16)
    copies = []
    for side, target_id in ((0, right), (1, left)):
        copy = pltpu.make_async_remote_copy(
            send.at[side], recv.at[side], ssem.at[side], rsem.at[side],
            device_id={"cols": target_id}, device_id_type=MESH)
        copy.start()
        copies.append(copy)
    weight_grad(g3_ref, slope, x3s, 0, 8 * h)
    for copy in copies:
        copy.wait()
    inner = (b + 8) * h
    split = inner - part
    from_left = jnp.where(me > 0, recv[0].astype(F32), 0.0)
    from_right = jnp.where(me < n - 1, recv[1].astype(F32), 0.0)
    acc[pl.ds(4 * h, part), :] += from_left
    acc[pl.ds(4 * h + split, part), :] += from_right
    back = acc[pl.ds(4 * h, inner), :]
    slope2 = inside(back * silu_slope(pre2[pl.ds(4 * h, inner), :]), -4).astype(BF16)
    prod = jnp.dot(slope2, w2_ref[...], preferred_element_type=F32)
    back = (
        gather_rows(prod, 4, h, 0)[8 * h : 8 * h + m]
        + gather_rows(prod, 4, h, 1)[4 * h : 4 * h + m]
        + gather_rows(prod, 4, h, 2)[0:m]
    )
    weight_grad(g2_ref, slope2.astype(F32)[4 * h : 4 * h + m], x3f, 8 * h, 4 * h)
    slope1 = back * silu_slope(pre1[pl.ds(12 * h, m), :])
    weight_grad(g1_ref, slope1, x3x, 12 * h, 2 * h)


def local_step(n, height, breadth, x_cells, x_edges, teacher, w1, w2, w3):
    sem = pltpu.SemaphoreType.DMA
    vmem = pl.BlockSpec(memory_space=pltpu.VMEM)
    h, b = height, breadth
    return pl.pallas_call(
        functools.partial(step_kernel, n, h, b),
        out_shape=tuple(jax.ShapeDtypeStruct(w.shape, BF16) for w in (w1, w2, w3)),
        in_specs=[vmem] * 6,
        out_specs=(vmem,) * 3,
        scratch_shapes=[
            pltpu.VMEM(((b + 28) * h, 3 * LANES), BF16),
            pltpu.VMEM(((b + 24) * h, 3 * LANES), BF16),
            pltpu.VMEM(((b + 16) * h, 3 * LANES), BF16),
            pltpu.VMEM(((b + 24) * h, LANES), F32),
            pltpu.VMEM(((b + 16) * h, LANES), F32),
            pltpu.VMEM(((b + 16) * h, LANES), F32),
            pltpu.VMEM((2, 12 * h, LANES), BF16),
            pltpu.VMEM((2, 12 * h, LANES), BF16),
            sem((2,)), sem((2,)),
        ],
        compiler_params=pltpu.CompilerParams(
            collective_id=1, has_side_effects=True, vmem_limit_bytes=56 << 20),
        name="student_step",
    )(x_cells, x_edges, teacher, w1, w2, w3)


def taps_by_column(w):
    rows, depth = w.shape[0], w.shape[1] // 9
    w = w.reshape(rows, 3, 3, depth).transpose(0, 2, 1, 3)
    w = jnp.pad(w, ((0, 0), (0, 0), (0, 0), (0, LANES - depth)))
    return w.reshape(rows, 9 * LANES)


def taps_by_row(g, depth):
    rows = g.shape[0]
    g = g.reshape(rows, 3, 3, LANES)[..., :depth].transpose(0, 2, 1, 3)
    return g.reshape(rows, 9 * depth)


class Line:
    def __init__(self, pos, zs, ys, src, out, first, rows, sems):
        self.pos, self.zs, self.ys = pos, zs, ys
        self.rows = pl.ds(first, rows)
        self.src, self.out = src.at[self.rows], out
        self.szr, self.rzr, self.szl, self.rzl, self.sy, self.ry, self.sc, self.rc = sems

    def copy(self, src, dst, ssem, rsem, device):
        return pltpu.make_async_remote_copy(
            src, dst, ssem, rsem, device_id=device, device_id_type=MESH)

    def block(self, zi, yi, c):
        return self.out.at[zi, yi, c, self.rows]

    def hop(self, way, s):
        z, y, core = self.pos
        zi = z - way * s
        src = self.src if s == 0 else self.block(zi, y, core)
        ss, rs = (self.szr, self.rzr) if way > 0 else (self.szl, self.rzl)
        ok = (zi >= 0) & (zi < self.zs) & (z + way >= 0) & (z + way < self.zs)
        return ok, self.copy(
            src, self.block(zi, y, core), ss.at[s], rs.at[s + 1], at(z + way, y, core, self.ys))

    def arrived(self, way, s):
        z, y, core = self.pos
        zi = z - way * s
        ss, rs = (self.szr, self.rzr) if way > 0 else (self.szl, self.rzl)
        ok = (zi >= 0) & (zi < self.zs)
        return ok, zi, self.copy(
            self.src, self.block(zi, y, core), ss.at[0], rs.at[s], at(z, y, 1 - core, self.ys))

    def to_y(self, j, zi, own):
        z, y, core = self.pos
        src = self.src if own else self.block(zi, y, core)
        return self.copy(src, self.block(zi, y, core), self.sy.at[j, zi], self.ry.at[j, zi],
                         at(z, lax.rem(y + j, self.ys), core, self.ys))

    def from_y(self, j, zi):
        z, y, core = self.pos
        yi = lax.rem(y + self.ys - j, self.ys)
        return self.copy(self.src, self.block(zi, yi, core), self.sy.at[j, zi], self.ry.at[j, zi],
                         at(z, lax.rem(y + j, self.ys), core, self.ys))

    def to_core(self, j, zi, own):
        z, y, core = self.pos
        yi = lax.rem(y + self.ys - j, self.ys)
        src = self.src if own else self.block(zi, yi, core)
        return self.copy(src, self.block(zi, yi, core), self.sc.at[j, zi], self.rc.at[j, zi],
                         at(z, y, 1 - core, self.ys))

    def from_core(self, j, zi):
        z, y, core = self.pos
        yi = lax.rem(y + self.ys - j, self.ys)
        return self.copy(self.src, self.block(zi, yi, 1 - core), self.sc.at[j, zi],
                         self.rc.at[j, zi], at(z, y, 1 - core, self.ys))

    def start(self):
        z, y, core = self.pos
        for way in (1, -1):
            ok, copy = self.hop(way, 0)
            pl.when(ok)(copy.start)
        for j in range(1, self.ys):
            self.to_y(j, z, True).start()
        self.to_core(0, z, True).start()
        self.out[z, y, core, self.rows] = self.src[...]

    def forward_z(self, s):
        for way in (1, -1):
            ok, zi, here = self.arrived(way, s)

            @pl.when(ok)
            def _():
                here.wait_recv()
                for j in range(1, self.ys):
                    self.to_y(j, zi, False).start()

            if s < self.zs - 1:
                more, on = self.hop(way, s)
                pl.when(more)(on.start)

            @pl.when(ok)
            def _():
                self.to_core(0, zi, False).start()

    def forward_y(self, s):
        z = self.pos[0]
        todo = [(None, z)] if s == 0 else [
            ((z - way * s >= 0) & (z - way * s < self.zs), z - way * s) for way in (1, -1)]
        for ok, zi in todo:

            def step(zi=zi):
                for j in range(1, self.ys):
                    self.from_y(j, zi).wait_recv()
                    self.to_core(j, zi, False).start()

            step() if ok is None else pl.when(ok)(step)

    def finish(self):
        for zi in range(self.zs):
            for j in range(self.ys):
                self.from_core(j, zi).wait_recv()

    def drain(self):
        for s in range(self.zs - 1):
            for way in (1, -1):
                ok, copy = self.hop(way, s)
                pl.when(ok)(copy.wait_send)
        for zi in range(self.zs):
            for j in range(self.ys):
                if j:
                    self.to_y(j, zi, False).wait_send()
                self.to_core(j, zi, False).wait_send()


def flip(v, i):
    bit = 1
    while bit <= i:
        if i & bit:
            v = v + bit - 2 * bit * lax.rem(v // bit, 2)
        bit *= 2
    return v


class Star:
    def __init__(self, pos, zs, ys, src, out, sems):
        self.pos, self.zs, self.ys, self.src, self.out = pos, zs, ys, src, out
        self.sz, self.rz, self.sy, self.ry, self.sc, self.rc = sems

    def copy(self, src, dst, ssem, rsem, device):
        return pltpu.make_async_remote_copy(
            src, dst, ssem, rsem, device_id=device, device_id_type=MESH)

    def block(self, i, j, k):
        z, y, core = self.pos
        return self.out.at[flip(z, i), flip(y, j), flip(core, k)]

    def held(self, i, j):
        return self.src if i == 0 and j == 0 else self.block(i, j, 0)

    def z_copy(self, i, arriving):
        z, y, core = self.pos
        return self.copy(self.src, self.block(i if arriving else 0, 0, 0), self.sz.at[i],
                         self.rz.at[i], at(flip(z, i), y, core, self.ys))

    def y_copy(self, j, i, arriving):
        z, y, core = self.pos
        return self.copy(self.held(i, 0), self.block(i, j if arriving else 0, 0), self.sy.at[j, i],
                         self.ry.at[j, i], at(z, flip(y, j), core, self.ys))

    def core_copy(self, j, i, arriving):
        z, y, core = self.pos
        return self.copy(self.held(i, j), self.block(i, j, 1 if arriving else 0), self.sc.at[j, i],
                         self.rc.at[j, i], at(z, y, 1 - core, self.ys))

    def start(self):
        for i in reversed(range(1, self.zs)):
            self.z_copy(i, False).start()
        for j in range(1, self.ys):
            self.y_copy(j, 0, False).start()
        self.core_copy(0, 0, False).start()
        z, y, core = self.pos
        self.out[z, y, core] = self.src[...]

    def forward_z(self, i):
        self.z_copy(i, True).wait_recv()
        for j in range(1, self.ys):
            self.y_copy(j, i, False).start()
        self.core_copy(0, i, False).start()

    def forward_y(self, i):
        for j in range(1, self.ys):
            self.y_copy(j, i, True).wait_recv()
            self.core_copy(j, i, False).start()

    def finish(self):
        for i in range(self.zs):
            for j in range(self.ys):
                self.core_copy(j, i, True).wait_recv()

    def drain(self):
        for i in range(self.zs):
            if i:
                self.z_copy(i, False).wait_send()
            for j in range(self.ys):
                if j:
                    self.y_copy(j, i, False).wait_send()
                self.core_copy(j, i, False).wait_send()


class Pair:
    def __init__(self, me, n, sides):
        self.has_right, self.has_left = me < n - 1, me > 0
        self.copies = [pltpu.make_async_remote_copy(
            src, dst, ssem, rsem, device_id={"cols": peer}, device_id_type=MESH)
            for (src, dst, ssem, rsem), peer in zip(
                sides, (lax.rem(me + 1, n), lax.rem(me + n - 1, n)))]

    def start(self):
        pl.when(self.has_right)(self.copies[0].start)
        pl.when(self.has_left)(self.copies[1].start)

    def wait(self):
        pl.when(self.has_left)(self.copies[0].wait_recv)
        pl.when(self.has_right)(self.copies[1].wait_recv)
        pl.when(self.has_right)(self.copies[0].wait_send)
        pl.when(self.has_left)(self.copies[1].wait_send)


class Sum:
    def __init__(self, pos, zs, ys, terms, bufs, sems):
        self.pos, self.zs, self.ys, self.terms = pos, zs, ys, terms
        self.s1, self.s2, self.bufc, self.bufy, self.bufz = bufs
        self.sc, self.rc, self.sy, self.ry, self.sz, self.rz = sems
        self.zorder = list(range(1, zs)) + [0]
        self.yorder = list(range(1, ys)) + [0]

    def zi(self, i):
        return lax.rem(self.pos[0] + i, self.zs)

    def yi(self, j):
        return lax.rem(self.pos[1] + j, self.ys)

    def copy(self, src, dst, ssem, rsem, device):
        return pltpu.make_async_remote_copy(
            src, dst, ssem, rsem, device_id=device, device_id_type=MESH)

    def core_copy(self, j, i):
        z, y, core = self.pos
        return self.copy(self.terms.at[self.zi(i), self.yi(j), 1 - core], self.bufc.at[j, i],
                         self.sc.at[j, i], self.rc.at[j, i], at(z, y, 1 - core, self.ys))

    def y_copy(self, j, i):
        z, y, core = self.pos
        return self.copy(self.s1.at[j, i], self.bufy.at[j, i], self.sy.at[j, i],
                         self.ry.at[j, i], at(z, self.yi(j), core, self.ys))

    def z_copy(self, i):
        z, y, core = self.pos
        return self.copy(self.s2.at[i], self.bufz.at[i], self.sz.at[i], self.rz.at[i],
                         at(self.zi(i), y, core, self.ys))

    def start(self):
        for j in self.yorder:
            for i in self.zorder:
                self.core_copy(j, i).start()

    def pair(self):
        core = self.pos[2]
        for j in self.yorder:
            for i in self.zorder:
                self.core_copy(j, i).wait_recv()
                both = self.terms[self.zi(i), self.yi(j), core].astype(F32)
                self.s1[j, i] = (both + self.bufc[j, i].astype(F32)).astype(BF16)
                if j:
                    self.y_copy(j, i).start()

    def along_y(self, begin, end):
        for i in self.zorder[begin:end]:
            total = self.s1[0, i].astype(F32)
            for j in range(1, self.ys):
                self.y_copy(j, i).wait_recv()
                total = total + self.bufy[j, i].astype(F32)
            if i:
                self.s2[i] = total.astype(BF16)
                self.z_copy(i).start()
            else:
                self.own = total

    def along_z(self):
        total = self.own
        for i in range(1, self.zs):
            self.z_copy(i).wait_recv()
            total = total + self.bufz[i].astype(F32)
        return total

    def drain_first(self):
        for j in self.yorder:
            for i in self.zorder:
                self.core_copy(j, i).wait_send()
                if j:
                    self.y_copy(j, i).wait_send()

    def drain_last(self):
        for i in range(1, self.zs):
            self.z_copy(i).wait_send()


class Sum2:
    def __init__(self, pos, zs, ys, terms, cut, bufs, sems):
        self.pos, self.zs, self.ys, self.terms = pos, zs, ys, terms
        (self.s1a, self.s1b, self.bufca, self.bufcb, self.bufy, self.s2a, self.bufz, self.bufw,
         self.s2b, self.bufv) = bufs
        (self.sc, self.rc, self.sy, self.ry, self.sz, self.rz, self.sw, self.rw, self.sv, self.rv,
         self.sb, self.rb) = sems
        self.cut, width = cut, terms.shape[-1]
        self.lanes_a, self.lanes_b = pl.ds(0, cut), pl.ds(cut, width - cut)
        self.zorder = list(range(1, zs)) + [0]
        self.yorder = list(range(1, ys)) + [0]

    def zi(self, i):
        return lax.rem(self.pos[0] + i, self.zs)

    def yi(self, j):
        return lax.rem(self.pos[1] + j, self.ys)

    def y_peer(self, j):
        return at(self.pos[0], self.yi(j), self.pos[2], self.ys)

    def z_peer(self, i):
        return at(self.zi(i), self.pos[1], self.pos[2], self.ys)

    def copy(self, src, dst, ssem, rsem, device):
        return pltpu.make_async_remote_copy(
            src, dst, ssem, rsem, device_id=device, device_id_type=MESH)

    def core_copy(self, j, i):
        z, y, core = self.pos
        return self.copy(self.terms.at[self.zi(i), self.yi(j), 1 - core, :, self.lanes_a], self.bufca.at[j, i],
                         self.sc.at[j, i], self.rc.at[j, i], at(z, y, 1 - core, self.ys))

    def core_copy_b(self):
        z, y, core = self.pos
        return self.copy(self.terms.at[:, :, 1 - core, :, self.lanes_b], self.bufcb, self.sb.at[0],
                         self.rb.at[0], at(z, y, 1 - core, self.ys))

    def y_copies(self, j):
        return [self.copy(self.s1a.at[j, i], self.bufy.at[j, i], self.sy.at[j, i],
                          self.ry.at[j, i], self.y_peer(j)) for i in self.zorder]

    def w_copy(self, i):
        return self.copy(self.s1b.at[i], self.bufw.at[i], self.sw.at[i],
                         self.rw.at[i], self.z_peer(i))

    def z_copy(self, i):
        return self.copy(self.s2a.at[i], self.bufz.at[i], self.sz.at[i], self.rz.at[i], self.z_peer(i))

    def v_copy(self, j):
        return self.copy(self.s2b.at[j], self.bufv.at[j], self.sv.at[j], self.rv.at[j], self.y_peer(j))

    def start_b(self):
        self.core_copy_b().start()

    def start_a(self):
        for j in self.yorder:
            for i in self.zorder:
                self.core_copy(j, i).start()

    def pair_b(self):
        core = self.pos[2]
        self.core_copy_b().wait_recv()
        for i in self.zorder:
            for j in range(self.ys):
                both = self.terms[self.zi(i), self.yi(j), core, :, self.lanes_b].astype(F32)
                self.s1b[i, j] = (both + self.bufcb[self.zi(i), self.yi(j)].astype(F32)).astype(BF16)
            if i:
                self.w_copy(i).start()

    def pair_a(self):
        core = self.pos[2]
        for j in self.yorder:
            for i in self.zorder:
                self.core_copy(j, i).wait_recv()
                both = self.terms[self.zi(i), self.yi(j), core, :, self.lanes_a].astype(F32)
                self.s1a[j, i] = (both + self.bufca[j, i].astype(F32)).astype(BF16)
                if j:
                    self.y_copies(j)[self.zorder.index(i)].start()

    def second_b(self):
        for i in self.zorder[:-1]:
            self.w_copy(i).wait_recv()
        for j in self.yorder:
            total = self.s1b[0, j].astype(F32)
            for i in self.zorder[:-1]:
                total = total + self.bufw[i, j].astype(F32)
            if j:
                self.s2b[j] = total.astype(BF16)
                self.v_copy(j).start()
            else:
                self.own_b = total

    def second_a(self, begin, end):
        for i in self.zorder[begin:end]:
            total = self.s1a[0, i].astype(F32)
            for j in range(1, self.ys):
                copies = self.y_copies(j)
                if len(copies) > 1:
                    copies[self.zorder.index(i)].wait_recv()
                elif i == self.zorder[0]:
                    copies[0].wait_recv()
                total = total + self.bufy[j, i].astype(F32)
            if i:
                self.s2a[i] = total.astype(BF16)
                self.z_copy(i).start()
            else:
                self.own_a = total

    def last_b(self):
        total = self.own_b
        for j in range(1, self.ys):
            self.v_copy(j).wait_recv()
            total = total + self.bufv[j].astype(F32)
        return total

    def last_a(self):
        total = self.own_a
        for i in range(1, self.zs):
            self.z_copy(i).wait_recv()
            total = total + self.bufz[i].astype(F32)
        return total

    def drain_first(self):
        self.core_copy_b().wait_send()
        for j in self.yorder:
            for i in self.zorder:
                self.core_copy(j, i).wait_send()
            if j:
                for copy in self.y_copies(j):
                    copy.wait_send()
        for i in range(1, self.zs):
            self.w_copy(i).wait_send()

    def drain_last(self):
        for j in range(1, self.ys):
            self.v_copy(j).wait_send()
        for i in range(1, self.zs):
            self.z_copy(i).wait_send()


def tap(t):
    return slice(t * LANES, (t + 1) * LANES)


def conv_taps(ref, w, start, step, count):
    total = None
    for kx in range(3):
        rhs = jnp.concatenate([w[:, tap(3 * ky + kx)] for ky in range(3)], axis=1)
        term = lax.dot_general(ref[pl.ds(start + kx * step, count), :], rhs,
                               (((1,), (1,)), ((), ())), preferred_element_type=F32)
        total = term if total is None else total + term
    return total


def join_rows(prod, d, height, kx):
    up = from_below(prod[:, tap(kx)], d, height)
    down = from_above(prod[:, tap(6 + kx)], d, height)
    return up + prod[:, tap(3 + kx)] + down


def put_terms(ref, place, value):
    zs, ys = ref.shape[0], ref.shape[1]
    (first, count), t = place
    ref[:, :, :, first : first + count, tap(t)] = value.reshape(zs, ys, 2, count, LANES).astype(BF16)


def grad_taps(ref, places, turned, acts, start, step, kxs=range(3)):
    count = turned.shape[1]
    for kx in kxs:
        prod = jnp.dot(turned, acts[pl.ds(start + kx * step, count), :],
                       preferred_element_type=F32)
        for ky in range(3):
            put_terms(ref, places[3 * ky + kx], prod[:, tap(ky)])


def fused_kernel(
    n, zs, ys, height, breadth, rl, rm, rf,
    x_ref, t_ref, wl_ref, wm_ref, wf_ref, o1_ref, o2_ref, o3_ref,
    xv, tv, wlv, wmv, wfv,
    pa, ga, gb, ta, tb, xh, xs, x9, x3f, x3s, pre1, pre2, acc, send, recv, tf, tn,
    a1, a2, a3, a4, a5, b1, b2, b3, b4, b5, b6, b7, b8, b9, b10, lsem, sx, rx, ssem, rsem, *sems,
):
    me, z, y, core = place(n, zs, ys)
    pos = (z, y, core)
    h, b = height, breadth
    depth = wf_ref.shape[1] // 9
    left, right = lax.rem(me + n - 1, n), lax.rem(me + 1, n)
    loads = [pltpu.make_async_copy(src, dst, lsem.at[i]) for i, (src, dst) in enumerate(
        ((wm_ref, wmv), (wf_ref, wfv), (x_ref, xv), (wl_ref, wlv), (t_ref, tv)))]
    for load in loads:
        load.start()
    peers = (
        [at(flip(z, i), y, core, ys) for i in range(1, zs)]
        + [at(z, flip(y, j), core, ys) for j in range(1, ys)]
        + [at(z, y, 1 - core, ys), {"cols": left}, {"cols": right}]
    )
    call(peers)
    middle = [((0, rm), t) if t < 7 else ((rm, rf), t - 7) for t in range(9)]
    first = [((rm, rf), t + 2) for t in range(5)]
    low = Star(pos, zs, ys, pa, ga, sems[0:6])
    cut = rl // 16 * 8
    parts = ((0, cut), (cut, rl - cut)) if cut else ((0, rl),)
    high = [Line(pos, zs, ys, wlv, gb, begin, rows, sems[8 * i + 6 : 8 * i + 14])
            for i, (begin, rows) in enumerate(parts)]
    sum_a = Sum(pos, zs, ys, ta, (a1, a2, a3, a4, a5), sems[22:28])
    sum_b = Sum2(pos, zs, ys, tb, 6 * LANES, (b1, b2, b3, b4, b5, b6, b7, b8, b9, b10),
                 sems[28:40])
    loads[0].wait()
    loads[1].wait()
    pa[0:rm, :] = wmv[:, 0 : 7 * LANES]
    pa[rm : rm + rf, 0 : 2 * LANES] = wmv[:, 7 * LANES : 9 * LANES]
    pa[rm : rm + rf, 6 * LANES : 7 * LANES] = jnp.zeros((rf, LANES), BF16)
    pa[rm : rm + rf, 2 * LANES : 2 * LANES + 9 * depth] = wfv[...]
    hear(peers)
    low.start()
    loads[2].wait()
    edge = 14 * depth
    halo = Pair(me, n, [(xv.at[:, pl.ds(b * depth - edge, edge)], xh.at[0], sx.at[0], rx.at[0]),
                        (xv.at[:, pl.ds(0, edge)], xh.at[1], sx.at[1], rx.at[1])])
    halo.start()
    loads[3].wait()
    for line in high:
        line.start()

    loads[4].wait()
    target = tv[...].astype(F32)
    t_norm = jnp.sqrt(jnp.sum(target * target, -1, keepdims=True) + epsilon)
    target = target / t_norm
    for q in range(tf.shape[0]):
        tf[q] = target[:, tap(q)]
    for i in reversed(range(1, zs)):
        low.forward_z(i)
    for c in range(b):
        for q in range(tf.shape[0]):
            tn[pl.ds(c * h, h), tap(q)] = tf[q, pl.ds(c, h, stride=b), :]
    for line in high:
        line.forward_z(1)

    first_col = me * b
    width = n * b

    def inside(v, first):
        cols = column_of(v.shape[0], h, first_col + first)
        return jnp.where((cols >= 0) & (cols < width), v, 0.0)

    halo.wait()
    half = lax.broadcasted_iota(jnp.int32, (h, LANES), 1) < depth
    at_col = 0
    for part, pairs in ((xh[0], 7), (xv[...], b // 2), (xh[1], 7)):
        part = part.astype(F32)
        for q in range(pairs):
            both = part[:, tap(q)]
            turned = pltpu.roll(both, depth, 1)
            xs[pl.ds(at_col * h, h), :] = jnp.where(half, both, turned)
            xs[pl.ds((at_col + 1) * h, h), :] = jnp.where(half, turned, both)
            at_col += 2
    for i in [0] + list(reversed(range(1, zs))):
        low.forward_y(i)
    for line in high:
        line.forward_z(2)
    wide_x = inside(xs[...], -14)
    count1 = (b + 24) * h
    rows3 = (from_above(wide_x, 2, h), wide_x, from_below(wide_x, 2, h))

    def piece(t):
        ky, kx = t // 3, t % 3
        return rows3[ky][kx * 2 * h : kx * 2 * h + count1]

    lower = lax.broadcasted_iota(jnp.int32, (count1, LANES), 1) < depth
    for q in range(5):
        odd = piece(2 * q + 1) if q < 4 else 0.0
        x9[:, tap(q)] = jnp.where(lower, piece(2 * q), odd).astype(BF16)
    for s in range(3, zs):
        for line in high:
            line.forward_z(s)
    low.finish()
    w1 = ga[:, :, :, rm : rm + rf, 2 * LANES : 7 * LANES].reshape(n * rf, 5 * LANES)
    v = lax.dot_general(x9[...], w1, (((1,), (1,)), ((), ())), preferred_element_type=F32)
    pre1[...] = v
    act = inside(v * sigmoid(v), -12).astype(BF16).astype(F32)
    spread_rows(x3f, act, 4, h)
    for line in high:
        for s in range(zs - 1):
            line.forward_y(s)
    w2 = jnp.concatenate([
        ga[:, :, :, 0:rm, :].reshape(n * rm, 7 * LANES),
        ga[:, :, :, rm : rm + rf, 0 : 2 * LANES].reshape(n * rm, 2 * LANES)], axis=1)
    v = conv_taps(x3f, w2, 0, 4 * h, (b + 16) * h)
    pre2[...] = v
    act = inside(v * sigmoid(v), -8).astype(BF16).astype(F32)
    spread_rows(x3s, act, 8, h)
    for line in high:
        line.forward_y(zs - 1)
    for line in high:
        line.finish()
    w3 = gb[...].reshape(n * rl, 9 * LANES)
    student = conv_taps(x3s, w3, 0, 8 * h, b * h)
    s_norm = jnp.sqrt(jnp.sum(student * student, -1, keepdims=True) + epsilon)
    s_unit = student / s_norm
    differ = s_unit - tn[...]
    slope = (differ - s_unit * jnp.sum(s_unit * differ, -1, keepdims=True)) / s_norm

    prod = jnp.dot(slope.astype(BF16), w3, preferred_element_type=F32)
    e = 8 * h
    m = b * h
    acc[pl.ds(0, m), :] = join_rows(prod, 8, h, 0)
    acc[pl.ds(m, 2 * e), :] = jnp.zeros((2 * e, LANES), F32)
    acc[pl.ds(e, m), :] += join_rows(prod, 8, h, 1)
    acc[pl.ds(2 * e, m), :] += join_rows(prod, 8, h, 2)
    part = 12 * h
    send[0] = acc[pl.ds(m + 2 * e - part, part), :].astype(BF16)
    send[1] = acc[pl.ds(0, part), :].astype(BF16)
    copies = Pair(me, n, [(send.at[side], recv.at[side], ssem.at[side], rsem.at[side])
                          for side in range(2)])
    copies.start()
    turned = slope.T.astype(BF16)
    last = [((0, rl), 3 * (t % 3) + t // 3) for t in range(9)]
    grad_taps(tb, last, turned, x3s, 0, 8 * h, (2,))
    sum_b.start_b()
    grad_taps(tb, last, turned, x3s, 0, 8 * h, (0, 1))
    sum_b.start_a()
    sum_b.pair_b()
    sum_b.pair_a()
    for line in (low, *high):
        line.drain()
    copies.wait()
    inner = (b + 8) * h
    split = inner - part
    from_left = jnp.where(me > 0, recv[0].astype(F32), 0.0)
    from_right = jnp.where(me < n - 1, recv[1].astype(F32), 0.0)
    acc[pl.ds(4 * h, part), :] += from_left
    acc[pl.ds(4 * h + split, part), :] += from_right
    back = acc[pl.ds(4 * h, inner), :]
    slope2 = inside(back * silu_slope(pre2[pl.ds(4 * h, inner), :]), -4).astype(BF16)
    prod = jnp.dot(slope2, w2, preferred_element_type=F32)
    back = (
        join_rows(prod, 4, h, 0)[8 * h : 8 * h + m]
        + join_rows(prod, 4, h, 1)[4 * h : 4 * h + m]
        + join_rows(prod, 4, h, 2)[0:m]
    )
    grad_taps(ta, middle, slope2.astype(F32)[4 * h : 4 * h + m].T.astype(BF16), x3f, 8 * h, 4 * h)
    slope1 = back * silu_slope(pre1[pl.ds(12 * h, m), :])
    prod = jnp.dot(slope1.T.astype(BF16), x9[pl.ds(12 * h, m), :], preferred_element_type=F32)
    for q in range(5):
        put_terms(ta, first[q], prod[:, tap(q)])
    sum_a.start()
    sum_b.second_a(0, 1)
    sum_a.pair()
    sum_b.second_a(1, 2)
    sum_b.second_b()
    sum_b.second_a(2, zs)
    sum_a.along_y(0, zs)
    sum_b.drain_first()
    sum_a.drain_first()
    for kxs, total in (((0, 1), sum_b.last_a()), ((2,), sum_b.last_b())):
        for i, kx in enumerate(kxs):
            for ky in range(3):
                o3_ref[:, tap(3 * ky + kx)] = total[:, tap(3 * i + ky)]
    total = sum_a.along_z()
    o2_ref[:, 0 : 7 * LANES] = total[0:rm]
    o2_ref[:, 7 * LANES : 9 * LANES] = total[rm : rm + rf, 0 : 2 * LANES]
    o1_ref[...] = total[rm : rm + rf, 2 * LANES : 2 * LANES + 9 * depth]
    sum_a.drain_last()
    sum_b.drain_last()


def hand_over_kernel(a_ref, b_ref, c_ref, x_ref, y_ref, z_ref):
    x_ref[...] = a_ref[...]
    y_ref[...] = b_ref[...]
    z_ref[...] = c_ref[...]


def hand_over(arrays):
    vmem = pl.BlockSpec(memory_space=pltpu.VMEM)
    return pl.pallas_call(
        hand_over_kernel,
        out_shape=tuple(jax.ShapeDtypeStruct(a.shape, a.dtype) for a in arrays),
        in_specs=[vmem] * 3,
        out_specs=(vmem,) * 3,
        name="hand_over",
    )(*(pltpu.with_memory_space_constraint(a, pltpu.VMEM) for a in arrays))


def fused(n, height, breadth, x, t, wl, wm, wf):
    zs, ys = split_axis(n)
    sem = pltpu.SemaphoreType.DMA
    vmem = pl.BlockSpec(memory_space=pltpu.VMEM)
    h, b = height, breadth
    rl, rm, rf = wl.shape[0], wm.shape[0], wf.shape[0]
    wide = wl.shape[1]
    low, high = (rm + rf, 7 * LANES), (rl, wide)
    channels = t.shape[1]

    def sum_bufs(block):
        return [
            pltpu.VMEM((ys, zs) + block, BF16), pltpu.VMEM((zs,) + block, BF16),
            pltpu.VMEM((ys, zs) + block, BF16), pltpu.VMEM((ys, zs) + block, BF16),
            pltpu.VMEM((zs,) + block, BF16),
        ]

    def sum2_bufs(block, cut):
        rows, width = block
        part_a, part_b = (rows, cut), (rows, width - cut)
        return [
            pltpu.VMEM((ys, zs) + part_a, BF16), pltpu.VMEM((zs, ys) + part_b, BF16),
            pltpu.VMEM((ys, zs) + part_a, BF16), pltpu.VMEM((zs, ys) + part_b, BF16),
            pltpu.VMEM((ys, zs) + part_a, BF16), pltpu.VMEM((zs,) + part_a, BF16),
            pltpu.VMEM((zs,) + part_a, BF16), pltpu.VMEM((zs, ys) + part_b, BF16),
            pltpu.VMEM((ys,) + part_b, BF16), pltpu.VMEM((ys,) + part_b, BF16),
        ]

    star_sems = [sem((zs,))] * 2 + [sem((ys, zs))] * 4
    line_sems = [sem((zs,))] * 4 + [sem((ys, zs))] * 4
    sum_sems = [sem((ys, zs))] * 4 + [sem((zs,))] * 2
    sum2_sems = [sem((ys, zs))] * 4 + [sem((zs,))] * 4 + [sem((ys,))] * 2 + [sem((1,))] * 2
    return pl.pallas_call(
        functools.partial(fused_kernel, n, zs, ys, h, b, rl, rm, rf),
        out_shape=tuple(pltpu.VMEM(w.shape, F32) for w in (wf, wm, wl)),
        in_specs=[pl.BlockSpec(memory_space=pltpu.HBM)] * 5,
        out_specs=(vmem,) * 3,
        scratch_shapes=[pltpu.VMEM(w.shape, BF16) for w in (x, t, wl, wm, wf)] + [
            pltpu.VMEM(low, BF16),
            pltpu.VMEM((zs, ys, 2) + low, BF16),
            pltpu.VMEM((zs, ys, 2) + high, BF16),
            pltpu.VMEM((zs, ys, 2) + low, BF16),
            pltpu.VMEM((zs, ys, 2) + high, BF16),
            pltpu.VMEM((2, h, 14 * wf.shape[1] // 9), BF16),
            pltpu.VMEM(((b + 28) * h, LANES), F32),
            pltpu.VMEM(((b + 24) * h, 5 * LANES), BF16),
            pltpu.VMEM(((b + 24) * h, 3 * LANES), BF16),
            pltpu.VMEM(((b + 16) * h, 3 * LANES), BF16),
            pltpu.VMEM(((b + 24) * h, LANES), F32),
            pltpu.VMEM(((b + 16) * h, LANES), F32),
            pltpu.VMEM(((b + 16) * h, LANES), F32),
            pltpu.VMEM((2, 12 * h, LANES), BF16),
            pltpu.VMEM((2, 12 * h, LANES), BF16),
            pltpu.VMEM((channels // LANES, b * h, LANES), F32),
            pltpu.VMEM((b * h, channels), F32),
        ]
        + sum_bufs(low) + sum2_bufs(high, 6 * LANES)
        + [sem((5,))] + [sem((2,))] * 4 + star_sems + line_sems * 2 + sum_sems + sum2_sems,
        compiler_params=pltpu.CompilerParams(
            collective_id=3, has_side_effects=True, vmem_limit_bytes=56 << 20),
        name="fused_step",
    )(x, t, wl, wm, wf)


def on_device(n, image_feats, teacher, w_first, w_middle, w_last):
    height, breadth, channels = teacher.shape
    in_depth = w_first.shape[1] // 9
    rl, rm, rf = w_last.shape[0], w_middle.shape[0], w_first.shape[0]
    if (split_axis(n)[0] > 2 and n & (n - 1) == 0 and rm == rf and all(r % 8 == 0 for r in (rl, rm, rf))
            and breadth % 8 == 0 and 2 * in_depth == LANES):
        return hand_over(fused(n, height, breadth, image_feats,
                               teacher.reshape(height * breadth, channels), w_last, w_middle, w_first))
    packed = jnp.concatenate([taps_by_column(w) for w in (w_last, w_middle, w_first)], axis=0)
    x = image_feats.reshape(height, breadth, in_depth).transpose(1, 0, 2)
    x = jnp.pad(x, ((0, 0), (0, 0), (0, LANES - in_depth)))
    x_cells = x.reshape(breadth * height, LANES)
    t_cells = teacher.transpose(1, 0, 2).reshape(breadth * height, channels)
    gathered, x_edges = gather(n, packed, x_cells, 14 * height)
    g = gathered.reshape((n,) + packed.shape)
    w3 = g[:, :rl].reshape(n * rl, -1)
    w2 = g[:, rl : rl + rm].reshape(n * rm, -1)
    w1 = g[:, rl + rm :].reshape(n * rf, -1)
    g1, g2, g3 = local_step(n, height, breadth, x_cells, x_edges, t_cells, w1, w2, w3)
    terms = jnp.concatenate(
        [g3.reshape(n, rl, -1), g2.reshape(n, rm, -1), g1.reshape(n, rf, -1)], axis=1)
    out = scatter(n, terms.reshape(gathered.shape))
    return (
        taps_by_row(out[rl + rm :], in_depth),
        taps_by_row(out[rl : rl + rm], LANES),
        taps_by_row(out[:rl], LANES),
    )


def solution(mesh):
    placed = (
        P("groups", "cols"),
        P("groups", "cols", None),
        P("cols", None),
        P("cols", None),
        P("cols", None),
    )
    return jax.shard_map(
        functools.partial(on_device, mesh.shape["cols"]),
        mesh=mesh,
        in_specs=placed,
        out_specs=(P(("groups", "cols"), None),) * 3,
        check_vma=False,
    )
```

```python
import functools

import jax
import jax.numpy as jnp
from jax import lax
from jax.experimental import pallas as pl
from jax.experimental.pallas import tpu as pltpu
from jax.sharding import PartitionSpec as P

epsilon = 1e-06
MESH = pl.DeviceIdType.MESH
LANES = 128
F32 = jnp.float32
BF16 = jnp.bfloat16


def split_axis(n):
    half = n // 2
    y = 1
    while 4 * y * y <= half:
        y *= 2
    return half // y, y


def place(n, z_size, y_size):
    me = lax.axis_index("cols")
    core = lax.rem(me, 2)
    y = lax.rem(me // 2, y_size)
    z = me // (2 * y_size)
    return me, z, y, core


def at(z, y, core, y_size):
    return {"cols": (z * y_size + y) * 2 + core}


def call(peers):
    barrier = pltpu.get_barrier_semaphore()
    for peer in peers:
        pl.semaphore_signal(barrier, inc=1, device_id=peer, device_id_type=MESH)


def hear(peers):
    pl.semaphore_wait(pltpu.get_barrier_semaphore(), len(peers))


def greet(peers):
    call(peers)
    hear(peers)


def gather_kernel(n, zs, ys, edge, p_ref, x_ref, g_ref, xh_ref, sz, rz, sy, ry, sc, rc, sx, rx):
    me, z, y, core = place(n, zs, ys)
    other = 1 - core
    zmod = [lax.rem(z + i, zs) for i in range(zs)]
    zback = [lax.rem(z + zs - i, zs) for i in range(zs)]
    ymod = [lax.rem(y + i, ys) for i in range(ys)]
    yback = [lax.rem(y + ys - i, ys) for i in range(ys)]
    left, right = lax.rem(me + n - 1, n), lax.rem(me + 1, n)
    greet(
        [at(zmod[i], y, core, ys) for i in range(1, zs)]
        + [at(z, ymod[j], core, ys) for j in range(1, ys)]
        + [at(z, y, other, ys), {"cols": left}, {"cols": right}]
    )

    def block(zi, yi, c):
        return g_ref.at[zi, yi, c]

    def to_z(i):
        return pltpu.make_async_remote_copy(
            p_ref, block(z, y, core), sz.at[i], rz.at[i],
            device_id=at(zmod[i], y, core, ys), device_id_type=MESH)

    def from_z(i):
        return pltpu.make_async_remote_copy(
            p_ref, block(zback[i], y, core), sz.at[i], rz.at[i],
            device_id=at(zmod[i], y, core, ys), device_id_type=MESH)

    def to_y(j, i):
        src = p_ref if i == 0 else block(zback[i], y, core)
        return pltpu.make_async_remote_copy(
            src, block(zback[i], y, core), sy.at[j, i], ry.at[j, i],
            device_id=at(z, ymod[j], core, ys), device_id_type=MESH)

    def from_y(j, i):
        return pltpu.make_async_remote_copy(
            p_ref, block(zback[i], yback[j], core), sy.at[j, i], ry.at[j, i],
            device_id=at(z, ymod[j], core, ys), device_id_type=MESH)

    def to_core(j, i):
        src = p_ref if i == 0 and j == 0 else block(zback[i], yback[j], core)
        return pltpu.make_async_remote_copy(
            src, block(zback[i], yback[j], core), sc.at[j, i], rc.at[j, i],
            device_id=at(z, y, other, ys), device_id_type=MESH)

    def from_core(j, i):
        return pltpu.make_async_remote_copy(
            p_ref, block(zback[i], yback[j], other), sc.at[j, i], rc.at[j, i],
            device_id=at(z, y, other, ys), device_id_type=MESH)

    cells = x_ref.shape[0]
    to_right = pltpu.make_async_remote_copy(
        x_ref.at[pl.ds(cells - edge, edge)], xh_ref.at[0], sx.at[0], rx.at[0],
        device_id={"cols": right}, device_id_type=MESH)
    to_left = pltpu.make_async_remote_copy(
        x_ref.at[pl.ds(0, edge)], xh_ref.at[1], sx.at[1], rx.at[1],
        device_id={"cols": left}, device_id_type=MESH)
    started = []

    def go(copy):
        copy.start()
        started.append(copy)

    for i in range(1, zs):
        go(to_z(i))
    for j in range(1, ys):
        go(to_y(j, 0))
    go(to_right)
    go(to_left)
    go(to_core(0, 0))
    g_ref[z, y, core] = p_ref[...]
    for i in range(1, zs):
        from_z(i).wait_recv()
        for j in range(1, ys):
            go(to_y(j, i))
        go(to_core(0, i))
    for i in range(zs):
        for j in range(1, ys):
            from_y(j, i).wait_recv()
            go(to_core(j, i))
    to_right.wait_recv()
    to_left.wait_recv()
    for i in range(zs):
        for j in range(ys):
            from_core(j, i).wait_recv()
    for copy in started:
        copy.wait_send()


def gather(n, packed, x_cells, edge):
    zs, ys = split_axis(n)
    sem = pltpu.SemaphoreType.DMA
    vmem = pl.BlockSpec(memory_space=pltpu.VMEM)
    return pl.pallas_call(
        functools.partial(gather_kernel, n, zs, ys, edge),
        out_shape=(
            jax.ShapeDtypeStruct((zs, ys, 2) + packed.shape, BF16),
            jax.ShapeDtypeStruct((2, edge, x_cells.shape[1]), BF16),
        ),
        in_specs=[vmem, vmem],
        out_specs=(vmem, vmem),
        scratch_shapes=[
            sem((zs,)), sem((zs,)), sem((ys, zs)), sem((ys, zs)), sem((ys, zs)), sem((ys, zs)),
            sem((2,)), sem((2,)),
        ],
        compiler_params=pltpu.CompilerParams(
            collective_id=0, has_side_effects=True, vmem_limit_bytes=48 << 20),
        name="gather_weights",
    )(packed, x_cells)


def scatter_kernel(n, zs, ys, t_ref, out_ref, s1, s2, bufc, bufy, bufz, sc, rc, sy, ry, sz, rz):
    me, z, y, core = place(n, zs, ys)
    other = 1 - core
    zmod = [lax.rem(z + i, zs) for i in range(zs)]
    ymod = [lax.rem(y + i, ys) for i in range(ys)]
    greet(
        [at(zmod[i], y, core, ys) for i in range(1, zs)]
        + [at(z, ymod[j], core, ys) for j in range(1, ys)]
        + [at(z, y, other, ys)]
    )
    zorder = list(range(1, zs)) + [0]
    yorder = list(range(1, ys)) + [0]

    def core_copy(j, i):
        return pltpu.make_async_remote_copy(
            t_ref.at[zmod[i], ymod[j], other], bufc.at[j, i], sc.at[j, i], rc.at[j, i],
            device_id=at(z, y, other, ys), device_id_type=MESH)

    def y_copy(j, i):
        return pltpu.make_async_remote_copy(
            s1.at[j, i], bufy.at[j, i], sy.at[j, i], ry.at[j, i],
            device_id=at(z, ymod[j], core, ys), device_id_type=MESH)

    def z_copy(i):
        return pltpu.make_async_remote_copy(
            s2.at[i], bufz.at[i], sz.at[i], rz.at[i],
            device_id=at(zmod[i], y, core, ys), device_id_type=MESH)

    started = []

    def go(copy):
        copy.start()
        started.append(copy)

    for j in yorder:
        for i in zorder:
            go(core_copy(j, i))
    for j in yorder:
        for i in zorder:
            core_copy(j, i).wait_recv()
            both = t_ref[zmod[i], ymod[j], core].astype(F32) + bufc[j, i].astype(F32)
            s1[j, i] = both.astype(BF16)
            if j:
                go(y_copy(j, i))
    for i in zorder:
        total = s1[0, i].astype(F32)
        for j in range(1, ys):
            y_copy(j, i).wait_recv()
            total = total + bufy[j, i].astype(F32)
        if i:
            s2[i] = total.astype(BF16)
            go(z_copy(i))
        else:
            out_ref[...] = total
    for i in range(1, zs):
        z_copy(i).wait_recv()
        out_ref[...] = out_ref[...] + bufz[i].astype(F32)
    for copy in started:
        copy.wait_send()


def scatter(n, terms):
    zs, ys = split_axis(n)
    sem = pltpu.SemaphoreType.DMA
    block = terms.shape[3:]
    vmem = pl.BlockSpec(memory_space=pltpu.VMEM)
    return pl.pallas_call(
        functools.partial(scatter_kernel, n, zs, ys),
        out_shape=jax.ShapeDtypeStruct(block, F32),
        in_specs=[vmem],
        out_specs=vmem,
        scratch_shapes=[
            pltpu.VMEM((ys, zs) + block, BF16),
            pltpu.VMEM((zs,) + block, BF16),
            pltpu.VMEM((ys, zs) + block, BF16),
            pltpu.VMEM((ys, zs) + block, BF16),
            pltpu.VMEM((zs,) + block, BF16),
            sem((ys, zs)), sem((ys, zs)), sem((ys, zs)), sem((ys, zs)), sem((zs,)), sem((zs,)),
        ],
        compiler_params=pltpu.CompilerParams(
            collective_id=2, has_side_effects=True, vmem_limit_bytes=48 << 20),
        name="scatter_terms",
    )(terms)


def row_of(count, height):
    return lax.rem(lax.broadcasted_iota(jnp.int32, (count, LANES), 0), height)


def column_of(count, height, first):
    return lax.broadcasted_iota(jnp.int32, (count, LANES), 0) // height + first


def from_above(v, d, height):
    return jnp.where(row_of(v.shape[0], height) >= d, pltpu.roll(v, d, 0), 0.0)


def from_below(v, d, height):
    count = v.shape[0]
    return jnp.where(row_of(count, height) < height - d, pltpu.roll(v, count - d, 0), 0.0)


def spread_rows(ref, v, d, height):
    ref[:, 0:LANES] = from_above(v, d, height).astype(BF16)
    ref[:, LANES : 2 * LANES] = v.astype(BF16)
    ref[:, 2 * LANES : 3 * LANES] = from_below(v, d, height).astype(BF16)


def sigmoid(v):
    return 1.0 / (1.0 + jnp.exp(-v))


def silu_slope(pre):
    sigma = sigmoid(pre)
    return sigma * (1.0 + pre * (1.0 - sigma))


def conv(ref, w_ref, start, step, count):
    total = None
    for kx in range(3):
        term = lax.dot_general(
            ref[pl.ds(start + kx * step, count), :],
            w_ref[:, kx * 3 * LANES : (kx + 1) * 3 * LANES],
            (((1,), (1,)), ((), ())),
            preferred_element_type=F32,
        )
        total = term if total is None else total + term
    return total


def gather_rows(prod, d, height, kx):
    base = kx * 3 * LANES
    up = from_below(prod[:, base : base + LANES], d, height)
    same = prod[:, base + LANES : base + 2 * LANES]
    down = from_above(prod[:, base + 2 * LANES : base + 3 * LANES], d, height)
    return up + same + down


def weight_grad(out_ref, slope_f32, ref, start, step):
    count = slope_f32.shape[0]
    turned = slope_f32.T.astype(BF16)
    for kx in range(3):
        out_ref[:, kx * 3 * LANES : (kx + 1) * 3 * LANES] = jnp.dot(
            turned, ref[pl.ds(start + kx * step, count), :], preferred_element_type=F32
        ).astype(BF16)


def step_kernel(
    n, height, breadth,
    x_ref, xh_ref, t_ref, w1_ref, w2_ref, w3_ref, g1_ref, g2_ref, g3_ref,
    x3x, x3f, x3s, pre1, pre2, acc, send, recv, ssem, rsem,
):
    me = lax.axis_index("cols")
    left, right = lax.rem(me + n - 1, n), lax.rem(me + 1, n)
    greet([{"cols": left}, {"cols": right}])
    h, b = height, breadth
    first_col = me * b
    width = n * b

    def inside(v, first):
        cols = column_of(v.shape[0], h, first_col + first)
        return jnp.where((cols >= 0) & (cols < width), v, 0.0)

    wide_x = jnp.concatenate([xh_ref[0], x_ref[...], xh_ref[1]], axis=0).astype(F32)
    spread_rows(x3x, inside(wide_x, -14), 2, h)
    v = conv(x3x, w1_ref, 0, 2 * h, (b + 24) * h)
    pre1[...] = v
    act = inside(v * sigmoid(v), -12).astype(BF16).astype(F32)
    spread_rows(x3f, act, 4, h)
    v = conv(x3f, w2_ref, 0, 4 * h, (b + 16) * h)
    pre2[...] = v
    act = inside(v * sigmoid(v), -8).astype(BF16).astype(F32)
    spread_rows(x3s, act, 8, h)
    student = conv(x3s, w3_ref, 0, 8 * h, b * h)
    s_norm = jnp.sqrt(jnp.sum(student * student, -1, keepdims=True) + epsilon)
    target = t_ref[...].astype(F32)
    t_norm = jnp.sqrt(jnp.sum(target * target, -1, keepdims=True) + epsilon)
    s_unit = student / s_norm
    differ = s_unit - target / t_norm
    slope = (differ - s_unit * jnp.sum(s_unit * differ, -1, keepdims=True)) / s_norm
    slope_b = slope.astype(BF16)

    prod = jnp.dot(slope_b, w3_ref[...], preferred_element_type=F32)
    u0 = gather_rows(prod, 8, h, 0)
    u1 = gather_rows(prod, 8, h, 1)
    u2 = gather_rows(prod, 8, h, 2)
    e = 8 * h
    m = b * h
    acc[pl.ds(0, m), :] = u0
    acc[pl.ds(m, 2 * e), :] = jnp.zeros((2 * e, LANES), F32)
    acc[pl.ds(e, m), :] += u1
    acc[pl.ds(2 * e, m), :] += u2
    part = 12 * h
    send[0] = acc[pl.ds(m + 2 * e - part, part), :].astype(BF16)
    send[1] = acc[pl.ds(0, part), :].astype(BF16)
    copies = []
    for side, target_id in ((0, right), (1, left)):
        copy = pltpu.make_async_remote_copy(
            send.at[side], recv.at[side], ssem.at[side], rsem.at[side],
            device_id={"cols": target_id}, device_id_type=MESH)
        copy.start()
        copies.append(copy)
    weight_grad(g3_ref, slope, x3s, 0, 8 * h)
    for copy in copies:
        copy.wait()
    inner = (b + 8) * h
    split = inner - part
    from_left = jnp.where(me > 0, recv[0].astype(F32), 0.0)
    from_right = jnp.where(me < n - 1, recv[1].astype(F32), 0.0)
    acc[pl.ds(4 * h, part), :] += from_left
    acc[pl.ds(4 * h + split, part), :] += from_right
    back = acc[pl.ds(4 * h, inner), :]
    slope2 = inside(back * silu_slope(pre2[pl.ds(4 * h, inner), :]), -4).astype(BF16)
    prod = jnp.dot(slope2, w2_ref[...], preferred_element_type=F32)
    back = (
        gather_rows(prod, 4, h, 0)[8 * h : 8 * h + m]
        + gather_rows(prod, 4, h, 1)[4 * h : 4 * h + m]
        + gather_rows(prod, 4, h, 2)[0:m]
    )
    weight_grad(g2_ref, slope2.astype(F32)[4 * h : 4 * h + m], x3f, 8 * h, 4 * h)
    slope1 = back * silu_slope(pre1[pl.ds(12 * h, m), :])
    weight_grad(g1_ref, slope1, x3x, 12 * h, 2 * h)


def local_step(n, height, breadth, x_cells, x_edges, teacher, w1, w2, w3):
    sem = pltpu.SemaphoreType.DMA
    vmem = pl.BlockSpec(memory_space=pltpu.VMEM)
    h, b = height, breadth
    return pl.pallas_call(
        functools.partial(step_kernel, n, h, b),
        out_shape=tuple(jax.ShapeDtypeStruct(w.shape, BF16) for w in (w1, w2, w3)),
        in_specs=[vmem] * 6,
        out_specs=(vmem,) * 3,
        scratch_shapes=[
            pltpu.VMEM(((b + 28) * h, 3 * LANES), BF16),
            pltpu.VMEM(((b + 24) * h, 3 * LANES), BF16),
            pltpu.VMEM(((b + 16) * h, 3 * LANES), BF16),
            pltpu.VMEM(((b + 24) * h, LANES), F32),
            pltpu.VMEM(((b + 16) * h, LANES), F32),
            pltpu.VMEM(((b + 16) * h, LANES), F32),
            pltpu.VMEM((2, 12 * h, LANES), BF16),
            pltpu.VMEM((2, 12 * h, LANES), BF16),
            sem((2,)), sem((2,)),
        ],
        compiler_params=pltpu.CompilerParams(
            collective_id=1, has_side_effects=True, vmem_limit_bytes=56 << 20),
        name="student_step",
    )(x_cells, x_edges, teacher, w1, w2, w3)


def taps_by_column(w):
    rows, depth = w.shape[0], w.shape[1] // 9
    w = w.reshape(rows, 3, 3, depth).transpose(0, 2, 1, 3)
    w = jnp.pad(w, ((0, 0), (0, 0), (0, 0), (0, LANES - depth)))
    return w.reshape(rows, 9 * LANES)


def taps_by_row(g, depth):
    rows = g.shape[0]
    g = g.reshape(rows, 3, 3, LANES)[..., :depth].transpose(0, 2, 1, 3)
    return g.reshape(rows, 9 * depth)


class Line:
    def __init__(self, pos, zs, ys, src, out, first, rows, sems):
        self.pos, self.zs, self.ys = pos, zs, ys
        self.rows = pl.ds(first, rows)
        self.src, self.out = src.at[self.rows], out
        self.szr, self.rzr, self.szl, self.rzl, self.sy, self.ry, self.sc, self.rc = sems

    def copy(self, src, dst, ssem, rsem, device):
        return pltpu.make_async_remote_copy(
            src, dst, ssem, rsem, device_id=device, device_id_type=MESH)

    def block(self, zi, yi, c):
        return self.out.at[zi, yi, c, self.rows]

    def hop(self, way, s):
        z, y, core = self.pos
        zi = z - way * s
        src = self.src if s == 0 else self.block(zi, y, core)
        ss, rs = (self.szr, self.rzr) if way > 0 else (self.szl, self.rzl)
        ok = (zi >= 0) & (zi < self.zs) & (z + way >= 0) & (z + way < self.zs)
        return ok, self.copy(
            src, self.block(zi, y, core), ss.at[s], rs.at[s + 1], at(z + way, y, core, self.ys))

    def arrived(self, way, s):
        z, y, core = self.pos
        zi = z - way * s
        ss, rs = (self.szr, self.rzr) if way > 0 else (self.szl, self.rzl)
        ok = (zi >= 0) & (zi < self.zs)
        return ok, zi, self.copy(
            self.src, self.block(zi, y, core), ss.at[0], rs.at[s], at(z, y, 1 - core, self.ys))

    def to_y(self, j, zi, own):
        z, y, core = self.pos
        src = self.src if own else self.block(zi, y, core)
        return self.copy(src, self.block(zi, y, core), self.sy.at[j, zi], self.ry.at[j, zi],
                         at(z, lax.rem(y + j, self.ys), core, self.ys))

    def from_y(self, j, zi):
        z, y, core = self.pos
        yi = lax.rem(y + self.ys - j, self.ys)
        return self.copy(self.src, self.block(zi, yi, core), self.sy.at[j, zi], self.ry.at[j, zi],
                         at(z, lax.rem(y + j, self.ys), core, self.ys))

    def to_core(self, j, zi, own):
        z, y, core = self.pos
        yi = lax.rem(y + self.ys - j, self.ys)
        src = self.src if own else self.block(zi, yi, core)
        return self.copy(src, self.block(zi, yi, core), self.sc.at[j, zi], self.rc.at[j, zi],
                         at(z, y, 1 - core, self.ys))

    def from_core(self, j, zi):
        z, y, core = self.pos
        yi = lax.rem(y + self.ys - j, self.ys)
        return self.copy(self.src, self.block(zi, yi, 1 - core), self.sc.at[j, zi],
                         self.rc.at[j, zi], at(z, y, 1 - core, self.ys))

    def start(self):
        z, y, core = self.pos
        for way in (1, -1):
            ok, copy = self.hop(way, 0)
            pl.when(ok)(copy.start)
        for j in range(1, self.ys):
            self.to_y(j, z, True).start()
        self.to_core(0, z, True).start()
        self.out[z, y, core, self.rows] = self.src[...]

    def forward_z(self, s):
        for way in (1, -1):
            ok, zi, here = self.arrived(way, s)

            @pl.when(ok)
            def _():
                here.wait_recv()
                for j in range(1, self.ys):
                    self.to_y(j, zi, False).start()

            if s < self.zs - 1:
                more, on = self.hop(way, s)
                pl.when(more)(on.start)

            @pl.when(ok)
            def _():
                self.to_core(0, zi, False).start()

    def forward_y(self, s):
        z = self.pos[0]
        todo = [(None, z)] if s == 0 else [
            ((z - way * s >= 0) & (z - way * s < self.zs), z - way * s) for way in (1, -1)]
        for ok, zi in todo:

            def step(zi=zi):
                for j in range(1, self.ys):
                    self.from_y(j, zi).wait_recv()
                    self.to_core(j, zi, False).start()

            step() if ok is None else pl.when(ok)(step)

    def finish(self):
        for zi in range(self.zs):
            for j in range(self.ys):
                self.from_core(j, zi).wait_recv()

    def drain(self):
        for s in range(self.zs - 1):
            for way in (1, -1):
                ok, copy = self.hop(way, s)
                pl.when(ok)(copy.wait_send)
        for zi in range(self.zs):
            for j in range(self.ys):
                if j:
                    self.to_y(j, zi, False).wait_send()
                self.to_core(j, zi, False).wait_send()


def flip(v, i):
    bit = 1
    while bit <= i:
        if i & bit:
            v = v + bit - 2 * bit * lax.rem(v // bit, 2)
        bit *= 2
    return v


class Star:
    def __init__(self, pos, zs, ys, src, out, sems):
        self.pos, self.zs, self.ys, self.src, self.out = pos, zs, ys, src, out
        self.sz, self.rz, self.sy, self.ry, self.sc, self.rc = sems

    def copy(self, src, dst, ssem, rsem, device):
        return pltpu.make_async_remote_copy(
            src, dst, ssem, rsem, device_id=device, device_id_type=MESH)

    def block(self, i, j, k):
        z, y, core = self.pos
        return self.out.at[flip(z, i), flip(y, j), flip(core, k)]

    def held(self, i, j):
        return self.src if i == 0 and j == 0 else self.block(i, j, 0)

    def z_copy(self, i, arriving):
        z, y, core = self.pos
        return self.copy(self.src, self.block(i if arriving else 0, 0, 0), self.sz.at[i],
                         self.rz.at[i], at(flip(z, i), y, core, self.ys))

    def y_copy(self, j, i, arriving):
        z, y, core = self.pos
        return self.copy(self.held(i, 0), self.block(i, j if arriving else 0, 0), self.sy.at[j, i],
                         self.ry.at[j, i], at(z, flip(y, j), core, self.ys))

    def core_copy(self, j, i, arriving):
        z, y, core = self.pos
        return self.copy(self.held(i, j), self.block(i, j, 1 if arriving else 0), self.sc.at[j, i],
                         self.rc.at[j, i], at(z, y, 1 - core, self.ys))

    def start(self):
        for i in reversed(range(1, self.zs)):
            self.z_copy(i, False).start()
        for j in range(1, self.ys):
            self.y_copy(j, 0, False).start()
        self.core_copy(0, 0, False).start()
        z, y, core = self.pos
        self.out[z, y, core] = self.src[...]

    def forward_z(self, i):
        self.z_copy(i, True).wait_recv()
        for j in range(1, self.ys):
            self.y_copy(j, i, False).start()
        self.core_copy(0, i, False).start()

    def forward_y(self, i):
        for j in range(1, self.ys):
            self.y_copy(j, i, True).wait_recv()
            self.core_copy(j, i, False).start()

    def finish(self):
        for i in range(self.zs):
            for j in range(self.ys):
                self.core_copy(j, i, True).wait_recv()

    def drain(self):
        for i in range(self.zs):
            if i:
                self.z_copy(i, False).wait_send()
            for j in range(self.ys):
                if j:
                    self.y_copy(j, i, False).wait_send()
                self.core_copy(j, i, False).wait_send()


class Pair:
    def __init__(self, me, n, sides):
        self.has_right, self.has_left = me < n - 1, me > 0
        self.copies = [pltpu.make_async_remote_copy(
            src, dst, ssem, rsem, device_id={"cols": peer}, device_id_type=MESH)
            for (src, dst, ssem, rsem), peer in zip(
                sides, (lax.rem(me + 1, n), lax.rem(me + n - 1, n)))]

    def start(self):
        pl.when(self.has_right)(self.copies[0].start)
        pl.when(self.has_left)(self.copies[1].start)

    def wait(self):
        pl.when(self.has_left)(self.copies[0].wait_recv)
        pl.when(self.has_right)(self.copies[1].wait_recv)

    def drain(self):
        pl.when(self.has_right)(self.copies[0].wait_send)
        pl.when(self.has_left)(self.copies[1].wait_send)


class Sum:
    def __init__(self, pos, zs, ys, terms, bufs, sems):
        self.pos, self.zs, self.ys, self.terms = pos, zs, ys, terms
        self.s1, self.s2, self.bufc, self.bufy, self.bufz = bufs
        self.sc, self.rc, self.sy, self.ry, self.sz, self.rz = sems
        self.zorder = list(range(1, zs)) + [0]
        self.yorder = list(range(1, ys)) + [0]

    def zi(self, i):
        return lax.rem(self.pos[0] + i, self.zs)

    def yi(self, j):
        return lax.rem(self.pos[1] + j, self.ys)

    def copy(self, src, dst, ssem, rsem, device):
        return pltpu.make_async_remote_copy(
            src, dst, ssem, rsem, device_id=device, device_id_type=MESH)

    def core_copy(self, j, i):
        z, y, core = self.pos
        return self.copy(self.terms.at[self.zi(i), self.yi(j), 1 - core], self.bufc.at[j, i],
                         self.sc.at[j, i], self.rc.at[j, i], at(z, y, 1 - core, self.ys))

    def y_copy(self, j, i):
        z, y, core = self.pos
        return self.copy(self.s1.at[j, i], self.bufy.at[j, i], self.sy.at[j, i],
                         self.ry.at[j, i], at(z, self.yi(j), core, self.ys))

    def z_copy(self, i):
        z, y, core = self.pos
        return self.copy(self.s2.at[i], self.bufz.at[i], self.sz.at[i], self.rz.at[i],
                         at(self.zi(i), y, core, self.ys))

    def start(self):
        for j in self.yorder:
            for i in self.zorder:
                self.core_copy(j, i).start()

    def pair(self):
        core = self.pos[2]
        for j in self.yorder:
            for i in self.zorder:
                self.core_copy(j, i).wait_recv()
                both = self.terms[self.zi(i), self.yi(j), core].astype(F32)
                self.s1[j, i] = (both + self.bufc[j, i].astype(F32)).astype(BF16)
                if j:
                    self.y_copy(j, i).start()

    def along_y(self, begin, end):
        for i in self.zorder[begin:end]:
            total = self.s1[0, i].astype(F32)
            for j in range(1, self.ys):
                self.y_copy(j, i).wait_recv()
                total = total + self.bufy[j, i].astype(F32)
            if i:
                self.s2[i] = total.astype(BF16)
                self.z_copy(i).start()
            else:
                self.own = total

    def along_z(self):
        total = self.own
        for i in range(1, self.zs):
            self.z_copy(i).wait_recv()
            total = total + self.bufz[i].astype(F32)
        return total

    def drain_first(self):
        for j in self.yorder:
            for i in self.zorder:
                self.core_copy(j, i).wait_send()
                if j:
                    self.y_copy(j, i).wait_send()

    def drain_last(self):
        for i in range(1, self.zs):
            self.z_copy(i).wait_send()


class Sum2:
    def __init__(self, pos, zs, ys, terms, cut, bufs, sems):
        self.pos, self.zs, self.ys, self.terms = pos, zs, ys, terms
        (self.s1a, self.s1b, self.bufca, self.bufcb, self.bufy, self.s2a, self.bufz, self.bufw,
         self.s2b, self.bufv) = bufs
        (self.sc, self.rc, self.sy, self.ry, self.sz, self.rz, self.sw, self.rw, self.sv, self.rv,
         self.sb, self.rb) = sems
        self.cut, width = cut, terms.shape[-1]
        self.lanes_a, self.lanes_b = pl.ds(0, cut), pl.ds(cut, width - cut)
        self.zorder = list(range(1, zs)) + [0]
        self.yorder = list(range(1, ys)) + [0]

    def zi(self, i):
        return lax.rem(self.pos[0] + i, self.zs)

    def yi(self, j):
        return lax.rem(self.pos[1] + j, self.ys)

    def y_peer(self, j):
        return at(self.pos[0], self.yi(j), self.pos[2], self.ys)

    def z_peer(self, i):
        return at(self.zi(i), self.pos[1], self.pos[2], self.ys)

    def copy(self, src, dst, ssem, rsem, device):
        return pltpu.make_async_remote_copy(
            src, dst, ssem, rsem, device_id=device, device_id_type=MESH)

    def core_copy(self, j, i):
        z, y, core = self.pos
        return self.copy(self.terms.at[self.zi(i), self.yi(j), 1 - core, :, self.lanes_a], self.bufca.at[j, i],
                         self.sc.at[j, i], self.rc.at[j, i], at(z, y, 1 - core, self.ys))

    def core_copy_b(self):
        z, y, core = self.pos
        return self.copy(self.terms.at[:, :, 1 - core, :, self.lanes_b], self.bufcb, self.sb.at[0],
                         self.rb.at[0], at(z, y, 1 - core, self.ys))

    def y_copies(self, j):
        return [self.copy(self.s1a.at[j, i], self.bufy.at[j, i], self.sy.at[j, i],
                          self.ry.at[j, i], self.y_peer(j)) for i in self.zorder]

    def w_copy(self, i):
        return self.copy(self.s1b.at[i], self.bufw.at[i], self.sw.at[i],
                         self.rw.at[i], self.z_peer(i))

    def z_copy(self, i):
        return self.copy(self.s2a.at[i], self.bufz.at[i], self.sz.at[i], self.rz.at[i], self.z_peer(i))

    def v_copy(self, j):
        return self.copy(self.s2b.at[j], self.bufv.at[j], self.sv.at[j], self.rv.at[j], self.y_peer(j))

    def start_b(self):
        self.core_copy_b().start()

    def start_a(self):
        for j in self.yorder:
            for i in self.zorder:
                self.core_copy(j, i).start()

    def pair_b(self):
        core = self.pos[2]
        self.core_copy_b().wait_recv()
        for i in self.zorder:
            for j in range(self.ys):
                both = self.terms[self.zi(i), self.yi(j), core, :, self.lanes_b].astype(F32)
                self.s1b[i, j] = (both + self.bufcb[self.zi(i), self.yi(j)].astype(F32)).astype(BF16)
            if i:
                self.w_copy(i).start()

    def pair_a(self):
        core = self.pos[2]
        for j in self.yorder:
            for i in self.zorder:
                self.core_copy(j, i).wait_recv()
                both = self.terms[self.zi(i), self.yi(j), core, :, self.lanes_a].astype(F32)
                self.s1a[j, i] = (both + self.bufca[j, i].astype(F32)).astype(BF16)
                if j:
                    self.y_copies(j)[self.zorder.index(i)].start()

    def second_b(self):
        for i in self.zorder[:-1]:
            self.w_copy(i).wait_recv()
        for j in self.yorder:
            total = self.s1b[0, j].astype(F32)
            for i in self.zorder[:-1]:
                total = total + self.bufw[i, j].astype(F32)
            if j:
                self.s2b[j] = total.astype(BF16)
                self.v_copy(j).start()
            else:
                self.own_b = total

    def second_a(self, begin, end):
        for i in self.zorder[begin:end]:
            total = self.s1a[0, i].astype(F32)
            for j in range(1, self.ys):
                copies = self.y_copies(j)
                if len(copies) > 1:
                    copies[self.zorder.index(i)].wait_recv()
                elif i == self.zorder[0]:
                    copies[0].wait_recv()
                total = total + self.bufy[j, i].astype(F32)
            if i:
                self.s2a[i] = total.astype(BF16)
                self.z_copy(i).start()
            else:
                self.own_a = total

    def last_b(self):
        total = self.own_b
        for j in range(1, self.ys):
            self.v_copy(j).wait_recv()
            total = total + self.bufv[j].astype(F32)
        return total

    def last_a(self):
        total = self.own_a
        for i in range(1, self.zs):
            self.z_copy(i).wait_recv()
            total = total + self.bufz[i].astype(F32)
        return total

    def drain_first(self):
        self.core_copy_b().wait_send()
        for j in self.yorder:
            for i in self.zorder:
                self.core_copy(j, i).wait_send()
            if j:
                for copy in self.y_copies(j):
                    copy.wait_send()
        for i in range(1, self.zs):
            self.w_copy(i).wait_send()

    def drain_last(self):
        for j in range(1, self.ys):
            self.v_copy(j).wait_send()
        for i in range(1, self.zs):
            self.z_copy(i).wait_send()


def tap(t):
    return slice(t * LANES, (t + 1) * LANES)


def conv_taps(ref, w, start, step, count):
    total = None
    for kx in range(3):
        rhs = jnp.concatenate([w[:, tap(3 * ky + kx)] for ky in range(3)], axis=1)
        term = lax.dot_general(ref[pl.ds(start + kx * step, count), :], rhs,
                               (((1,), (1,)), ((), ())), preferred_element_type=F32)
        total = term if total is None else total + term
    return total


def join_rows(prod, d, height, kx):
    up = from_below(prod[:, tap(kx)], d, height)
    down = from_above(prod[:, tap(6 + kx)], d, height)
    return up + prod[:, tap(3 + kx)] + down


def put_terms(ref, place, value):
    zs, ys = ref.shape[0], ref.shape[1]
    (first, count), t = place
    ref[:, :, :, first : first + count, tap(t)] = value.reshape(zs, ys, 2, count, LANES).astype(BF16)


def grad_taps(ref, places, turned, acts, start, step, kxs=range(3)):
    count = turned.shape[1]
    for kx in kxs:
        prod = jnp.dot(turned, acts[pl.ds(start + kx * step, count), :],
                       preferred_element_type=F32)
        for ky in range(3):
            put_terms(ref, places[3 * ky + kx], prod[:, tap(ky)])


def fused_kernel(
    n, zs, ys, height, breadth, rl, rm, rf,
    x_ref, t_ref, wl_ref, wm_ref, wf_ref, o1_ref, o2_ref, o3_ref,
    xv, tv, wlv, wmv, wfv,
    pa, ga, gb, ta, tb, xh, xs, x9, x3f, x3s, pre1, pre2, acc, send, recv, tf, tn,
    a1, a2, a3, a4, a5, b1, b2, b3, b4, b5, b6, b7, b8, b9, b10, lsem, sx, rx, ssem, rsem, *sems,
):
    me, z, y, core = place(n, zs, ys)
    pos = (z, y, core)
    h, b = height, breadth
    depth = wf_ref.shape[1] // 9
    left, right = lax.rem(me + n - 1, n), lax.rem(me + 1, n)
    loads = [pltpu.make_async_copy(src, dst, lsem.at[i]) for i, (src, dst) in enumerate(
        ((wm_ref, wmv), (wf_ref, wfv), (x_ref, xv), (wl_ref, wlv), (t_ref, tv)))]
    for load in loads:
        load.start()
    peers = (
        [at(flip(z, i), y, core, ys) for i in range(1, zs)]
        + [at(z, flip(y, j), core, ys) for j in range(1, ys)]
        + [at(z, y, 1 - core, ys), {"cols": left}, {"cols": right}]
    )
    call(peers)
    middle = [((0, rm), t) if t < 7 else ((rm, rf), t - 7) for t in range(9)]
    first = [((rm, rf), t + 2) for t in range(5)]
    low = Star(pos, zs, ys, pa, ga, sems[0:6])
    cut = rl // 16 * 8
    parts = ((0, cut), (cut, rl - cut)) if cut else ((0, rl),)
    high = [Line(pos, zs, ys, wlv, gb, begin, rows, sems[8 * i + 6 : 8 * i + 14])
            for i, (begin, rows) in enumerate(parts)]
    sum_a = Sum(pos, zs, ys, ta, (a1, a2, a3, a4, a5), sems[22:28])
    sum_b = Sum2(pos, zs, ys, tb, 6 * LANES, (b1, b2, b3, b4, b5, b6, b7, b8, b9, b10),
                 sems[28:40])
    loads[0].wait()
    loads[1].wait()
    pa[0:rm, :] = wmv[:, 0 : 7 * LANES]
    pa[rm : rm + rf, 0 : 2 * LANES] = wmv[:, 7 * LANES : 9 * LANES]
    pa[rm : rm + rf, 6 * LANES : 7 * LANES] = jnp.zeros((rf, LANES), BF16)
    pa[rm : rm + rf, 2 * LANES : 2 * LANES + 9 * depth] = wfv[...]
    hear(peers)
    low.start()
    loads[2].wait()
    edge = 14 * depth
    halo = Pair(me, n, [(xv.at[:, pl.ds(b * depth - edge, edge)], xh.at[0], sx.at[0], rx.at[0]),
                        (xv.at[:, pl.ds(0, edge)], xh.at[1], sx.at[1], rx.at[1])])
    halo.start()
    loads[3].wait()
    for line in high:
        line.start()

    loads[4].wait()
    target = tv[...].astype(F32)
    t_norm = jnp.sqrt(jnp.sum(target * target, -1, keepdims=True) + epsilon)
    target = target / t_norm
    for q in range(tf.shape[0]):
        tf[q] = target[:, tap(q)]
    for i in reversed(range(1, zs)):
        low.forward_z(i)
    for c in range(b):
        for q in range(tf.shape[0]):
            tn[pl.ds(c * h, h), tap(q)] = tf[q, pl.ds(c, h, stride=b), :]
    for line in high:
        line.forward_z(1)

    first_col = me * b
    width = n * b

    def inside(v, first):
        cols = column_of(v.shape[0], h, first_col + first)
        return jnp.where((cols >= 0) & (cols < width), v, 0.0)

    halo.wait()
    half = lax.broadcasted_iota(jnp.int32, (h, LANES), 1) < depth
    at_col = 0
    for part, pairs in ((xh[0], 7), (xv[...], b // 2), (xh[1], 7)):
        part = part.astype(F32)
        for q in range(pairs):
            both = part[:, tap(q)]
            turned = pltpu.roll(both, depth, 1)
            xs[pl.ds(at_col * h, h), :] = jnp.where(half, both, turned)
            xs[pl.ds((at_col + 1) * h, h), :] = jnp.where(half, turned, both)
            at_col += 2
    for i in [0] + list(reversed(range(1, zs))):
        low.forward_y(i)
    for line in high:
        line.forward_z(2)
    wide_x = inside(xs[...], -14)
    count1 = (b + 24) * h
    rows3 = (from_above(wide_x, 2, h), wide_x, from_below(wide_x, 2, h))

    def piece(t):
        ky, kx = t // 3, t % 3
        return rows3[ky][kx * 2 * h : kx * 2 * h + count1]

    lower = lax.broadcasted_iota(jnp.int32, (count1, LANES), 1) < depth
    for q in range(5):
        odd = piece(2 * q + 1) if q < 4 else 0.0
        x9[:, tap(q)] = jnp.where(lower, piece(2 * q), odd).astype(BF16)
    for s in range(3, zs):
        for line in high:
            line.forward_z(s)
    low.finish()
    w1 = ga[:, :, :, rm : rm + rf, 2 * LANES : 7 * LANES].reshape(n * rf, 5 * LANES)
    v = lax.dot_general(x9[...], w1, (((1,), (1,)), ((), ())), preferred_element_type=F32)
    pre1[...] = v
    act = inside(v * sigmoid(v), -12).astype(BF16).astype(F32)
    spread_rows(x3f, act, 4, h)
    for line in high:
        for s in range(zs - 1):
            line.forward_y(s)
    w2 = jnp.concatenate([
        ga[:, :, :, 0:rm, :].reshape(n * rm, 7 * LANES),
        ga[:, :, :, rm : rm + rf, 0 : 2 * LANES].reshape(n * rm, 2 * LANES)], axis=1)
    v = conv_taps(x3f, w2, 0, 4 * h, (b + 16) * h)
    pre2[...] = v
    act = inside(v * sigmoid(v), -8).astype(BF16).astype(F32)
    spread_rows(x3s, act, 8, h)
    for line in high:
        line.forward_y(zs - 1)
    for line in high:
        line.finish()
    w3 = gb[...].reshape(n * rl, 9 * LANES)
    student = conv_taps(x3s, w3, 0, 8 * h, b * h)
    s_norm = jnp.sqrt(jnp.sum(student * student, -1, keepdims=True) + epsilon)
    s_unit = student / s_norm
    differ = s_unit - tn[...]
    slope = (differ - s_unit * jnp.sum(s_unit * differ, -1, keepdims=True)) / s_norm

    prod = jnp.dot(slope.astype(BF16), w3, preferred_element_type=F32)
    e = 8 * h
    m = b * h
    acc[pl.ds(0, m), :] = join_rows(prod, 8, h, 0)
    acc[pl.ds(m, 2 * e), :] = jnp.zeros((2 * e, LANES), F32)
    acc[pl.ds(e, m), :] += join_rows(prod, 8, h, 1)
    acc[pl.ds(2 * e, m), :] += join_rows(prod, 8, h, 2)
    part = 12 * h
    send[0] = acc[pl.ds(m + 2 * e - part, part), :].astype(BF16)
    send[1] = acc[pl.ds(0, part), :].astype(BF16)
    copies = Pair(me, n, [(send.at[side], recv.at[side], ssem.at[side], rsem.at[side])
                          for side in range(2)])
    copies.start()
    turned = slope.T.astype(BF16)
    last = [((0, rl), 3 * (t % 3) + t // 3) for t in range(9)]
    grad_taps(tb, last, turned, x3s, 0, 8 * h, (2,))
    sum_b.start_b()
    grad_taps(tb, last, turned, x3s, 0, 8 * h, (0, 1))
    sum_b.start_a()
    sum_b.pair_b()
    sum_b.pair_a()
    for each in (halo, low, *high):
        each.drain()
    copies.wait()
    inner = (b + 8) * h
    split = inner - part
    from_left = jnp.where(me > 0, recv[0].astype(F32), 0.0)
    from_right = jnp.where(me < n - 1, recv[1].astype(F32), 0.0)
    acc[pl.ds(4 * h, part), :] += from_left
    acc[pl.ds(4 * h + split, part), :] += from_right
    back = acc[pl.ds(4 * h, inner), :]
    slope2 = inside(back * silu_slope(pre2[pl.ds(4 * h, inner), :]), -4).astype(BF16)
    prod = jnp.dot(slope2, w2, preferred_element_type=F32)
    back = (
        join_rows(prod, 4, h, 0)[8 * h : 8 * h + m]
        + join_rows(prod, 4, h, 1)[4 * h : 4 * h + m]
        + join_rows(prod, 4, h, 2)[0:m]
    )
    grad_taps(ta, middle, slope2.astype(F32)[4 * h : 4 * h + m].T.astype(BF16), x3f, 8 * h, 4 * h)
    slope1 = back * silu_slope(pre1[pl.ds(12 * h, m), :])
    prod = jnp.dot(slope1.T.astype(BF16), x9[pl.ds(12 * h, m), :], preferred_element_type=F32)
    for q in range(5):
        put_terms(ta, first[q], prod[:, tap(q)])
    sum_a.start()
    sum_b.second_a(0, 1)
    sum_a.pair()
    sum_b.second_a(1, 2)
    sum_b.second_b()
    sum_b.second_a(2, zs)
    sum_a.along_y(0, zs)
    copies.drain()
    sum_b.drain_first()
    sum_a.drain_first()
    for kxs, total in (((0, 1), sum_b.last_a()), ((2,), sum_b.last_b())):
        for i, kx in enumerate(kxs):
            for ky in range(3):
                o3_ref[:, tap(3 * ky + kx)] = total[:, tap(3 * i + ky)]
    total = sum_a.along_z()
    o2_ref[:, 0 : 7 * LANES] = total[0:rm]
    o2_ref[:, 7 * LANES : 9 * LANES] = total[rm : rm + rf, 0 : 2 * LANES]
    o1_ref[...] = total[rm : rm + rf, 2 * LANES : 2 * LANES + 9 * depth]
    sum_a.drain_last()
    sum_b.drain_last()


def hand_over_kernel(a_ref, b_ref, c_ref, x_ref, y_ref, z_ref):
    x_ref[...] = a_ref[...]
    y_ref[...] = b_ref[...]
    z_ref[...] = c_ref[...]


def hand_over(arrays):
    vmem = pl.BlockSpec(memory_space=pltpu.VMEM)
    return pl.pallas_call(
        hand_over_kernel,
        out_shape=tuple(jax.ShapeDtypeStruct(a.shape, a.dtype) for a in arrays),
        in_specs=[vmem] * 3,
        out_specs=(vmem,) * 3,
        name="hand_over",
    )(*(pltpu.with_memory_space_constraint(a, pltpu.VMEM) for a in arrays))


def fused(n, height, breadth, x, t, wl, wm, wf):
    zs, ys = split_axis(n)
    sem = pltpu.SemaphoreType.DMA
    vmem = pl.BlockSpec(memory_space=pltpu.VMEM)
    h, b = height, breadth
    rl, rm, rf = wl.shape[0], wm.shape[0], wf.shape[0]
    wide = wl.shape[1]
    low, high = (rm + rf, 7 * LANES), (rl, wide)
    channels = t.shape[1]

    def sum_bufs(block):
        return [
            pltpu.VMEM((ys, zs) + block, BF16), pltpu.VMEM((zs,) + block, BF16),
            pltpu.VMEM((ys, zs) + block, BF16), pltpu.VMEM((ys, zs) + block, BF16),
            pltpu.VMEM((zs,) + block, BF16),
        ]

    def sum2_bufs(block, cut):
        rows, width = block
        part_a, part_b = (rows, cut), (rows, width - cut)
        return [
            pltpu.VMEM((ys, zs) + part_a, BF16), pltpu.VMEM((zs, ys) + part_b, BF16),
            pltpu.VMEM((ys, zs) + part_a, BF16), pltpu.VMEM((zs, ys) + part_b, BF16),
            pltpu.VMEM((ys, zs) + part_a, BF16), pltpu.VMEM((zs,) + part_a, BF16),
            pltpu.VMEM((zs,) + part_a, BF16), pltpu.VMEM((zs, ys) + part_b, BF16),
            pltpu.VMEM((ys,) + part_b, BF16), pltpu.VMEM((ys,) + part_b, BF16),
        ]

    star_sems = [sem((zs,))] * 2 + [sem((ys, zs))] * 4
    line_sems = [sem((zs,))] * 4 + [sem((ys, zs))] * 4
    sum_sems = [sem((ys, zs))] * 4 + [sem((zs,))] * 2
    sum2_sems = [sem((ys, zs))] * 4 + [sem((zs,))] * 4 + [sem((ys,))] * 2 + [sem((1,))] * 2
    return pl.pallas_call(
        functools.partial(fused_kernel, n, zs, ys, h, b, rl, rm, rf),
        out_shape=tuple(pltpu.VMEM(w.shape, F32) for w in (wf, wm, wl)),
        in_specs=[pl.BlockSpec(memory_space=pltpu.HBM)] * 5,
        out_specs=(vmem,) * 3,
        scratch_shapes=[pltpu.VMEM(w.shape, BF16) for w in (x, t, wl, wm, wf)] + [
            pltpu.VMEM(low, BF16),
            pltpu.VMEM((zs, ys, 2) + low, BF16),
            pltpu.VMEM((zs, ys, 2) + high, BF16),
            pltpu.VMEM((zs, ys, 2) + low, BF16),
            pltpu.VMEM((zs, ys, 2) + high, BF16),
            pltpu.VMEM((2, h, 14 * wf.shape[1] // 9), BF16),
            pltpu.VMEM(((b + 28) * h, LANES), F32),
            pltpu.VMEM(((b + 24) * h, 5 * LANES), BF16),
            pltpu.VMEM(((b + 24) * h, 3 * LANES), BF16),
            pltpu.VMEM(((b + 16) * h, 3 * LANES), BF16),
            pltpu.VMEM(((b + 24) * h, LANES), F32),
            pltpu.VMEM(((b + 16) * h, LANES), F32),
            pltpu.VMEM(((b + 16) * h, LANES), F32),
            pltpu.VMEM((2, 12 * h, LANES), BF16),
            pltpu.VMEM((2, 12 * h, LANES), BF16),
            pltpu.VMEM((channels // LANES, b * h, LANES), F32),
            pltpu.VMEM((b * h, channels), F32),
        ]
        + sum_bufs(low) + sum2_bufs(high, 6 * LANES)
        + [sem((5,))] + [sem((2,))] * 4 + star_sems + line_sems * 2 + sum_sems + sum2_sems,
        compiler_params=pltpu.CompilerParams(
            collective_id=3, has_side_effects=True, vmem_limit_bytes=56 << 20),
        name="fused_step",
    )(x, t, wl, wm, wf)


def on_device(n, image_feats, teacher, w_first, w_middle, w_last):
    height, breadth, channels = teacher.shape
    in_depth = w_first.shape[1] // 9
    rl, rm, rf = w_last.shape[0], w_middle.shape[0], w_first.shape[0]
    if (split_axis(n)[0] > 2 and n & (n - 1) == 0 and rm == rf and all(r % 8 == 0 for r in (rl, rm, rf))
            and breadth % 8 == 0 and 2 * in_depth == LANES):
        return hand_over(fused(n, height, breadth, image_feats,
                               teacher.reshape(height * breadth, channels), w_last, w_middle, w_first))
    packed = jnp.concatenate([taps_by_column(w) for w in (w_last, w_middle, w_first)], axis=0)
    x = image_feats.reshape(height, breadth, in_depth).transpose(1, 0, 2)
    x = jnp.pad(x, ((0, 0), (0, 0), (0, LANES - in_depth)))
    x_cells = x.reshape(breadth * height, LANES)
    t_cells = teacher.transpose(1, 0, 2).reshape(breadth * height, channels)
    gathered, x_edges = gather(n, packed, x_cells, 14 * height)
    g = gathered.reshape((n,) + packed.shape)
    w3 = g[:, :rl].reshape(n * rl, -1)
    w2 = g[:, rl : rl + rm].reshape(n * rm, -1)
    w1 = g[:, rl + rm :].reshape(n * rf, -1)
    g1, g2, g3 = local_step(n, height, breadth, x_cells, x_edges, t_cells, w1, w2, w3)
    terms = jnp.concatenate(
        [g3.reshape(n, rl, -1), g2.reshape(n, rm, -1), g1.reshape(n, rf, -1)], axis=1)
    out = scatter(n, terms.reshape(gathered.shape))
    return (
        taps_by_row(out[rl + rm :], in_depth),
        taps_by_row(out[rl : rl + rm], LANES),
        taps_by_row(out[:rl], LANES),
    )


def solution(mesh):
    placed = (
        P("groups", "cols"),
        P("groups", "cols", None),
        P("cols", None),
        P("cols", None),
        P("cols", None),
    )
    return jax.shard_map(
        functools.partial(on_device, mesh.shape["cols"]),
        mesh=mesh,
        in_specs=placed,
        out_specs=(P(("groups", "cols"), None),) * 3,
        check_vma=False,
    )
```

```python
import functools

import jax
import jax.numpy as jnp
from jax import lax
from jax.experimental import pallas as pl
from jax.experimental.pallas import tpu as pltpu
from jax.sharding import PartitionSpec as P

epsilon = 1e-06
MESH = pl.DeviceIdType.MESH
LANES = 128
F32 = jnp.float32
BF16 = jnp.bfloat16


def split_axis(n):
    half = n // 2
    y = 1
    while 4 * y * y <= half:
        y *= 2
    return half // y, y


def place(n, z_size, y_size):
    me = lax.axis_index("cols")
    core = lax.rem(me, 2)
    y = lax.rem(me // 2, y_size)
    z = me // (2 * y_size)
    return me, z, y, core


def at(z, y, core, y_size):
    return {"cols": (z * y_size + y) * 2 + core}


def call(peers):
    barrier = pltpu.get_barrier_semaphore()
    for peer in peers:
        pl.semaphore_signal(barrier, inc=1, device_id=peer, device_id_type=MESH)


def hear(peers):
    pl.semaphore_wait(pltpu.get_barrier_semaphore(), len(peers))


def greet(peers):
    call(peers)
    hear(peers)


def gather_kernel(n, zs, ys, edge, p_ref, x_ref, g_ref, xh_ref, sz, rz, sy, ry, sc, rc, sx, rx):
    me, z, y, core = place(n, zs, ys)
    other = 1 - core
    zmod = [lax.rem(z + i, zs) for i in range(zs)]
    zback = [lax.rem(z + zs - i, zs) for i in range(zs)]
    ymod = [lax.rem(y + i, ys) for i in range(ys)]
    yback = [lax.rem(y + ys - i, ys) for i in range(ys)]
    left, right = lax.rem(me + n - 1, n), lax.rem(me + 1, n)
    greet(
        [at(zmod[i], y, core, ys) for i in range(1, zs)]
        + [at(z, ymod[j], core, ys) for j in range(1, ys)]
        + [at(z, y, other, ys), {"cols": left}, {"cols": right}]
    )

    def block(zi, yi, c):
        return g_ref.at[zi, yi, c]

    def to_z(i):
        return pltpu.make_async_remote_copy(
            p_ref, block(z, y, core), sz.at[i], rz.at[i],
            device_id=at(zmod[i], y, core, ys), device_id_type=MESH)

    def from_z(i):
        return pltpu.make_async_remote_copy(
            p_ref, block(zback[i], y, core), sz.at[i], rz.at[i],
            device_id=at(zmod[i], y, core, ys), device_id_type=MESH)

    def to_y(j, i):
        src = p_ref if i == 0 else block(zback[i], y, core)
        return pltpu.make_async_remote_copy(
            src, block(zback[i], y, core), sy.at[j, i], ry.at[j, i],
            device_id=at(z, ymod[j], core, ys), device_id_type=MESH)

    def from_y(j, i):
        return pltpu.make_async_remote_copy(
            p_ref, block(zback[i], yback[j], core), sy.at[j, i], ry.at[j, i],
            device_id=at(z, ymod[j], core, ys), device_id_type=MESH)

    def to_core(j, i):
        src = p_ref if i == 0 and j == 0 else block(zback[i], yback[j], core)
        return pltpu.make_async_remote_copy(
            src, block(zback[i], yback[j], core), sc.at[j, i], rc.at[j, i],
            device_id=at(z, y, other, ys), device_id_type=MESH)

    def from_core(j, i):
        return pltpu.make_async_remote_copy(
            p_ref, block(zback[i], yback[j], other), sc.at[j, i], rc.at[j, i],
            device_id=at(z, y, other, ys), device_id_type=MESH)

    cells = x_ref.shape[0]
    to_right = pltpu.make_async_remote_copy(
        x_ref.at[pl.ds(cells - edge, edge)], xh_ref.at[0], sx.at[0], rx.at[0],
        device_id={"cols": right}, device_id_type=MESH)
    to_left = pltpu.make_async_remote_copy(
        x_ref.at[pl.ds(0, edge)], xh_ref.at[1], sx.at[1], rx.at[1],
        device_id={"cols": left}, device_id_type=MESH)
    started = []

    def go(copy):
        copy.start()
        started.append(copy)

    for i in range(1, zs):
        go(to_z(i))
    for j in range(1, ys):
        go(to_y(j, 0))
    go(to_right)
    go(to_left)
    go(to_core(0, 0))
    g_ref[z, y, core] = p_ref[...]
    for i in range(1, zs):
        from_z(i).wait_recv()
        for j in range(1, ys):
            go(to_y(j, i))
        go(to_core(0, i))
    for i in range(zs):
        for j in range(1, ys):
            from_y(j, i).wait_recv()
            go(to_core(j, i))
    to_right.wait_recv()
    to_left.wait_recv()
    for i in range(zs):
        for j in range(ys):
            from_core(j, i).wait_recv()
    for copy in started:
        copy.wait_send()


def gather(n, packed, x_cells, edge):
    zs, ys = split_axis(n)
    sem = pltpu.SemaphoreType.DMA
    vmem = pl.BlockSpec(memory_space=pltpu.VMEM)
    return pl.pallas_call(
        functools.partial(gather_kernel, n, zs, ys, edge),
        out_shape=(
            jax.ShapeDtypeStruct((zs, ys, 2) + packed.shape, BF16),
            jax.ShapeDtypeStruct((2, edge, x_cells.shape[1]), BF16),
        ),
        in_specs=[vmem, vmem],
        out_specs=(vmem, vmem),
        scratch_shapes=[
            sem((zs,)), sem((zs,)), sem((ys, zs)), sem((ys, zs)), sem((ys, zs)), sem((ys, zs)),
            sem((2,)), sem((2,)),
        ],
        compiler_params=pltpu.CompilerParams(
            collective_id=0, has_side_effects=True, vmem_limit_bytes=48 << 20),
        name="gather_weights",
    )(packed, x_cells)


def scatter_kernel(n, zs, ys, t_ref, out_ref, s1, s2, bufc, bufy, bufz, sc, rc, sy, ry, sz, rz):
    me, z, y, core = place(n, zs, ys)
    other = 1 - core
    zmod = [lax.rem(z + i, zs) for i in range(zs)]
    ymod = [lax.rem(y + i, ys) for i in range(ys)]
    greet(
        [at(zmod[i], y, core, ys) for i in range(1, zs)]
        + [at(z, ymod[j], core, ys) for j in range(1, ys)]
        + [at(z, y, other, ys)]
    )
    zorder = list(range(1, zs)) + [0]
    yorder = list(range(1, ys)) + [0]

    def core_copy(j, i):
        return pltpu.make_async_remote_copy(
            t_ref.at[zmod[i], ymod[j], other], bufc.at[j, i], sc.at[j, i], rc.at[j, i],
            device_id=at(z, y, other, ys), device_id_type=MESH)

    def y_copy(j, i):
        return pltpu.make_async_remote_copy(
            s1.at[j, i], bufy.at[j, i], sy.at[j, i], ry.at[j, i],
            device_id=at(z, ymod[j], core, ys), device_id_type=MESH)

    def z_copy(i):
        return pltpu.make_async_remote_copy(
            s2.at[i], bufz.at[i], sz.at[i], rz.at[i],
            device_id=at(zmod[i], y, core, ys), device_id_type=MESH)

    started = []

    def go(copy):
        copy.start()
        started.append(copy)

    for j in yorder:
        for i in zorder:
            go(core_copy(j, i))
    for j in yorder:
        for i in zorder:
            core_copy(j, i).wait_recv()
            both = t_ref[zmod[i], ymod[j], core].astype(F32) + bufc[j, i].astype(F32)
            s1[j, i] = both.astype(BF16)
            if j:
                go(y_copy(j, i))
    for i in zorder:
        total = s1[0, i].astype(F32)
        for j in range(1, ys):
            y_copy(j, i).wait_recv()
            total = total + bufy[j, i].astype(F32)
        if i:
            s2[i] = total.astype(BF16)
            go(z_copy(i))
        else:
            out_ref[...] = total
    for i in range(1, zs):
        z_copy(i).wait_recv()
        out_ref[...] = out_ref[...] + bufz[i].astype(F32)
    for copy in started:
        copy.wait_send()


def scatter(n, terms):
    zs, ys = split_axis(n)
    sem = pltpu.SemaphoreType.DMA
    block = terms.shape[3:]
    vmem = pl.BlockSpec(memory_space=pltpu.VMEM)
    return pl.pallas_call(
        functools.partial(scatter_kernel, n, zs, ys),
        out_shape=jax.ShapeDtypeStruct(block, F32),
        in_specs=[vmem],
        out_specs=vmem,
        scratch_shapes=[
            pltpu.VMEM((ys, zs) + block, BF16),
            pltpu.VMEM((zs,) + block, BF16),
            pltpu.VMEM((ys, zs) + block, BF16),
            pltpu.VMEM((ys, zs) + block, BF16),
            pltpu.VMEM((zs,) + block, BF16),
            sem((ys, zs)), sem((ys, zs)), sem((ys, zs)), sem((ys, zs)), sem((zs,)), sem((zs,)),
        ],
        compiler_params=pltpu.CompilerParams(
            collective_id=2, has_side_effects=True, vmem_limit_bytes=48 << 20),
        name="scatter_terms",
    )(terms)


def row_of(count, height):
    return lax.rem(lax.broadcasted_iota(jnp.int32, (count, LANES), 0), height)


def column_of(count, height, first):
    return lax.broadcasted_iota(jnp.int32, (count, LANES), 0) // height + first


def from_above(v, d, height):
    return jnp.where(row_of(v.shape[0], height) >= d, pltpu.roll(v, d, 0), 0.0)


def from_below(v, d, height):
    count = v.shape[0]
    return jnp.where(row_of(count, height) < height - d, pltpu.roll(v, count - d, 0), 0.0)


def spread_rows(ref, v, d, height):
    ref[:, 0:LANES] = from_above(v, d, height).astype(BF16)
    ref[:, LANES : 2 * LANES] = v.astype(BF16)
    ref[:, 2 * LANES : 3 * LANES] = from_below(v, d, height).astype(BF16)


def sigmoid(v):
    return 1.0 / (1.0 + jnp.exp(-v))


def silu_slope(pre):
    sigma = sigmoid(pre)
    return sigma * (1.0 + pre * (1.0 - sigma))


def conv(ref, w_ref, start, step, count):
    total = None
    for kx in range(3):
        term = lax.dot_general(
            ref[pl.ds(start + kx * step, count), :],
            w_ref[:, kx * 3 * LANES : (kx + 1) * 3 * LANES],
            (((1,), (1,)), ((), ())),
            preferred_element_type=F32,
        )
        total = term if total is None else total + term
    return total


def gather_rows(prod, d, height, kx):
    base = kx * 3 * LANES
    up = from_below(prod[:, base : base + LANES], d, height)
    same = prod[:, base + LANES : base + 2 * LANES]
    down = from_above(prod[:, base + 2 * LANES : base + 3 * LANES], d, height)
    return up + same + down


def weight_grad(out_ref, slope_f32, ref, start, step):
    count = slope_f32.shape[0]
    turned = slope_f32.T.astype(BF16)
    for kx in range(3):
        out_ref[:, kx * 3 * LANES : (kx + 1) * 3 * LANES] = jnp.dot(
            turned, ref[pl.ds(start + kx * step, count), :], preferred_element_type=F32
        ).astype(BF16)


def step_kernel(
    n, height, breadth,
    x_ref, xh_ref, t_ref, w1_ref, w2_ref, w3_ref, g1_ref, g2_ref, g3_ref,
    x3x, x3f, x3s, pre1, pre2, acc, send, recv, ssem, rsem,
):
    me = lax.axis_index("cols")
    left, right = lax.rem(me + n - 1, n), lax.rem(me + 1, n)
    greet([{"cols": left}, {"cols": right}])
    h, b = height, breadth
    first_col = me * b
    width = n * b

    def inside(v, first):
        cols = column_of(v.shape[0], h, first_col + first)
        return jnp.where((cols >= 0) & (cols < width), v, 0.0)

    wide_x = jnp.concatenate([xh_ref[0], x_ref[...], xh_ref[1]], axis=0).astype(F32)
    spread_rows(x3x, inside(wide_x, -14), 2, h)
    v = conv(x3x, w1_ref, 0, 2 * h, (b + 24) * h)
    pre1[...] = v
    act = inside(v * sigmoid(v), -12).astype(BF16).astype(F32)
    spread_rows(x3f, act, 4, h)
    v = conv(x3f, w2_ref, 0, 4 * h, (b + 16) * h)
    pre2[...] = v
    act = inside(v * sigmoid(v), -8).astype(BF16).astype(F32)
    spread_rows(x3s, act, 8, h)
    student = conv(x3s, w3_ref, 0, 8 * h, b * h)
    s_norm = jnp.sqrt(jnp.sum(student * student, -1, keepdims=True) + epsilon)
    target = t_ref[...].astype(F32)
    t_norm = jnp.sqrt(jnp.sum(target * target, -1, keepdims=True) + epsilon)
    s_unit = student / s_norm
    differ = s_unit - target / t_norm
    slope = (differ - s_unit * jnp.sum(s_unit * differ, -1, keepdims=True)) / s_norm
    slope_b = slope.astype(BF16)

    prod = jnp.dot(slope_b, w3_ref[...], preferred_element_type=F32)
    u0 = gather_rows(prod, 8, h, 0)
    u1 = gather_rows(prod, 8, h, 1)
    u2 = gather_rows(prod, 8, h, 2)
    e = 8 * h
    m = b * h
    acc[pl.ds(0, m), :] = u0
    acc[pl.ds(m, 2 * e), :] = jnp.zeros((2 * e, LANES), F32)
    acc[pl.ds(e, m), :] += u1
    acc[pl.ds(2 * e, m), :] += u2
    part = 12 * h
    send[0] = acc[pl.ds(m + 2 * e - part, part), :].astype(BF16)
    send[1] = acc[pl.ds(0, part), :].astype(BF16)
    copies = []
    for side, target_id in ((0, right), (1, left)):
        copy = pltpu.make_async_remote_copy(
            send.at[side], recv.at[side], ssem.at[side], rsem.at[side],
            device_id={"cols": target_id}, device_id_type=MESH)
        copy.start()
        copies.append(copy)
    weight_grad(g3_ref, slope, x3s, 0, 8 * h)
    for copy in copies:
        copy.wait()
    inner = (b + 8) * h
    split = inner - part
    from_left = jnp.where(me > 0, recv[0].astype(F32), 0.0)
    from_right = jnp.where(me < n - 1, recv[1].astype(F32), 0.0)
    acc[pl.ds(4 * h, part), :] += from_left
    acc[pl.ds(4 * h + split, part), :] += from_right
    back = acc[pl.ds(4 * h, inner), :]
    slope2 = inside(back * silu_slope(pre2[pl.ds(4 * h, inner), :]), -4).astype(BF16)
    prod = jnp.dot(slope2, w2_ref[...], preferred_element_type=F32)
    back = (
        gather_rows(prod, 4, h, 0)[8 * h : 8 * h + m]
        + gather_rows(prod, 4, h, 1)[4 * h : 4 * h + m]
        + gather_rows(prod, 4, h, 2)[0:m]
    )
    weight_grad(g2_ref, slope2.astype(F32)[4 * h : 4 * h + m], x3f, 8 * h, 4 * h)
    slope1 = back * silu_slope(pre1[pl.ds(12 * h, m), :])
    weight_grad(g1_ref, slope1, x3x, 12 * h, 2 * h)


def local_step(n, height, breadth, x_cells, x_edges, teacher, w1, w2, w3):
    sem = pltpu.SemaphoreType.DMA
    vmem = pl.BlockSpec(memory_space=pltpu.VMEM)
    h, b = height, breadth
    return pl.pallas_call(
        functools.partial(step_kernel, n, h, b),
        out_shape=tuple(jax.ShapeDtypeStruct(w.shape, BF16) for w in (w1, w2, w3)),
        in_specs=[vmem] * 6,
        out_specs=(vmem,) * 3,
        scratch_shapes=[
            pltpu.VMEM(((b + 28) * h, 3 * LANES), BF16),
            pltpu.VMEM(((b + 24) * h, 3 * LANES), BF16),
            pltpu.VMEM(((b + 16) * h, 3 * LANES), BF16),
            pltpu.VMEM(((b + 24) * h, LANES), F32),
            pltpu.VMEM(((b + 16) * h, LANES), F32),
            pltpu.VMEM(((b + 16) * h, LANES), F32),
            pltpu.VMEM((2, 12 * h, LANES), BF16),
            pltpu.VMEM((2, 12 * h, LANES), BF16),
            sem((2,)), sem((2,)),
        ],
        compiler_params=pltpu.CompilerParams(
            collective_id=1, has_side_effects=True, vmem_limit_bytes=56 << 20),
        name="student_step",
    )(x_cells, x_edges, teacher, w1, w2, w3)


def taps_by_column(w):
    rows, depth = w.shape[0], w.shape[1] // 9
    w = w.reshape(rows, 3, 3, depth).transpose(0, 2, 1, 3)
    w = jnp.pad(w, ((0, 0), (0, 0), (0, 0), (0, LANES - depth)))
    return w.reshape(rows, 9 * LANES)


def taps_by_row(g, depth):
    rows = g.shape[0]
    g = g.reshape(rows, 3, 3, LANES)[..., :depth].transpose(0, 2, 1, 3)
    return g.reshape(rows, 9 * depth)


class Line:
    def __init__(self, pos, zs, ys, src, out, first, rows, sems):
        self.pos, self.zs, self.ys = pos, zs, ys
        self.rows = pl.ds(first, rows)
        self.src, self.out = src.at[self.rows], out
        self.szr, self.rzr, self.szl, self.rzl, self.sy, self.ry, self.sc, self.rc = sems

    def copy(self, src, dst, ssem, rsem, device):
        return pltpu.make_async_remote_copy(
            src, dst, ssem, rsem, device_id=device, device_id_type=MESH)

    def block(self, zi, yi, c):
        return self.out.at[zi, yi, c, self.rows]

    def hop(self, way, s):
        z, y, core = self.pos
        zi = z - way * s
        src = self.src if s == 0 else self.block(zi, y, core)
        ss, rs = (self.szr, self.rzr) if way > 0 else (self.szl, self.rzl)
        ok = (zi >= 0) & (zi < self.zs) & (z + way >= 0) & (z + way < self.zs)
        return ok, self.copy(
            src, self.block(zi, y, core), ss.at[s], rs.at[s + 1], at(z + way, y, core, self.ys))

    def arrived(self, way, s):
        z, y, core = self.pos
        zi = z - way * s
        ss, rs = (self.szr, self.rzr) if way > 0 else (self.szl, self.rzl)
        ok = (zi >= 0) & (zi < self.zs)
        return ok, zi, self.copy(
            self.src, self.block(zi, y, core), ss.at[0], rs.at[s], at(z, y, 1 - core, self.ys))

    def to_y(self, j, zi, own):
        z, y, core = self.pos
        src = self.src if own else self.block(zi, y, core)
        return self.copy(src, self.block(zi, y, core), self.sy.at[j, zi], self.ry.at[j, zi],
                         at(z, lax.rem(y + j, self.ys), core, self.ys))

    def from_y(self, j, zi):
        z, y, core = self.pos
        yi = lax.rem(y + self.ys - j, self.ys)
        return self.copy(self.src, self.block(zi, yi, core), self.sy.at[j, zi], self.ry.at[j, zi],
                         at(z, lax.rem(y + j, self.ys), core, self.ys))

    def to_core(self, j, zi, own):
        z, y, core = self.pos
        yi = lax.rem(y + self.ys - j, self.ys)
        src = self.src if own else self.block(zi, yi, core)
        return self.copy(src, self.block(zi, yi, core), self.sc.at[j, zi], self.rc.at[j, zi],
                         at(z, y, 1 - core, self.ys))

    def from_core(self, j, zi):
        z, y, core = self.pos
        yi = lax.rem(y + self.ys - j, self.ys)
        return self.copy(self.src, self.block(zi, yi, 1 - core), self.sc.at[j, zi],
                         self.rc.at[j, zi], at(z, y, 1 - core, self.ys))

    def start(self):
        z, y, core = self.pos
        for way in (1, -1):
            ok, copy = self.hop(way, 0)
            pl.when(ok)(copy.start)
        for j in range(1, self.ys):
            self.to_y(j, z, True).start()
        self.to_core(0, z, True).start()
        self.out[z, y, core, self.rows] = self.src[...]

    def forward_z(self, s):
        for way in (1, -1):
            ok, zi, here = self.arrived(way, s)

            @pl.when(ok)
            def _():
                here.wait_recv()
                for j in range(1, self.ys):
                    self.to_y(j, zi, False).start()

            if s < self.zs - 1:
                more, on = self.hop(way, s)
                pl.when(more)(on.start)

            @pl.when(ok)
            def _():
                self.to_core(0, zi, False).start()

    def forward_y(self, s):
        z = self.pos[0]
        todo = [(None, z)] if s == 0 else [
            ((z - way * s >= 0) & (z - way * s < self.zs), z - way * s) for way in (1, -1)]
        for ok, zi in todo:

            def step(zi=zi):
                for j in range(1, self.ys):
                    self.from_y(j, zi).wait_recv()
                    self.to_core(j, zi, False).start()

            step() if ok is None else pl.when(ok)(step)

    def finish(self):
        for zi in range(self.zs):
            for j in range(self.ys):
                self.from_core(j, zi).wait_recv()

    def drain(self):
        for s in range(self.zs - 1):
            for way in (1, -1):
                ok, copy = self.hop(way, s)
                pl.when(ok)(copy.wait_send)
        for zi in range(self.zs):
            for j in range(self.ys):
                if j:
                    self.to_y(j, zi, False).wait_send()
                self.to_core(j, zi, False).wait_send()


def flip(v, i):
    bit = 1
    while bit <= i:
        if i & bit:
            v = v + bit - 2 * bit * lax.rem(v // bit, 2)
        bit *= 2
    return v


class Star:
    def __init__(self, pos, zs, ys, src, out, sems):
        self.pos, self.zs, self.ys, self.src, self.out = pos, zs, ys, src, out
        self.sz, self.rz, self.sy, self.ry, self.sc, self.rc = sems

    def copy(self, src, dst, ssem, rsem, device):
        return pltpu.make_async_remote_copy(
            src, dst, ssem, rsem, device_id=device, device_id_type=MESH)

    def block(self, i, j, k):
        z, y, core = self.pos
        return self.out.at[flip(z, i), flip(y, j), flip(core, k)]

    def held(self, i, j):
        return self.src if i == 0 and j == 0 else self.block(i, j, 0)

    def z_copy(self, i, arriving):
        z, y, core = self.pos
        return self.copy(self.src, self.block(i if arriving else 0, 0, 0), self.sz.at[i],
                         self.rz.at[i], at(flip(z, i), y, core, self.ys))

    def y_copy(self, j, i, arriving):
        z, y, core = self.pos
        return self.copy(self.held(i, 0), self.block(i, j if arriving else 0, 0), self.sy.at[j, i],
                         self.ry.at[j, i], at(z, flip(y, j), core, self.ys))

    def core_copy(self, j, i, arriving):
        z, y, core = self.pos
        return self.copy(self.held(i, j), self.block(i, j, 1 if arriving else 0), self.sc.at[j, i],
                         self.rc.at[j, i], at(z, y, 1 - core, self.ys))

    def start(self):
        for i in reversed(range(1, self.zs)):
            self.z_copy(i, False).start()
        for j in range(1, self.ys):
            self.y_copy(j, 0, False).start()
        self.core_copy(0, 0, False).start()
        z, y, core = self.pos
        self.out[z, y, core] = self.src[...]

    def forward_z(self, i):
        self.z_copy(i, True).wait_recv()
        for j in range(1, self.ys):
            self.y_copy(j, i, False).start()
        self.core_copy(0, i, False).start()

    def forward_y(self, i):
        for j in range(1, self.ys):
            self.y_copy(j, i, True).wait_recv()
            self.core_copy(j, i, False).start()

    def finish(self):
        for i in range(self.zs):
            for j in range(self.ys):
                self.core_copy(j, i, True).wait_recv()

    def drain(self):
        for i in range(self.zs):
            if i:
                self.z_copy(i, False).wait_send()
            for j in range(self.ys):
                if j:
                    self.y_copy(j, i, False).wait_send()
                self.core_copy(j, i, False).wait_send()


class Pair:
    def __init__(self, me, n, sides):
        self.has_right, self.has_left = me < n - 1, me > 0
        self.copies = [pltpu.make_async_remote_copy(
            src, dst, ssem, rsem, device_id={"cols": peer}, device_id_type=MESH)
            for (src, dst, ssem, rsem), peer in zip(
                sides, (lax.rem(me + 1, n), lax.rem(me + n - 1, n)))]

    def start(self):
        pl.when(self.has_right)(self.copies[0].start)
        pl.when(self.has_left)(self.copies[1].start)

    def wait(self):
        pl.when(self.has_left)(self.copies[0].wait_recv)
        pl.when(self.has_right)(self.copies[1].wait_recv)

    def drain(self):
        pl.when(self.has_right)(self.copies[0].wait_send)
        pl.when(self.has_left)(self.copies[1].wait_send)


class Sum:
    def __init__(self, pos, zs, ys, terms, bufs, sems):
        self.pos, self.zs, self.ys, self.terms = pos, zs, ys, terms
        self.s1, self.s2, self.bufc, self.bufy, self.bufz = bufs
        self.sc, self.rc, self.sy, self.ry, self.sz, self.rz = sems
        self.zorder = list(range(1, zs)) + [0]
        self.yorder = list(range(1, ys)) + [0]

    def zi(self, i):
        return lax.rem(self.pos[0] + i, self.zs)

    def yi(self, j):
        return lax.rem(self.pos[1] + j, self.ys)

    def copy(self, src, dst, ssem, rsem, device):
        return pltpu.make_async_remote_copy(
            src, dst, ssem, rsem, device_id=device, device_id_type=MESH)

    def core_copy(self, j, i):
        z, y, core = self.pos
        return self.copy(self.terms.at[self.zi(i), self.yi(j), 1 - core], self.bufc.at[j, i],
                         self.sc.at[j, i], self.rc.at[j, i], at(z, y, 1 - core, self.ys))

    def y_copy(self, j, i):
        z, y, core = self.pos
        return self.copy(self.s1.at[j, i], self.bufy.at[j, i], self.sy.at[j, i],
                         self.ry.at[j, i], at(z, self.yi(j), core, self.ys))

    def z_copy(self, i):
        z, y, core = self.pos
        return self.copy(self.s2.at[i], self.bufz.at[i], self.sz.at[i], self.rz.at[i],
                         at(self.zi(i), y, core, self.ys))

    def start(self):
        for j in self.yorder:
            for i in self.zorder:
                self.core_copy(j, i).start()

    def pair(self):
        core = self.pos[2]
        for j in self.yorder:
            for i in self.zorder:
                self.core_copy(j, i).wait_recv()
                both = self.terms[self.zi(i), self.yi(j), core].astype(F32)
                self.s1[j, i] = (both + self.bufc[j, i].astype(F32)).astype(BF16)
                if j:
                    self.y_copy(j, i).start()

    def along_y(self, begin, end):
        for i in self.zorder[begin:end]:
            total = self.s1[0, i].astype(F32)
            for j in range(1, self.ys):
                self.y_copy(j, i).wait_recv()
                total = total + self.bufy[j, i].astype(F32)
            if i:
                self.s2[i] = total.astype(BF16)
                self.z_copy(i).start()
            else:
                self.own = total

    def along_z(self):
        total = self.own
        for i in range(1, self.zs):
            self.z_copy(i).wait_recv()
            total = total + self.bufz[i].astype(F32)
        return total

    def drain_first(self):
        for j in self.yorder:
            for i in self.zorder:
                self.core_copy(j, i).wait_send()
                if j:
                    self.y_copy(j, i).wait_send()

    def drain_last(self):
        for i in range(1, self.zs):
            self.z_copy(i).wait_send()


class Sum2:
    def __init__(self, pos, zs, ys, terms, cut, bufs, sems):
        self.pos, self.zs, self.ys, self.terms = pos, zs, ys, terms
        (self.s1a, self.s1b, self.bufca, self.bufcb, self.bufy, self.s2a, self.bufz, self.bufw,
         self.s2b, self.bufv) = bufs
        (self.sc, self.rc, self.sy, self.ry, self.sz, self.rz, self.sw, self.rw, self.sv, self.rv,
         self.sb, self.rb) = sems
        self.cut, width = cut, terms.shape[-1]
        self.lanes_a, self.lanes_b = pl.ds(0, cut), pl.ds(cut, width - cut)
        self.zorder = list(range(1, zs)) + [0]
        self.yorder = list(range(1, ys)) + [0]

    def zi(self, i):
        return lax.rem(self.pos[0] + i, self.zs)

    def yi(self, j):
        return lax.rem(self.pos[1] + j, self.ys)

    def y_peer(self, j):
        return at(self.pos[0], self.yi(j), self.pos[2], self.ys)

    def z_peer(self, i):
        return at(self.zi(i), self.pos[1], self.pos[2], self.ys)

    def copy(self, src, dst, ssem, rsem, device):
        return pltpu.make_async_remote_copy(
            src, dst, ssem, rsem, device_id=device, device_id_type=MESH)

    def core_copy(self, j, i):
        z, y, core = self.pos
        return self.copy(self.terms.at[self.zi(i), self.yi(j), 1 - core, :, self.lanes_a], self.bufca.at[j, i],
                         self.sc.at[j, i], self.rc.at[j, i], at(z, y, 1 - core, self.ys))

    def core_copy_b(self):
        z, y, core = self.pos
        return self.copy(self.terms.at[:, :, 1 - core, :, self.lanes_b], self.bufcb, self.sb.at[0],
                         self.rb.at[0], at(z, y, 1 - core, self.ys))

    def y_copies(self, j):
        return [self.copy(self.s1a.at[j, i], self.bufy.at[j, i], self.sy.at[j, i],
                          self.ry.at[j, i], self.y_peer(j)) for i in self.zorder]

    def w_copy(self, i):
        return self.copy(self.s1b.at[i], self.bufw.at[i], self.sw.at[i],
                         self.rw.at[i], self.z_peer(i))

    def z_copy(self, i):
        return self.copy(self.s2a.at[i], self.bufz.at[i], self.sz.at[i], self.rz.at[i], self.z_peer(i))

    def v_copy(self, j):
        return self.copy(self.s2b.at[j], self.bufv.at[j], self.sv.at[j], self.rv.at[j], self.y_peer(j))

    def start_b(self):
        self.core_copy_b().start()

    def start_a(self):
        for j in self.yorder:
            for i in self.zorder:
                self.core_copy(j, i).start()

    def pair_b(self):
        core = self.pos[2]
        self.core_copy_b().wait_recv()
        for i in self.zorder:
            for j in range(self.ys):
                both = self.terms[self.zi(i), self.yi(j), core, :, self.lanes_b].astype(F32)
                self.s1b[i, j] = (both + self.bufcb[self.zi(i), self.yi(j)].astype(F32)).astype(BF16)
            if i:
                self.w_copy(i).start()

    def pair_a(self):
        core = self.pos[2]
        for j in self.yorder:
            for i in self.zorder:
                self.core_copy(j, i).wait_recv()
                both = self.terms[self.zi(i), self.yi(j), core, :, self.lanes_a].astype(F32)
                self.s1a[j, i] = (both + self.bufca[j, i].astype(F32)).astype(BF16)
                if j:
                    self.y_copies(j)[self.zorder.index(i)].start()

    def second_b(self):
        for i in self.zorder[:-1]:
            self.w_copy(i).wait_recv()
        for j in self.yorder:
            total = self.s1b[0, j].astype(F32)
            for i in self.zorder[:-1]:
                total = total + self.bufw[i, j].astype(F32)
            if j:
                self.s2b[j] = total.astype(BF16)
                self.v_copy(j).start()
            else:
                self.own_b = total

    def second_a(self, begin, end):
        for i in self.zorder[begin:end]:
            total = self.s1a[0, i].astype(F32)
            for j in range(1, self.ys):
                copies = self.y_copies(j)
                if len(copies) > 1:
                    copies[self.zorder.index(i)].wait_recv()
                elif i == self.zorder[0]:
                    copies[0].wait_recv()
                total = total + self.bufy[j, i].astype(F32)
            if i:
                self.s2a[i] = total.astype(BF16)
                self.z_copy(i).start()
            else:
                self.own_a = total

    def last_b(self):
        total = self.own_b
        for j in range(1, self.ys):
            self.v_copy(j).wait_recv()
            total = total + self.bufv[j].astype(F32)
        return total

    def last_a(self):
        total = self.own_a
        for i in range(1, self.zs):
            self.z_copy(i).wait_recv()
            total = total + self.bufz[i].astype(F32)
        return total

    def drain_first(self):
        self.core_copy_b().wait_send()
        for j in self.yorder:
            for i in self.zorder:
                self.core_copy(j, i).wait_send()
            if j:
                for copy in self.y_copies(j):
                    copy.wait_send()
        for i in range(1, self.zs):
            self.w_copy(i).wait_send()

    def drain_last(self):
        for j in range(1, self.ys):
            self.v_copy(j).wait_send()
        for i in range(1, self.zs):
            self.z_copy(i).wait_send()


def tap(t):
    return slice(t * LANES, (t + 1) * LANES)


def conv_taps(ref, w, start, step, count):
    total = None
    for kx in range(3):
        rhs = jnp.concatenate([w[:, tap(3 * ky + kx)] for ky in range(3)], axis=1)
        term = lax.dot_general(ref[pl.ds(start + kx * step, count), :], rhs,
                               (((1,), (1,)), ((), ())), preferred_element_type=F32)
        total = term if total is None else total + term
    return total


def join_rows(prod, d, height, kx):
    up = from_below(prod[:, tap(kx)], d, height)
    down = from_above(prod[:, tap(6 + kx)], d, height)
    return up + prod[:, tap(3 + kx)] + down


def put_terms(ref, place, value):
    zs, ys = ref.shape[0], ref.shape[1]
    (first, count), t = place
    ref[:, :, :, first : first + count, tap(t)] = value.reshape(zs, ys, 2, count, LANES).astype(BF16)


def grad_taps(ref, places, turned, acts, start, step, kxs=range(3)):
    count = turned.shape[1]
    for kx in kxs:
        prod = jnp.dot(turned, acts[pl.ds(start + kx * step, count), :],
                       preferred_element_type=F32)
        for ky in range(3):
            put_terms(ref, places[3 * ky + kx], prod[:, tap(ky)])


def fused_kernel(
    n, zs, ys, height, breadth, rl, rm, rf,
    x_ref, t_ref, wl_ref, wm_ref, wf_ref, o1_ref, o2_ref, o3_ref,
    xv, tv, wlv, wmv, wfv,
    pa, ga, gb, ta, tb, xh, xs, x9, x3f, x3s, pre1, pre2, acc, send, recv, tf, tn,
    a1, a2, a3, a4, a5, b1, b2, b3, b4, b5, b6, b7, b8, b9, b10, lsem, sx, rx, ssem, rsem, *sems,
):
    me, z, y, core = place(n, zs, ys)
    pos = (z, y, core)
    h, b = height, breadth
    depth = wf_ref.shape[1] // 9
    left, right = lax.rem(me + n - 1, n), lax.rem(me + 1, n)
    loads = [pltpu.make_async_copy(src, dst, lsem.at[i]) for i, (src, dst) in enumerate(
        ((wm_ref, wmv), (wf_ref, wfv), (x_ref, xv), (wl_ref, wlv), (t_ref, tv)))]
    for load in loads:
        load.start()
    peers = (
        [at(flip(z, i), y, core, ys) for i in range(1, zs)]
        + [at(z, flip(y, j), core, ys) for j in range(1, ys)]
        + [at(z, y, 1 - core, ys), {"cols": left}, {"cols": right}]
    )
    call(peers)
    middle = [((0, rm), t) if t < 7 else ((rm, rf), t - 7) for t in range(9)]
    first = [((rm, rf), t + 2) for t in range(5)]
    low = Star(pos, zs, ys, pa, ga, sems[0:6])
    cut = rl // 16 * 8
    parts = ((0, cut), (cut, rl - cut)) if cut else ((0, rl),)
    high = [Line(pos, zs, ys, wlv, gb, begin, rows, sems[8 * i + 6 : 8 * i + 14])
            for i, (begin, rows) in enumerate(parts)]
    sum_a = Sum(pos, zs, ys, ta, (a1, a2, a3, a4, a5), sems[22:28])
    sum_b = Sum2(pos, zs, ys, tb, 6 * LANES, (b1, b2, b3, b4, b5, b6, b7, b8, b9, b10),
                 sems[28:40])
    loads[0].wait()
    loads[1].wait()
    pa[0:rm, :] = wmv[:, 0 : 7 * LANES]
    pa[rm : rm + rf, 0 : 2 * LANES] = wmv[:, 7 * LANES : 9 * LANES]
    pa[rm : rm + rf, 6 * LANES : 7 * LANES] = jnp.zeros((rf, LANES), BF16)
    pa[rm : rm + rf, 2 * LANES : 2 * LANES + 9 * depth] = wfv[...]
    hear(peers)
    low.start()
    loads[2].wait()
    edge = 14 * depth
    halo = Pair(me, n, [(xv.at[:, pl.ds(b * depth - edge, edge)], xh.at[0], sx.at[0], rx.at[0]),
                        (xv.at[:, pl.ds(0, edge)], xh.at[1], sx.at[1], rx.at[1])])
    halo.start()
    loads[3].wait()
    for line in high:
        line.start()

    for i in reversed(range(1, zs)):
        low.forward_z(i)
    for line in high:
        line.forward_z(1)
    loads[4].wait()
    target = tv[...].astype(F32)
    t_norm = jnp.sqrt(jnp.sum(target * target, -1, keepdims=True) + epsilon)
    target = target * (1.0 / t_norm)
    for q in range(tf.shape[0]):
        tf[q] = target[:, tap(q)]
    for c in range(b):
        for q in range(tf.shape[0]):
            tn[pl.ds(c * h, h), tap(q)] = tf[q, pl.ds(c, h, stride=b), :]

    first_col = me * b
    width = n * b

    def inside(v, first):
        cols = column_of(v.shape[0], h, first_col + first)
        return jnp.where((cols >= 0) & (cols < width), v, 0.0)

    halo.wait()
    half = lax.broadcasted_iota(jnp.int32, (h, LANES), 1) < depth
    at_col = 0
    for part, pairs in ((xh[0], 7), (xv[...], b // 2), (xh[1], 7)):
        part = part.astype(F32)
        for q in range(pairs):
            both = part[:, tap(q)]
            turned = pltpu.roll(both, depth, 1)
            xs[pl.ds(at_col * h, h), :] = jnp.where(half, both, turned)
            xs[pl.ds((at_col + 1) * h, h), :] = jnp.where(half, turned, both)
            at_col += 2
    for i in [0] + list(reversed(range(1, zs))):
        low.forward_y(i)
    for line in high:
        line.forward_z(2)
    wide_x = inside(xs[...], -14)
    count1 = (b + 24) * h
    rows3 = (from_above(wide_x, 2, h), wide_x, from_below(wide_x, 2, h))

    def piece(t):
        ky, kx = t // 3, t % 3
        return rows3[ky][kx * 2 * h : kx * 2 * h + count1]

    lower = lax.broadcasted_iota(jnp.int32, (count1, LANES), 1) < depth
    for q in range(5):
        odd = piece(2 * q + 1) if q < 4 else 0.0
        x9[:, tap(q)] = jnp.where(lower, piece(2 * q), odd).astype(BF16)
    for s in range(3, zs):
        for line in high:
            line.forward_z(s)
    low.finish()
    w1 = ga[:, :, :, rm : rm + rf, 2 * LANES : 7 * LANES].reshape(n * rf, 5 * LANES)
    v = lax.dot_general(x9[...], w1, (((1,), (1,)), ((), ())), preferred_element_type=F32)
    pre1[...] = v
    act = inside(v * sigmoid(v), -12).astype(BF16).astype(F32)
    spread_rows(x3f, act, 4, h)
    for line in high:
        for s in range(zs - 1):
            line.forward_y(s)
    w2 = jnp.concatenate([
        ga[:, :, :, 0:rm, :].reshape(n * rm, 7 * LANES),
        ga[:, :, :, rm : rm + rf, 0 : 2 * LANES].reshape(n * rm, 2 * LANES)], axis=1)
    v = conv_taps(x3f, w2, 0, 4 * h, (b + 16) * h)
    pre2[...] = v
    act = inside(v * sigmoid(v), -8).astype(BF16).astype(F32)
    spread_rows(x3s, act, 8, h)
    for line in high:
        line.forward_y(zs - 1)
    for line in high:
        line.finish()
    w3 = gb[...].reshape(n * rl, 9 * LANES)
    student = conv_taps(x3s, w3, 0, 8 * h, b * h)
    inverse = 1.0 / jnp.sqrt(jnp.sum(student * student, -1, keepdims=True) + epsilon)
    s_unit = student * inverse
    differ = s_unit - tn[...]
    slope = (differ - s_unit * jnp.sum(s_unit * differ, -1, keepdims=True)) * inverse

    prod = jnp.dot(slope.astype(BF16), w3, preferred_element_type=F32)
    e = 8 * h
    m = b * h
    acc[pl.ds(0, m), :] = join_rows(prod, 8, h, 0)
    acc[pl.ds(m, 2 * e), :] = jnp.zeros((2 * e, LANES), F32)
    acc[pl.ds(e, m), :] += join_rows(prod, 8, h, 1)
    acc[pl.ds(2 * e, m), :] += join_rows(prod, 8, h, 2)
    part = 12 * h
    send[0] = acc[pl.ds(m + 2 * e - part, part), :].astype(BF16)
    send[1] = acc[pl.ds(0, part), :].astype(BF16)
    copies = Pair(me, n, [(send.at[side], recv.at[side], ssem.at[side], rsem.at[side])
                          for side in range(2)])
    copies.start()
    turned = slope.T.astype(BF16)
    last = [((0, rl), 3 * (t % 3) + t // 3) for t in range(9)]
    grad_taps(tb, last, turned, x3s, 0, 8 * h, (2,))
    sum_b.start_b()
    grad_taps(tb, last, turned, x3s, 0, 8 * h, (0, 1))
    sum_b.start_a()
    sum_b.pair_b()
    sum_b.pair_a()
    for each in (halo, low, *high):
        each.drain()
    copies.wait()
    inner = (b + 8) * h
    split = inner - part
    from_left = jnp.where(me > 0, recv[0].astype(F32), 0.0)
    from_right = jnp.where(me < n - 1, recv[1].astype(F32), 0.0)
    acc[pl.ds(4 * h, part), :] += from_left
    acc[pl.ds(4 * h + split, part), :] += from_right
    back = acc[pl.ds(4 * h, inner), :]
    slope2 = inside(back * silu_slope(pre2[pl.ds(4 * h, inner), :]), -4).astype(BF16)
    prod = jnp.dot(slope2, w2, preferred_element_type=F32)
    back = (
        join_rows(prod, 4, h, 0)[8 * h : 8 * h + m]
        + join_rows(prod, 4, h, 1)[4 * h : 4 * h + m]
        + join_rows(prod, 4, h, 2)[0:m]
    )
    grad_taps(ta, middle, slope2.astype(F32)[4 * h : 4 * h + m].T.astype(BF16), x3f, 8 * h, 4 * h)
    slope1 = back * silu_slope(pre1[pl.ds(12 * h, m), :])
    prod = jnp.dot(slope1.T.astype(BF16), x9[pl.ds(12 * h, m), :], preferred_element_type=F32)
    for q in range(5):
        put_terms(ta, first[q], prod[:, tap(q)])
    sum_a.start()
    sum_b.second_a(0, 1)
    sum_a.pair()
    sum_b.second_a(1, 2)
    sum_b.second_b()
    sum_b.second_a(2, zs)
    sum_a.along_y(0, zs)
    copies.drain()
    sum_b.drain_first()
    sum_a.drain_first()
    for kxs, total in (((0, 1), sum_b.last_a()), ((2,), sum_b.last_b())):
        for i, kx in enumerate(kxs):
            for ky in range(3):
                o3_ref[:, tap(3 * ky + kx)] = total[:, tap(3 * i + ky)]
    total = sum_a.along_z()
    o2_ref[:, 0 : 7 * LANES] = total[0:rm]
    o2_ref[:, 7 * LANES : 9 * LANES] = total[rm : rm + rf, 0 : 2 * LANES]
    o1_ref[...] = total[rm : rm + rf, 2 * LANES : 2 * LANES + 9 * depth]
    sum_a.drain_last()
    sum_b.drain_last()


def hand_over_kernel(a_ref, b_ref, c_ref, x_ref, y_ref, z_ref):
    x_ref[...] = a_ref[...]
    y_ref[...] = b_ref[...]
    z_ref[...] = c_ref[...]


def hand_over(arrays):
    vmem = pl.BlockSpec(memory_space=pltpu.VMEM)
    return pl.pallas_call(
        hand_over_kernel,
        out_shape=tuple(jax.ShapeDtypeStruct(a.shape, a.dtype) for a in arrays),
        in_specs=[vmem] * 3,
        out_specs=(vmem,) * 3,
        name="hand_over",
    )(*(pltpu.with_memory_space_constraint(a, pltpu.VMEM) for a in arrays))


def fused(n, height, breadth, x, t, wl, wm, wf):
    zs, ys = split_axis(n)
    sem = pltpu.SemaphoreType.DMA
    vmem = pl.BlockSpec(memory_space=pltpu.VMEM)
    h, b = height, breadth
    rl, rm, rf = wl.shape[0], wm.shape[0], wf.shape[0]
    wide = wl.shape[1]
    low, high = (rm + rf, 7 * LANES), (rl, wide)
    channels = t.shape[1]

    def sum_bufs(block):
        return [
            pltpu.VMEM((ys, zs) + block, BF16), pltpu.VMEM((zs,) + block, BF16),
            pltpu.VMEM((ys, zs) + block, BF16), pltpu.VMEM((ys, zs) + block, BF16),
            pltpu.VMEM((zs,) + block, BF16),
        ]

    def sum2_bufs(block, cut):
        rows, width = block
        part_a, part_b = (rows, cut), (rows, width - cut)
        return [
            pltpu.VMEM((ys, zs) + part_a, BF16), pltpu.VMEM((zs, ys) + part_b, BF16),
            pltpu.VMEM((ys, zs) + part_a, BF16), pltpu.VMEM((zs, ys) + part_b, BF16),
            pltpu.VMEM((ys, zs) + part_a, BF16), pltpu.VMEM((zs,) + part_a, BF16),
            pltpu.VMEM((zs,) + part_a, BF16), pltpu.VMEM((zs, ys) + part_b, BF16),
            pltpu.VMEM((ys,) + part_b, BF16), pltpu.VMEM((ys,) + part_b, BF16),
        ]

    star_sems = [sem((zs,))] * 2 + [sem((ys, zs))] * 4
    line_sems = [sem((zs,))] * 4 + [sem((ys, zs))] * 4
    sum_sems = [sem((ys, zs))] * 4 + [sem((zs,))] * 2
    sum2_sems = [sem((ys, zs))] * 4 + [sem((zs,))] * 4 + [sem((ys,))] * 2 + [sem((1,))] * 2
    return pl.pallas_call(
        functools.partial(fused_kernel, n, zs, ys, h, b, rl, rm, rf),
        out_shape=tuple(pltpu.VMEM(w.shape, F32) for w in (wf, wm, wl)),
        in_specs=[pl.BlockSpec(memory_space=pltpu.HBM)] * 5,
        out_specs=(vmem,) * 3,
        scratch_shapes=[pltpu.VMEM(w.shape, BF16) for w in (x, t, wl, wm, wf)] + [
            pltpu.VMEM(low, BF16),
            pltpu.VMEM((zs, ys, 2) + low, BF16),
            pltpu.VMEM((zs, ys, 2) + high, BF16),
            pltpu.VMEM((zs, ys, 2) + low, BF16),
            pltpu.VMEM((zs, ys, 2) + high, BF16),
            pltpu.VMEM((2, h, 14 * wf.shape[1] // 9), BF16),
            pltpu.VMEM(((b + 28) * h, LANES), F32),
            pltpu.VMEM(((b + 24) * h, 5 * LANES), BF16),
            pltpu.VMEM(((b + 24) * h, 3 * LANES), BF16),
            pltpu.VMEM(((b + 16) * h, 3 * LANES), BF16),
            pltpu.VMEM(((b + 24) * h, LANES), F32),
            pltpu.VMEM(((b + 16) * h, LANES), F32),
            pltpu.VMEM(((b + 16) * h, LANES), F32),
            pltpu.VMEM((2, 12 * h, LANES), BF16),
            pltpu.VMEM((2, 12 * h, LANES), BF16),
            pltpu.VMEM((channels // LANES, b * h, LANES), F32),
            pltpu.VMEM((b * h, channels), F32),
        ]
        + sum_bufs(low) + sum2_bufs(high, 6 * LANES)
        + [sem((5,))] + [sem((2,))] * 4 + star_sems + line_sems * 2 + sum_sems + sum2_sems,
        compiler_params=pltpu.CompilerParams(
            collective_id=3, has_side_effects=True, vmem_limit_bytes=56 << 20),
        name="fused_step",
    )(x, t, wl, wm, wf)


def on_device(n, image_feats, teacher, w_first, w_middle, w_last):
    height, breadth, channels = teacher.shape
    in_depth = w_first.shape[1] // 9
    rl, rm, rf = w_last.shape[0], w_middle.shape[0], w_first.shape[0]
    if (split_axis(n)[0] > 2 and n & (n - 1) == 0 and rm == rf and all(r % 8 == 0 for r in (rl, rm, rf))
            and breadth % 8 == 0 and 2 * in_depth == LANES):
        return hand_over(fused(n, height, breadth, image_feats,
                               teacher.reshape(height * breadth, channels), w_last, w_middle, w_first))
    packed = jnp.concatenate([taps_by_column(w) for w in (w_last, w_middle, w_first)], axis=0)
    x = image_feats.reshape(height, breadth, in_depth).transpose(1, 0, 2)
    x = jnp.pad(x, ((0, 0), (0, 0), (0, LANES - in_depth)))
    x_cells = x.reshape(breadth * height, LANES)
    t_cells = teacher.transpose(1, 0, 2).reshape(breadth * height, channels)
    gathered, x_edges = gather(n, packed, x_cells, 14 * height)
    g = gathered.reshape((n,) + packed.shape)
    w3 = g[:, :rl].reshape(n * rl, -1)
    w2 = g[:, rl : rl + rm].reshape(n * rm, -1)
    w1 = g[:, rl + rm :].reshape(n * rf, -1)
    g1, g2, g3 = local_step(n, height, breadth, x_cells, x_edges, t_cells, w1, w2, w3)
    terms = jnp.concatenate(
        [g3.reshape(n, rl, -1), g2.reshape(n, rm, -1), g1.reshape(n, rf, -1)], axis=1)
    out = scatter(n, terms.reshape(gathered.shape))
    return (
        taps_by_row(out[rl + rm :], in_depth),
        taps_by_row(out[rl : rl + rm], LANES),
        taps_by_row(out[:rl], LANES),
    )


def solution(mesh):
    placed = (
        P("groups", "cols"),
        P("groups", "cols", None),
        P("cols", None),
        P("cols", None),
        P("cols", None),
    )
    return jax.shard_map(
        functools.partial(on_device, mesh.shape["cols"]),
        mesh=mesh,
        in_specs=placed,
        out_specs=(P(("groups", "cols"), None),) * 3,
        check_vma=False,
    )
```
